512 devices in a mesh: segment: 4 (over x), chan: 16 (over y, core), dp: 8 (over z).
Axes of the slice: x: 4, y: 8, z: 8, core: 2. Of those that a mesh axis runs over, the one named last changes fastest.
Arguments:
- grad_top: bfloat16 [8, 1536, 256], P('dp', None, 'chan'), may hold values from -6 to 6
- inputs_one: bfloat16 [4, 8, 1536, 256], P('segment', 'dp', 'chan'), may hold values from -6 to 6
- conv_one: bfloat16 [4, 8, 1536, 256], P('segment', 'dp', 'chan'), may hold values from -130 to 130
- inputs_two: bfloat16 [4, 8, 1536, 256], P('segment', 'dp', 'chan'), may hold values from -6 to 6
- conv_two: bfloat16 [4, 8, 1536, 256], P('segment', 'dp', 'chan'), may hold values from -130 to 130
- proj_weight: bfloat16 [4, 2, 1536, 1536], P('segment', None, 'chan'), may hold values from -0.15625 to 0.15625
- conv_weight: bfloat16 [4, 2, 1536, 432], P('segment', None, 'chan'), may hold values from -0.3125 to 0.3125
- norm_gain: float32 [4, 2, 1536], P('segment', None, 'chan'), may hold values from 0.1 to 1.9
- norm_bias: float32 [4, 2, 1536], P('segment', None, 'chan'), may hold values from -4 to 4
Outputs:
- grad_latent: bfloat16 [4, 8, 1536, 256], P('segment', 'dp', None, 'chan')
- grad_proj: float32 [4, 2, 1536, 1536], P('segment', None, 'chan')
- grad_conv: float32 [4, 2, 1536, 432], P('segment', None, 'chan')
- grad_gain: float32 [4, 2, 1536], P('segment', None, 'chan')
- grad_bias: float32 [4, 2, 1536], P('segment', None, 'chan')
The draws below stay inside these ranges and needn't reach their ends.
All inputs are finite; a program needn't handle non-finite values.
Results may differ from the reference program's by a relative error of at most 0.009.
Values may be sent and summed in bfloat16 or wider, within the bound.
No kernel may reach another device: no remote copies, remote signals or barrier semaphores. Data moves between devices by JAX's collectives and lax.ppermute only.
A program may use at most 64 MiB of HBM per device.

```python
import math
import jax
import jax.numpy as jnp
from jax import lax

C = 1536
GS = 48
WW = 64
ROWS = 4
SEGMENTS = 4
MBS = 8
P_SIZE = 256


def pre_norm_draw(key):
    first_key, second_key, third_key, fourth_key = jax.random.split(key, 4)
    chan_scale = jnp.exp(jax.random.uniform(second_key, (SEGMENTS, MBS, C, 1), jnp.float32) * math.log(10.0))
    pos_scale = jnp.exp(jax.random.uniform(third_key, (SEGMENTS, MBS, 1, P_SIZE), jnp.float32) * math.log(10.0))
    base = jnp.clip(jax.random.normal(first_key, (SEGMENTS, MBS, C, P_SIZE), jnp.float32), -4.0, 4.0)
    offset = jnp.clip(jax.random.normal(fourth_key, (SEGMENTS, MBS, C, 1), jnp.float32), -3.0, 3.0)
    return (base * chan_scale * pos_scale * 0.3 + offset).astype(jnp.bfloat16)


def draw_conv_one(key, part):
    return pre_norm_draw(jax.random.fold_in(key, 11))


def draw_conv_two(key, part):
    return pre_norm_draw(jax.random.fold_in(key, 12))


def shard_levels(rng, dims, cuts, low, high):
    def one(position, blocks):
        heights = jax.random.uniform(jax.random.fold_in(jax.random.fold_in(rng, 6), position), (blocks,), jnp.float32, low / len(cuts), high / len(cuts))
        return jnp.repeat(jnp.exp(heights), dims[position] // blocks).reshape((-1,) + (1,) * (len(dims) - position - 1))

    level = one(*cuts[0])
    for cut in cuts[1:]:
        level = level * one(*cut)
    return level


def gaussian(stream_key, shape, deviation, reach, cuts=(), dtype=jnp.bfloat16):
    drawn = jax.random.normal(stream_key, shape, jnp.float32) * deviation
    if len(cuts) > 0:
        drawn = shard_levels(stream_key, shape, cuts, -0.22, 0.18) * drawn
    return jnp.clip(drawn, min=-reach, max=reach).astype(dtype)


def setup_inputs(seed: int = 0) -> dict:
    seeds = jax.random.split(jax.random.key(seed), 10)
    grad_top = gaussian(seeds[0], (MBS, C, P_SIZE), 1.0, 6.0, ((0, 8), (2, 16)))
    inputs_one = gaussian(seeds[1], (SEGMENTS, MBS, C, P_SIZE), 1.0, 6.0, ((0, 4), (1, 8), (2, 16)))
    conv_one = draw_conv_one(jax.random.fold_in(seeds[9], 71), 0)
    inputs_two = gaussian(seeds[3], (SEGMENTS, MBS, C, P_SIZE), 1.0, 6.0, ((0, 4), (1, 8), (2, 16)))
    conv_two = draw_conv_two(jax.random.fold_in(seeds[9], 71), 0)
    proj_weight = gaussian(seeds[5], (SEGMENTS, 2, C, C), C ** -0.5, 0.15625, ((0, 4), (2, 16)))
    conv_weight = gaussian(seeds[6], (SEGMENTS, 2, C, 9 * GS), (9 * GS) ** -0.5, 0.3125, ((0, 4), (2, 16)))
    norm_gain = jnp.clip(1.0 + 0.18 * jax.random.normal(seeds[7], (SEGMENTS, 2, C), jnp.float32), 0.1, 1.9)
    norm_bias = gaussian(seeds[8], (SEGMENTS, 2, C), 1.0, 4.0, ((0, 4), (2, 16)), jnp.float32)
    return {"grad_top": grad_top, "inputs_one": inputs_one, "conv_one": conv_one, "inputs_two": inputs_two, "conv_two": conv_two, "proj_weight": proj_weight, "conv_weight": conv_weight, "norm_gain": norm_gain, "norm_bias": norm_bias}


NORM_EPS = 1e-05

def tap_shift(values, step_row, step_col):
    leading = values.shape[:2]
    grid_view = values.reshape(leading + (ROWS, WW))
    padded = jnp.pad(grid_view, ((0, 0), (0, 0), (1, 1), (1, 1)))
    window = padded[:, :, 1 + step_row:1 + step_row + ROWS, 1 + step_col:1 + step_col + WW]
    return window.reshape(leading + (ROWS * WW,))

def block_back(grad_in, saved_in, saved_pre, w_proj, w_conv, gain_vec, bias_vec):
    chans, positions = saved_pre.shape
    groups_here = chans // GS
    pre = saved_pre.astype(jnp.float32).reshape(groups_here, GS, positions)
    centre = lax.optimization_barrier(jnp.mean(pre, axis=(1, 2), keepdims=True))
    varied = lax.optimization_barrier(jnp.mean(jnp.square(pre - centre), axis=(1, 2), keepdims=True))
    inv_std = 1.0 / jnp.sqrt(varied + NORM_EPS)
    normed = (pre - centre) * inv_std
    gain_grid = gain_vec.reshape(groups_here, GS, 1)
    scaled = normed * gain_grid + bias_vec.reshape(groups_here, GS, 1)
    gate_vals = jax.nn.sigmoid(scaled)
    act_bf = (scaled * gate_vals).astype(jnp.bfloat16).reshape(chans, positions)
    grad_act = jnp.dot(w_proj, grad_in, preferred_element_type=jnp.float32).reshape(groups_here, GS, positions)
    proj_grad = jnp.dot(act_bf, grad_in.T, preferred_element_type=jnp.float32)
    grad_norm = grad_act * (gate_vals * (1.0 + scaled * (1.0 - gate_vals)))
    gain_grad = lax.optimization_barrier(jnp.sum(grad_norm * normed, axis=2)).reshape(chans)
    bias_grad = lax.optimization_barrier(jnp.sum(grad_norm, axis=2)).reshape(chans)
    weighted = grad_norm * gain_grid
    first_mean = lax.optimization_barrier(jnp.mean(weighted, axis=(1, 2), keepdims=True))
    second_mean = lax.optimization_barrier(jnp.mean(weighted * normed, axis=(1, 2), keepdims=True))
    grad_pre = (inv_std * (weighted - first_mean - normed * second_mean)).astype(jnp.bfloat16)
    saved_grid = saved_in.reshape(groups_here, GS, positions).astype(jnp.float32)
    grad_wide = grad_pre.astype(jnp.float32)
    taps_w = w_conv.astype(jnp.float32).reshape(groups_here, GS, 9, GS)
    conv_parts = []
    back_sum = jnp.zeros((groups_here, GS, positions), jnp.float32)
    for tap_row in (-1, 0, 1):
        for tap_col in (-1, 0, 1):
            tap_at = 3 * (tap_row + 1) + tap_col + 1
            source = tap_shift(saved_grid, tap_row, tap_col)
            conv_parts.append(jnp.einsum('gop,gjp->goj', grad_wide, source, precision=lax.Precision.HIGHEST))
            spread_back = jnp.einsum('goj,gop->gjp', taps_w[:, :, tap_at, :], grad_wide, precision=lax.Precision.HIGHEST)
            back_sum = back_sum + tap_shift(spread_back, -tap_row, -tap_col)
    conv_grad = jnp.stack(conv_parts, axis=2).reshape(chans, 9 * GS)
    branch = back_sum.reshape(chans, positions).astype(jnp.bfloat16)
    out_grad = (grad_in.astype(jnp.float32) + branch.astype(jnp.float32)).astype(jnp.bfloat16)
    return (out_grad, (proj_grad, conv_grad, gain_grad, bias_grad))

def section_back(entering, ins_one, pre_one, ins_two, pre_two, w_proj, w_conv, gains, biases):

    def one_micro(running, micro_items):
        grad_in, x_one, h_one, x_two, h_two = micro_items
        mid_grad, grads_two = block_back(grad_in, x_two, h_two, w_proj[1], w_conv[1], gains[1], biases[1])
        out_grad, grads_one = block_back(mid_grad, x_one, h_one, w_proj[0], w_conv[0], gains[0], biases[0])
        updated = tuple((acc + jnp.stack((first_part, second_part)) for acc, first_part, second_part in zip(running, grads_one, grads_two)))
        return (updated, out_grad)
    initial = (jnp.zeros((2, C, C), jnp.float32), jnp.zeros((2, C, 9 * GS), jnp.float32), jnp.zeros((2, C), jnp.float32), jnp.zeros((2, C), jnp.float32))
    return lax.scan(one_micro, initial, (entering, ins_one, pre_one, ins_two, pre_two))

def reference(grad_top, inputs_one, conv_one, inputs_two, conv_two, proj_weight, conv_weight, norm_gain, norm_bias):
    entering = grad_top
    latents, projs, convs, gains_out, biases_out = ([], [], [], [], [])
    for segment_at in range(SEGMENTS - 1, -1, -1):
        sums_here, grads_here = section_back(entering, inputs_one[segment_at], conv_one[segment_at], inputs_two[segment_at], conv_two[segment_at], proj_weight[segment_at], conv_weight[segment_at], norm_gain[segment_at], norm_bias[segment_at])
        latents.insert(0, grads_here)
        projs.insert(0, sums_here[0])
        convs.insert(0, sums_here[1])
        gains_out.insert(0, sums_here[2])
        biases_out.insert(0, sums_here[3])
        entering = grads_here
    return (jnp.stack(latents), jnp.stack(projs), jnp.stack(convs), jnp.stack(gains_out), jnp.stack(biases_out))
```

```python
import functools

import jax
import jax.numpy as jnp
from jax import lax
from jax.experimental import pallas as pl
from jax.experimental.pallas import tpu as pltpu
from jax.sharding import PartitionSpec as P

GS = 48
WW = 64
NORM_EPS = 1e-05
TAIL = 512
F32 = jnp.float32
BF16 = jnp.bfloat16
VMEM = pl.BlockSpec(memory_space=pltpu.VMEM)
SMEM = pl.BlockSpec(memory_space=pltpu.SMEM)
ANY = pl.BlockSpec(memory_space=pl.ANY)
NT = (((1,), (1,)), ((), ()))
TN = (((0,), (0,)), ((), ()))
PARAMS = pltpu.CompilerParams(vmem_limit_bytes=48 * 1024 * 1024)


def total(block):
    return jnp.sum(jnp.sum(block, axis=1, keepdims=True), axis=0, keepdims=True)


def forward_kernel(h_ref, gain_ref, bias_ref, xhat_ref, slope_ref, rate_ref, act_ref):
    chans, positions = h_ref.shape
    scale = 1.0 / (GS * positions)
    for at in range(0, chans, GS):
        rows = slice(at, at + GS)
        pre = h_ref[rows, :].astype(F32)
        pre = pre - total(pre) * scale
        inv_std = lax.rsqrt(total(pre * pre) * scale + NORM_EPS)
        xhat = pre * inv_std
        gain = gain_ref[rows, :]
        n = xhat * gain + bias_ref[rows, :]
        sig = jax.nn.sigmoid(n)
        slope = sig * (1.0 + n * (1.0 - sig))
        xhat_ref[rows, :] = xhat
        slope_ref[rows, :] = slope
        rate_ref[rows, :] = slope * (gain * inv_std)
        act_ref[rows, :] = (n * sig).astype(BF16)


def forward(h, gain, bias):
    full = jax.ShapeDtypeStruct(h.shape, F32)
    return pl.pallas_call(
        forward_kernel,
        out_shape=(full, full, full, jax.ShapeDtypeStruct(h.shape, BF16)),
        in_specs=[VMEM] * 3,
        out_specs=[VMEM] * 4,
        compiler_params=PARAMS,
        name="norm_forward",
    )(h, gain, bias)


def shifted(value, step_row, step_col, row, col):
    length = value.shape[1]
    rows = length // WW
    by = step_row * WW + step_col
    if by == 0:
        return value
    moved = pltpu.roll(value, (-by) % length, axis=1)
    inside = None
    if step_row:
        inside = row < rows - 1 if step_row > 0 else row > 0
    if step_col:
        here = col < WW - 1 if step_col > 0 else col > 0
        inside = here if inside is None else inside & here
    return jnp.where(inside, moved, 0.0)


def grid_of(shape):
    lane = lax.broadcasted_iota(jnp.int32, shape, 1)
    return lane // WW, lane % WW


def block_kernel(
    first, flags_ref, g_ref, w_ref, wc_ref, xhat_ref, rate_ref, *refs
):
    if first:
        out_ref, keep_ref, sg_ref, sgh_ref, sga_ref, sem = refs
    else:
        _, _, _, _, out_ref, keep_ref, sg_ref, sgh_ref, sga_ref, sem = refs
    chans, positions = xhat_ref.shape
    scale = 1.0 / (GS * positions)
    valid = flags_ref[0] > 0
    keep = pltpu.make_async_copy(g_ref, sg_ref, sem)
    if first:
        keep.start()
    else:

        @pl.when(valid)
        def _():
            keep.start()

    own = pl.multiple_of(flags_ref[1] * chans, chans)
    ga = jnp.dot(w_ref[...], g_ref[...], preferred_element_type=F32)
    row, col = grid_of((GS, positions))
    for at in range(0, chans, GS):
        rows = slice(at, at + GS)
        xhat = xhat_ref[rows, :]
        rw = ga[rows, :] * rate_ref[rows, :]
        gh = rw - total(rw) * scale - xhat * (total(rw * xhat) * scale)
        gh = gh.astype(BF16)
        spread = lax.dot_general(wc_ref[rows, :], gh, TN, preferred_element_type=F32)
        branch = None
        for step_col in (-1, 0, 1):
            part = None
            for step_row in (-1, 0, 1):
                tap = 3 * (step_row + 1) + step_col + 1
                term = shifted(spread[tap * GS : (tap + 1) * GS, :], -step_row, 0, row, col)
                part = term if part is None else part + term
            part = shifted(part, 0, -step_col, row, col)
            branch = part if branch is None else branch + part
        mine = g_ref[pl.ds(own + at, GS), :].astype(F32)
        result = (mine + branch.astype(BF16).astype(F32)).astype(BF16)
        out_ref[rows, :] = result
        if first:
            sgh_ref[rows, :] = gh
            sga_ref[rows, :] = ga[rows, :]
            keep_ref[rows, :] = result
        else:

            @pl.when(valid)
            def _():
                sgh_ref[rows, :] = gh
                sga_ref[rows, :] = ga[rows, :]
                keep_ref[rows, :] = result

    if first:
        keep.wait()
    else:

        @pl.when(valid)
        def _():
            keep.wait()


def block(flags, g, w, wc, xhat, rate, saved):
    chans, positions = xhat.shape
    first = saved is None
    shapes = (
        jax.ShapeDtypeStruct((chans, positions), BF16),
        jax.ShapeDtypeStruct((chans, positions), BF16),
        jax.ShapeDtypeStruct(g.shape, BF16),
        jax.ShapeDtypeStruct((chans, positions), BF16),
        jax.ShapeDtypeStruct((chans, positions), F32),
    )
    saved = () if first else saved
    result = pl.pallas_call(
        functools.partial(block_kernel, first),
        out_shape=shapes,
        in_specs=[SMEM] + [VMEM] * 5 + ([] if first else [VMEM, ANY, VMEM, VMEM]),
        out_specs=[VMEM, VMEM, ANY, VMEM, VMEM],
        scratch_shapes=[pltpu.SemaphoreType.DMA],
        input_output_aliases={} if first else {6: 1, 7: 2, 8: 3, 9: 4},
        compiler_params=PARAMS,
        name="block_backward",
    )(flags, g, w, wc, xhat, rate, *saved)
    return result[0], result[1:]


def weights_kernel(*refs):
    out_ref, stack = refs[-2:]
    chans, positions = refs[0].shape
    width = out_ref.shape[1] - TAIL
    row, col = grid_of((GS, positions))
    lane = lax.broadcasted_iota(jnp.int32, (GS, TAIL), 1)
    stack[9 * GS :, :] = jnp.zeros((TAIL - 9 * GS, positions), BF16)
    for b in range(2):
        act_ref, g_ref, gh_ref, ga_ref, x_ref, xhat_ref, slope_ref = refs[7 * b : 7 * b + 7]
        at = b * chans
        out_ref[at : at + chans, :width] = lax.dot_general(
            act_ref[...], g_ref[...], NT, preferred_element_type=F32
        ).astype(BF16)
        for q in range(0, chans, GS):
            rows = slice(q, q + GS)
            x = x_ref[rows, :].astype(F32)
            for step_row in (-1, 0, 1):
                for step_col in (-1, 0, 1):
                    tap = 3 * (step_row + 1) + step_col + 1
                    stack[tap * GS : (tap + 1) * GS, :] = shifted(
                        x, step_row, step_col, row, col
                    ).astype(BF16)
            taps = lax.dot_general(gh_ref[rows, :], stack[...], NT, preferred_element_type=F32)
            gn = ga_ref[rows, :] * slope_ref[rows, :]
            by_gain = jnp.sum(gn * xhat_ref[rows, :], axis=1, keepdims=True)
            by_bias = jnp.sum(gn, axis=1, keepdims=True)
            taps = jnp.where(lane == 9 * GS, by_gain, taps)
            taps = jnp.where(lane == 9 * GS + 1, by_bias, taps)
            out_ref[at + q : at + q + GS, width:] = taps.astype(BF16)


def weight_grads(first, second, width):
    chans, positions = first[0].shape
    return pl.pallas_call(
        weights_kernel,
        out_shape=jax.ShapeDtypeStruct((2 * chans, width + TAIL), BF16),
        in_specs=[VMEM] * 14,
        out_specs=VMEM,
        scratch_shapes=[pltpu.VMEM((TAIL, positions), BF16)],
        compiler_params=PARAMS,
        name="weight_grads",
    )(*first, *second)


def reduce_kernel(in_ref, out_ref):
    count = in_ref.shape[0]
    acc = in_ref[0].astype(F32)
    for m in range(1, count):
        acc = acc + in_ref[m].astype(F32)
    done = acc.astype(BF16)
    for m in range(count):
        out_ref[m] = done


def spread_sum(parts):
    return pl.pallas_call(
        reduce_kernel,
        out_shape=jax.ShapeDtypeStruct(parts.shape, BF16),
        in_specs=[VMEM],
        out_specs=VMEM,
        compiler_params=PARAMS,
        name="sum_microbatches",
    )(parts)


def widen_kernel(in_ref, proj_ref, conv_ref, tail_ref):
    chans, width = proj_ref.shape[1:]
    for b in range(2):
        rows = slice(b * chans, (b + 1) * chans)
        proj_ref[b] = in_ref[rows, :width].astype(F32)
        conv_ref[b] = in_ref[rows, width : width + 9 * GS].astype(F32)
        tail_ref[b] = in_ref[rows, width + TAIL - 128 :].astype(F32)


def widen(sums, chans, width):
    return pl.pallas_call(
        widen_kernel,
        out_shape=(
            jax.ShapeDtypeStruct((2, chans, width), F32),
            jax.ShapeDtypeStruct((2, chans, 9 * GS), F32),
            jax.ShapeDtypeStruct((2, chans, 128), F32),
        ),
        in_specs=[VMEM],
        out_specs=[VMEM] * 3,
        compiler_params=PARAMS,
        name="widen",
    )(sums)


def per_device(
    grad_top,
    inputs_one,
    conv_one,
    inputs_two,
    conv_two,
    proj_weight,
    conv_weight,
    norm_gain,
    norm_bias,
):
    segments = lax.axis_size("segment")
    segment_at = lax.axis_index("segment")
    chan_at = lax.axis_index("chan")
    members = lax.axis_size("dp")
    chans, positions = conv_one.shape[2:]
    width = proj_weight.shape[3]

    w = (proj_weight[0, 0], proj_weight[0, 1])
    wc = (conv_weight[0, 0], conv_weight[0, 1])
    gain = norm_gain[0][:, :, None]
    bias = norm_bias[0][:, :, None]
    state = (
        forward(conv_one[0, 0], gain[0], bias[0]),
        forward(conv_two[0, 0], gain[1], bias[1]),
    )
    saved = [None, None]
    out = None
    for tick in range(segments):
        valid = (segment_at == segments - 1 - tick).astype(jnp.int32)
        flags = jnp.stack([valid, chan_at.astype(jnp.int32)])
        if tick == 0:
            g = lax.all_gather(grad_top[0], "chan", axis=1, tiled=True)
        else:
            lower = segments - 1 - tick
            pair = [[lower, lower + 1]]
            rest = [s for s in range(segments) if s not in pair[0]]
            groups = sorted(pair + [rest[i : i + 2] for i in range(0, len(rest), 2)])
            both = lax.all_gather(
                out, "segment", axis=0, tiled=True, axis_index_groups=groups
            )
            g = lax.all_gather(both[chans:], "chan", axis=0, tiled=True)
        for b in (1, 0):
            out, saved[b] = block(
                flags, g, w[b], wc[b], state[b][0], state[b][2], saved[b]
            )
            if b == 1:
                g = lax.all_gather(out, "chan", axis=0, tiled=True)

    latent = lax.all_to_all(saved[0][0], "chan", split_axis=1, concat_axis=0, tiled=True)
    saved_in = (inputs_one[0, 0], inputs_two[0, 0])
    grads = weight_grads(
        *(
            (state[b][3],) + tuple(saved[b][1:]) + (saved_in[b], state[b][0], state[b][1])
            for b in (0, 1)
        ),
        width,
    )
    parts = grads.reshape(members, 2 * chans // members, width + TAIL)
    parts = lax.all_to_all(parts, "dp", split_axis=0, concat_axis=0, tiled=True)
    parts = spread_sum(parts)
    parts = lax.all_to_all(parts, "dp", split_axis=0, concat_axis=0, tiled=True)
    proj, conv, tail = widen(parts.reshape(2 * chans, width + TAIL), chans, width)
    at = 9 * GS - (TAIL - 128)
    return (
        latent[None, None],
        proj[None],
        conv[None],
        tail[None, :, :, at],
        tail[None, :, :, at + 1],
    )


def solution(mesh):
    return jax.shard_map(
        per_device,
        mesh=mesh,
        in_specs=(
            P("dp", None, "chan"),
            P("segment", "dp", "chan", None),
            P("segment", "dp", "chan", None),
            P("segment", "dp", "chan", None),
            P("segment", "dp", "chan", None),
            P("segment", None, "chan", None),
            P("segment", None, "chan", None),
            P("segment", None, "chan"),
            P("segment", None, "chan"),
        ),
        out_specs=(
            P("segment", "dp", None, "chan"),
            P("segment", None, "chan", None),
            P("segment", None, "chan", None),
            P("segment", None, "chan"),
            P("segment", None, "chan"),
        ),
        check_vma=False,
    )
```

```python
import functools

import jax
import jax.numpy as jnp
from jax import lax
from jax.experimental import pallas as pl
from jax.experimental.pallas import tpu as pltpu
from jax.sharding import PartitionSpec as P

GS = 48
WW = 64
NORM_EPS = 1e-05
TAIL = 512
F32 = jnp.float32
BF16 = jnp.bfloat16
VMEM = pl.BlockSpec(memory_space=pltpu.VMEM)
SMEM = pl.BlockSpec(memory_space=pltpu.SMEM)
ANY = pl.BlockSpec(memory_space=pl.ANY)
NT = (((1,), (1,)), ((), ()))
TN = (((0,), (0,)), ((), ()))
PARAMS = pltpu.CompilerParams(vmem_limit_bytes=32 * 1024 * 1024)


def shape_of(shape, dtype):
    return jax.ShapeDtypeStruct(shape, dtype)


def total(block):
    return jnp.sum(jnp.sum(block, axis=1, keepdims=True), axis=0, keepdims=True)


def norm_group(h, gain, bias):
    scale = 1.0 / (h.shape[0] * h.shape[1])
    pre = h.astype(F32)
    pre = pre - total(pre) * scale
    inv_std = lax.rsqrt(total(pre * pre) * scale + NORM_EPS)
    xhat = pre * inv_std
    n = xhat * gain + bias
    sig = jax.nn.sigmoid(n)
    slope = sig * (1.0 + n * (1.0 - sig))
    return xhat, n, sig, slope, inv_std


def column(line):
    count = line.shape[1]
    down = lax.broadcasted_iota(jnp.int32, (count, count), 0)
    across = lax.broadcasted_iota(jnp.int32, (count, count), 1)
    return jnp.sum(jnp.where(down == across, line, 0.0), axis=1, keepdims=True)


def prepare_kernel(
    w_ref, wc_ref, h1_ref, h2_ref, gain_ref, bias_ref,
    pack_ref, xhat_ref, slope_ref, rate_ref, act_ref,
):
    chans, width = w_ref.shape[2:]
    taps = wc_ref.shape[3]
    lane = lax.broadcasted_iota(jnp.int32, (chans, TAIL - 384), 1)
    for b, h_ref in enumerate((h1_ref, h2_ref)):
        pack_ref[b, :, :width] = w_ref[0, b]
        pack_ref[b, :, width : width + 384] = wc_ref[0, b, :, :384]
        last = wc_ref[0, b, :, 384:].astype(F32)
        last = jnp.concatenate(
            [last, jnp.zeros((chans, TAIL - taps), F32)], axis=1
        )
        gain = column(gain_ref[0, b : b + 1, :])
        bias = column(bias_ref[0, b : b + 1, :])
        at = taps - 384
        for whole in (gain, bias):
            rest = whole
            for _ in range(3):
                piece = rest.astype(BF16).astype(F32)
                rest = rest - piece
                last = jnp.where(lane == at, piece, last)
                at += 1
        pack_ref[b, :, width + 384 : width + TAIL] = last.astype(BF16)
        pack_ref[b, :, width + TAIL :] = h_ref[0, 0]
        for q in range(0, chans, GS):
            rows = slice(q, q + GS)
            xhat, n, sig, slope, inv_std = norm_group(
                h_ref[0, 0, rows, :], gain[rows], bias[rows]
            )
            xhat_ref[b, rows, :] = xhat
            slope_ref[b, rows, :] = slope
            rate_ref[b, rows, :] = slope * (gain[rows] * inv_std)
            act_ref[b, rows, :] = (n * sig).astype(BF16)


def prepare(proj_weight, conv_weight, conv_one, conv_two, gain, bias):
    chans, width = proj_weight.shape[2:]
    positions = conv_one.shape[3]
    full = shape_of((2, chans, positions), F32)
    return pl.pallas_call(
        prepare_kernel,
        out_shape=(
            shape_of((2, chans, width + TAIL + positions), BF16),
            full,
            full,
            full,
            shape_of((2, chans, positions), BF16),
        ),
        in_specs=[VMEM] * 6,
        out_specs=[VMEM] * 5,
        compiler_params=PARAMS,
        name="prepare",
    )(proj_weight, conv_weight, conv_one, conv_two, gain, bias)


def wide_norm_kernel(taps, tail_ref, h_ref, xhat_ref, rate_ref):
    count, _, chans, _ = tail_ref.shape
    at = taps - 384
    for b in range(2):
        for y in range(count):
            side = tail_ref[y, b, :, 384:].astype(F32)
            gain = side[:, at : at + 1] + side[:, at + 1 : at + 2] + side[:, at + 2 : at + 3]
            bias = side[:, at + 3 : at + 4] + side[:, at + 4 : at + 5] + side[:, at + 5 : at + 6]
            for q in range(0, chans, GS):
                rows = slice(q, q + GS)
                xhat, _, _, slope, inv_std = norm_group(
                    h_ref[y, b, rows, :], gain[rows], bias[rows]
                )
                to = slice(y * chans + q, y * chans + q + GS)
                xhat_ref[b, to, :] = xhat
                rate_ref[b, to, :] = slope * (gain[rows] * inv_std)


def wide_norm(packs, width, positions):
    count, _, chans, _ = packs.shape
    full = shape_of((2, count * chans, positions), F32)
    return pl.pallas_call(
        functools.partial(wide_norm_kernel, 9 * GS),
        out_shape=(full, full),
        grid=(1,),
        in_specs=[
            pl.BlockSpec((count, 2, chans, TAIL), lambda i: (0, 0, 0, width // TAIL)),
            pl.BlockSpec(
                (count, 2, chans, positions),
                lambda i: (0, 0, 0, (width + TAIL) // positions),
            ),
        ],
        out_specs=[VMEM] * 2,
        compiler_params=PARAMS,
        name="wide_norm",
    )(packs, packs)


def shifted(value, step_row, step_col, row, col):
    length = value.shape[1]
    rows = length // WW
    by = step_row * WW + step_col
    if by == 0:
        return value
    moved = pltpu.roll(value, (-by) % length, axis=1)
    inside = None
    if step_row:
        inside = row < rows - 1 if step_row > 0 else row > 0
    if step_col:
        here = col < WW - 1 if step_col > 0 else col > 0
        inside = here if inside is None else inside & here
    return jnp.where(inside, moved, 0.0)


def grid_of(shape):
    lane = lax.broadcasted_iota(jnp.int32, shape, 1)
    return lane // WW, lane % WW


def own_positions(g, chan_at, count):
    down = lax.broadcasted_iota(jnp.int32, (count, g.shape[1]), 0)
    across = lax.broadcasted_iota(jnp.int32, (count, g.shape[1]), 1)
    pick = jnp.where(across == down + chan_at * count, 1.0, 0.0).astype(BF16)
    return lax.dot_general(pick, g, NT, preferred_element_type=F32).astype(BF16)


def block(b, wide, flags, g, ordered, params, state, saved, latent, make_latent):
    xhat, rate = state
    chans, positions = xhat.shape[1:]
    own_rows = params[0].shape[-2]
    whole = g.shape[0]
    slab = positions // (whole // own_rows)
    first = saved is None
    has_latent = latent is not None or make_latent
    scale = 1.0 / (GS * positions)
    per = whole // 2 // own_rows

    def kernel(*refs):
        refs = list(refs)
        take = lambda k: [refs.pop(0) for _ in range(k)]
        flags_ref, g_ref = take(2)
        weights = take(len(params))
        xhat_ref, rate_ref = take(2)
        if not first:
            take(3)
        if latent is not None:
            take(1)
        out_ref, sg_ref, sgh_ref, sga_ref = take(4)
        lat_ref = take(1)[0] if has_latent else None
        ga_buf, gh_buf, g_buf, sem = take(4)
        valid = flags_ref[0] > 0
        late = flags_ref[1] > 0
        chan_at = flags_ref[2]
        core = chan_at & 1
        if ordered:
            src = g_ref
        else:
            for c in range(2):
                for y in range(per):
                    to = (2 * y + c) * own_rows
                    at = (c * per + y) * own_rows
                    g_buf[to : to + own_rows, :] = g_ref[at : at + own_rows, :]
            src = g_buf
        keep = pltpu.make_async_copy(src, sg_ref, sem)

        @pl.when(valid)
        def _():
            keep.start()

        if wide:
            (pack_ref,) = weights
            width = whole
            for y in range(per):
                ga_buf[y * own_rows : (y + 1) * own_rows, :] = jnp.dot(
                    pack_ref[y, b, :, :width], src[...], preferred_element_type=F32
                )
        else:
            w_ref, wc_ref = weights
            ga_buf[...] = jnp.dot(w_ref[0, b], src[...], preferred_element_type=F32)
        row, col = grid_of((GS, positions))
        for at in range(0, chans, GS):
            y, q = divmod(at, own_rows)
            rows = slice(at, at + GS)
            if wide:
                taps_w = pack_ref[y, b, q : q + GS, width : width + 9 * GS]
                mine_at = (2 * y + core) * own_rows + q
            else:
                taps_w = wc_ref[0, b, q : q + GS, :]
                mine_at = chan_at * own_rows + q
            xhat_q = xhat_ref[b, rows, :]
            rw = ga_buf[rows, :] * rate_ref[b, rows, :]
            gh = rw - total(rw) * scale - xhat_q * (total(rw * xhat_q) * scale)
            gh = gh.astype(BF16)
            gh_buf[rows, :] = gh
            spread = lax.dot_general(taps_w, gh, TN, preferred_element_type=F32)
            branch = None
            for step_col in (-1, 0, 1):
                part = None
                for step_row in (-1, 0, 1):
                    tap = 3 * (step_row + 1) + step_col + 1
                    term = shifted(spread[tap * GS : (tap + 1) * GS, :], -step_row, 0, row, col)
                    part = term if part is None else part + term
                part = shifted(part, 0, -step_col, row, col)
                branch = part if branch is None else branch + part
            mine = src[pl.ds(pl.multiple_of(mine_at, GS), GS), :].astype(F32)
            out_ref[rows, :] = (mine + branch.astype(BF16).astype(F32)).astype(BF16)

        @pl.when(valid)
        def _():
            mine = (chan_at >> 1) * own_rows if wide else 0
            mine = pl.multiple_of(mine, own_rows) if wide else 0
            sgh_ref[...] = gh_buf[pl.ds(mine, own_rows), :]
            sga_ref[...] = ga_buf[pl.ds(mine, own_rows), :]
            keep.wait()

        if has_latent:

            @pl.when(late)
            def _():
                lat_ref[...] = own_positions(src[...], chan_at, slab)

    shapes = [
        shape_of((chans, positions), BF16),
        shape_of((whole, positions), BF16),
        shape_of((own_rows, positions), BF16),
        shape_of((own_rows, positions), F32),
    ]
    out_specs = [VMEM, ANY, VMEM, VMEM]
    operands = [flags, g, *params, xhat, rate]
    in_specs = [SMEM] + [VMEM] * (len(operands) - 1)
    aliases = {}
    if not first:
        for i, kept in enumerate(saved):
            aliases[len(operands)] = 1 + i
            operands.append(kept)
            in_specs.append(out_specs[1 + i])
    if has_latent:
        shapes.append(shape_of((slab, whole), BF16))
        out_specs.append(VMEM)
        if latent is not None:
            aliases[len(operands)] = 4
            operands.append(latent)
            in_specs.append(VMEM)
    result = pl.pallas_call(
        kernel,
        out_shape=shapes,
        in_specs=in_specs,
        out_specs=out_specs,
        scratch_shapes=[
            pltpu.VMEM((chans, positions), F32),
            pltpu.VMEM((chans, positions), BF16),
            pltpu.VMEM((8, 128) if ordered else (whole, positions), BF16),
            pltpu.SemaphoreType.DMA,
        ],
        input_output_aliases=aliases,
        compiler_params=PARAMS,
        name="wide_block" if wide else "own_block",
    )(*operands)
    return result[0], tuple(result[1:4]), result[4] if has_latent else latent


def weights_kernel(*refs):
    flags_ref, last_ref, lat_in_ref = refs[:3]
    act_ref, xhat_ref, slope_ref = refs[3:6]
    x_refs = refs[6:8]
    saved_refs = (refs[8:11], refs[11:14])
    out_ref, lat_ref, stack, g_buf = refs[14:]
    chans, positions = x_refs[0].shape[2:]
    width = out_ref.shape[1] - TAIL
    row, col = grid_of((GS, positions))
    lane = lax.broadcasted_iota(jnp.int32, (GS, TAIL), 1)
    stack[9 * GS :, :] = jnp.zeros((TAIL - 9 * GS, positions), BF16)
    for b in range(2):
        g_ref, gh_ref, ga_ref = saved_refs[b]
        x_ref = x_refs[b]
        at = b * chans
        out_ref[at : at + chans, :width] = lax.dot_general(
            act_ref[b], g_ref[...], NT, preferred_element_type=F32
        ).astype(BF16)
        for q in range(0, chans, GS):
            rows = slice(q, q + GS)
            x = x_ref[0, 0, rows, :].astype(F32)
            for step_row in (-1, 0, 1):
                for step_col in (-1, 0, 1):
                    tap = 3 * (step_row + 1) + step_col + 1
                    stack[tap * GS : (tap + 1) * GS, :] = shifted(
                        x, step_row, step_col, row, col
                    ).astype(BF16)
            taps = lax.dot_general(gh_ref[rows, :], stack[...], NT, preferred_element_type=F32)
            gn = ga_ref[rows, :] * slope_ref[b, rows, :]
            by_gain = jnp.sum(gn * xhat_ref[b, rows, :], axis=1, keepdims=True)
            by_bias = jnp.sum(gn, axis=1, keepdims=True)
            taps = jnp.where(lane == 9 * GS, by_gain, taps)
            taps = jnp.where(lane == 9 * GS + 1, by_bias, taps)
            out_ref[at + q : at + q + GS, width:] = taps.astype(BF16)
    lat_ref[...] = lat_in_ref[...]

    @pl.when(flags_ref[0] > 0)
    def _():
        per = last_ref.shape[0] // 2 // chans
        for c in range(2):
            for y in range(per):
                to = (2 * y + c) * chans
                src = (c * per + y) * chans
                g_buf[to : to + chans, :] = last_ref[src : src + chans, :]
        lat_ref[...] = own_positions(g_buf[...], flags_ref[2], lat_ref.shape[0])


def weight_grads(flags, last, latent, act, xhat, slope, inputs, saved):
    chans, positions = act.shape[1:]
    width = last.shape[0]
    return pl.pallas_call(
        weights_kernel,
        out_shape=(
            shape_of((2 * chans, width + TAIL), BF16),
            shape_of(latent.shape, BF16),
        ),
        in_specs=[SMEM] + [VMEM] * 13,
        out_specs=[VMEM] * 2,
        scratch_shapes=[
            pltpu.VMEM((TAIL, positions), BF16),
            pltpu.VMEM((width, positions), BF16),
        ],
        compiler_params=PARAMS,
        name="weight_grads",
    )(flags, last, latent, act, xhat, slope, *inputs, *saved[0], *saved[1])


def reduce_kernel(in_ref, out_ref):
    count = in_ref.shape[0]
    acc = in_ref[0].astype(F32)
    for m in range(1, count):
        acc = acc + in_ref[m].astype(F32)
    done = acc.astype(BF16)
    for m in range(count):
        out_ref[m] = done


def spread_sum(parts):
    return pl.pallas_call(
        reduce_kernel,
        out_shape=shape_of(parts.shape, BF16),
        in_specs=[VMEM],
        out_specs=VMEM,
        compiler_params=PARAMS,
        name="sum_microbatches",
    )(parts)


def widen_kernel(in_ref, proj_ref, conv_ref, gain_ref, bias_ref):
    chans, width = proj_ref.shape[2:]
    down = lax.broadcasted_iota(jnp.int32, (chans, chans), 0)
    across = lax.broadcasted_iota(jnp.int32, (chans, chans), 1)
    at = 9 * GS - (TAIL - 128)
    for b in range(2):
        rows = slice(b * chans, (b + 1) * chans)
        proj_ref[0, b] = in_ref[rows, :width].astype(F32)
        conv_ref[0, b] = in_ref[rows, width : width + 9 * GS].astype(F32)
        tail = in_ref[rows, width + TAIL - 128 :].astype(F32)
        for i, ref in enumerate((gain_ref, bias_ref)):
            lined = jnp.where(down == across, tail[:, at + i : at + i + 1], 0.0)
            ref[0, b : b + 1, :] = jnp.sum(lined, axis=0, keepdims=True)


def widen(sums, chans, width):
    return pl.pallas_call(
        widen_kernel,
        out_shape=(
            shape_of((1, 2, chans, width), F32),
            shape_of((1, 2, chans, 9 * GS), F32),
            shape_of((1, 2, chans), F32),
            shape_of((1, 2, chans), F32),
        ),
        in_specs=[VMEM],
        out_specs=[VMEM] * 4,
        compiler_params=PARAMS,
        name="widen",
    )(sums)


def gather(block_, axis, groups=None):
    return lax.all_gather(block_, axis, axis=0, tiled=True, axis_index_groups=groups)


def per_device(
    grad_top,
    inputs_one,
    conv_one,
    inputs_two,
    conv_two,
    proj_weight,
    conv_weight,
    norm_gain,
    norm_bias,
):
    segments = lax.axis_size("segment")
    segment_at = lax.axis_index("segment")
    chan_at = lax.axis_index("chan")
    members = lax.axis_size("dp")
    shards = lax.axis_size("chan")
    chans, positions = conv_one.shape[2:]
    width = proj_weight.shape[3]
    cores = [[2 * y, 2 * y + 1] for y in range(shards // 2)]
    columns = [[2 * y + c for y in range(shards // 2)] for c in range(2)]

    pack, xhat, slope, rate, act = prepare(
        proj_weight, conv_weight, conv_one, conv_two, norm_gain, norm_bias
    )
    packs = gather(pack, "chan", columns).reshape((shards // 2,) + pack.shape)
    own = (proj_weight, conv_weight)
    wide_state = None
    saved = [None, None]
    latent = None
    out = None
    for tick in range(segments):
        flags = jnp.stack(
            [
                (segment_at == segments - 1 - tick).astype(jnp.int32),
                (segment_at == segments - tick).astype(jnp.int32),
                chan_at.astype(jnp.int32),
            ]
        )
        if tick == 0:
            g = lax.all_gather(grad_top[0], "chan", axis=1, tiled=True)
        else:
            lower = segments - 1 - tick
            rest = [s for s in range(segments) if s not in (lower, lower + 1)]
            groups = sorted(
                [[lower, lower + 1]] + [rest[i : i + 2] for i in range(0, len(rest), 2)]
            )
            half = out.shape[0]
            moved = gather(out, "segment", groups)[half:]
            g = gather(moved, "chan", None if half == chans else cores)
        for b in (1, 0):
            ordered = tick == 0 or out.shape[0] == chans
            wide = tick > 1 or (tick == 1 and b == 0)
            if wide and wide_state is None:
                packs, g = lax.optimization_barrier((packs, g))
                wide_state = wide_norm(packs, width, positions)
            out, saved[b], kept = block(
                b,
                wide,
                flags,
                g,
                ordered,
                (packs,) if wide else own,
                wide_state if wide else (xhat, rate),
                saved[b],
                latent if b == 1 else None,
                b == 1 and tick == 1,
            )
            latent = kept if b == 1 else latent
            if b == 1 or tick == segments - 1:
                g = gather(out, "chan", None if out.shape[0] == chans else cores)

    grads, latent = weight_grads(
        flags, g, latent, act, xhat, slope, (inputs_one, inputs_two), saved
    )
    parts = grads.reshape(members, 2 * chans // members, width + TAIL)
    parts = lax.all_to_all(parts, "dp", split_axis=0, concat_axis=0, tiled=True)
    parts = spread_sum(parts)
    parts = lax.all_to_all(parts, "dp", split_axis=0, concat_axis=0, tiled=True)
    proj, conv, by_gain, by_bias = widen(parts.reshape(2 * chans, width + TAIL), chans, width)
    return latent.T[None, None], proj, conv, by_gain, by_bias


def solution(mesh):
    return jax.shard_map(
        per_device,
        mesh=mesh,
        in_specs=(
            P("dp", None, "chan"),
            P("segment", "dp", "chan", None),
            P("segment", "dp", "chan", None),
            P("segment", "dp", "chan", None),
            P("segment", "dp", "chan", None),
            P("segment", None, "chan", None),
            P("segment", None, "chan", None),
            P("segment", None, "chan"),
            P("segment", None, "chan"),
        ),
        out_specs=(
            P("segment", "dp", None, "chan"),
            P("segment", None, "chan", None),
            P("segment", None, "chan", None),
            P("segment", None, "chan"),
            P("segment", None, "chan"),
        ),
        check_vma=False,
    )
```

```python
import functools

import jax
import jax.numpy as jnp
from jax import lax
from jax.experimental import pallas as pl
from jax.experimental.pallas import tpu as pltpu
from jax.sharding import PartitionSpec as P

GS = 48
WW = 64
NORM_EPS = 1e-05
TAIL = 512
F32 = jnp.float32
BF16 = jnp.bfloat16
VMEM = pl.BlockSpec(memory_space=pltpu.VMEM)
SMEM = pl.BlockSpec(memory_space=pltpu.SMEM)
ANY = pl.BlockSpec(memory_space=pl.ANY)
NT = (((1,), (1,)), ((), ()))
TN = (((0,), (0,)), ((), ()))
PARAMS = pltpu.CompilerParams(vmem_limit_bytes=32 * 1024 * 1024)


def shape_of(shape, dtype):
    return jax.ShapeDtypeStruct(shape, dtype)


def total(block):
    return jnp.sum(jnp.sum(block, axis=1, keepdims=True), axis=0, keepdims=True)


def norm_group(h, gain, bias):
    scale = 1.0 / (h.shape[0] * h.shape[1])
    pre = h.astype(F32)
    pre = pre - total(pre) * scale
    inv_std = lax.rsqrt(total(pre * pre) * scale + NORM_EPS)
    xhat = pre * inv_std
    n = xhat * gain + bias
    sig = jax.nn.sigmoid(n)
    slope = sig * (1.0 + n * (1.0 - sig))
    return xhat, n, sig, slope, inv_std


def column(line):
    count = line.shape[1]
    down = lax.broadcasted_iota(jnp.int32, (count, count), 0)
    across = lax.broadcasted_iota(jnp.int32, (count, count), 1)
    return jnp.sum(jnp.where(down == across, line, 0.0), axis=1, keepdims=True)


def prepare_kernel(*refs):
    pack_refs = (refs[6], refs[7])
    xhat_ref, slope_ref, rate_ref, act_ref = refs[8:12]
    w_ref, wc_ref, h1_ref, h2_ref, gain_ref, bias_ref, sems = refs[12:]
    copies = [
        pltpu.make_async_copy(refs[i], refs[12 + i], sems.at[i]) for i in range(6)
    ]
    for copy in copies:
        copy.start()
    for copy in copies:
        copy.wait()
    chans, width = w_ref.shape[2:]
    taps = wc_ref.shape[3]
    lane = lax.broadcasted_iota(jnp.int32, (chans, TAIL - 384), 1)
    for b, h_ref in ((1, h2_ref), (0, h1_ref)):
        pack_ref = pack_refs[b]
        pack_ref[:, :width] = w_ref[0, b]
        pack_ref[:, width : width + 384] = wc_ref[0, b, :, :384]
        last = wc_ref[0, b, :, 384:].astype(F32)
        last = jnp.concatenate(
            [last, jnp.zeros((chans, TAIL - taps), F32)], axis=1
        )
        gain = column(gain_ref[0, b : b + 1, :])
        bias = column(bias_ref[0, b : b + 1, :])
        at = taps - 384
        for whole in (gain, bias):
            rest = whole
            for _ in range(3):
                piece = rest.astype(BF16).astype(F32)
                rest = rest - piece
                last = jnp.where(lane == at, piece, last)
                at += 1
        pack_ref[:, width + 384 : width + TAIL] = last.astype(BF16)
        pack_ref[:, width + TAIL :] = h_ref[0, 0]
        for q in range(0, chans, GS):
            rows = slice(q, q + GS)
            xhat, n, sig, slope, inv_std = norm_group(
                h_ref[0, 0, rows, :], gain[rows], bias[rows]
            )
            xhat_ref[b, rows, :] = xhat
            slope_ref[b, rows, :] = slope
            rate_ref[b, rows, :] = slope * (gain[rows] * inv_std)
            act_ref[b, rows, :] = (n * sig).astype(BF16)


def prepare(*operands):
    chans, width = operands[0].shape[2:]
    positions = operands[2].shape[3]
    full = shape_of((2, chans, positions), F32)
    pack = shape_of((chans, width + TAIL + positions), BF16)
    return pl.pallas_call(
        prepare_kernel,
        out_shape=(pack, pack, full, full, full, shape_of((2, chans, positions), BF16)),
        in_specs=[pl.BlockSpec(memory_space=pltpu.HBM)] * 6,
        out_specs=[VMEM] * 6,
        scratch_shapes=[pltpu.VMEM(x.shape, x.dtype) for x in operands]
        + [pltpu.SemaphoreType.DMA((6,))],
        compiler_params=PARAMS,
        name="prepare",
    )(*operands)


def wide_norm_kernel(width, pack_ref, xhat_ref, rate_ref):
    chans = pack_ref.shape[0]
    at = 9 * GS - 384
    for q in range(0, chans, GS):
        rows = slice(q, q + GS)
        side = pack_ref[rows, width + 384 : width + TAIL].astype(F32)
        gain = side[:, at : at + 1] + side[:, at + 1 : at + 2] + side[:, at + 2 : at + 3]
        bias = side[:, at + 3 : at + 4] + side[:, at + 4 : at + 5] + side[:, at + 5 : at + 6]
        xhat, _, _, slope, inv_std = norm_group(pack_ref[rows, width + TAIL :], gain, bias)
        xhat_ref[0, rows, :] = xhat
        rate_ref[0, rows, :] = slope * (gain * inv_std)


def wide_norm(pack, width, positions):
    full = shape_of((1, pack.shape[0], positions), F32)
    return pl.pallas_call(
        functools.partial(wide_norm_kernel, width),
        out_shape=(full, full),
        in_specs=[VMEM],
        out_specs=[VMEM] * 2,
        compiler_params=PARAMS,
        name="wide_norm",
    )(pack)


def shifted(value, step_row, step_col, row, col):
    length = value.shape[1]
    rows = length // WW
    by = step_row * WW + step_col
    if by == 0:
        return value
    moved = pltpu.roll(value, (-by) % length, axis=1)
    inside = None
    if step_row:
        inside = row < rows - 1 if step_row > 0 else row > 0
    if step_col:
        here = col < WW - 1 if step_col > 0 else col > 0
        inside = here if inside is None else inside & here
    return jnp.where(inside, moved, 0.0)


def grid_of(shape):
    lane = lax.broadcasted_iota(jnp.int32, shape, 1)
    return lane // WW, lane % WW


def own_positions(g, chan_at, count):
    down = lax.broadcasted_iota(jnp.int32, (count, g.shape[1]), 0)
    across = lax.broadcasted_iota(jnp.int32, (count, g.shape[1]), 1)
    pick = jnp.where(across == down + chan_at * count, 1.0, 0.0).astype(BF16)
    return lax.dot_general(pick, g, NT, preferred_element_type=F32).astype(BF16)


def block(
    b, wide, flags, g, ordered, own_chans, params, state, saved, latent, make_latent
):
    xhat, rate = state
    chans, positions = xhat.shape[1:]
    own_rows = own_chans
    at_b = 0 if wide else b
    whole = g.shape[0]
    slab = positions // (whole // own_rows)
    first = saved is None
    has_latent = latent is not None or make_latent
    scale = 1.0 / (GS * positions)
    per = whole // 2 // own_rows

    def kernel(*refs):
        refs = list(refs)
        take = lambda k: [refs.pop(0) for _ in range(k)]
        flags_ref, g_ref = take(2)
        weights = take(len(params))
        xhat_ref, rate_ref = take(2)
        if not first:
            take(3)
        if latent is not None:
            take(1)
        out_ref, sg_ref, sgh_ref, sga_ref = take(4)
        lat_ref = take(1)[0] if has_latent else None
        ga_buf, gh_buf, g_buf, sem = take(4)
        valid = flags_ref[0] > 0
        late = flags_ref[1] > 0
        chan_at = flags_ref[2]
        core = chan_at & 1
        if ordered:
            src = g_ref
        else:
            for c in range(2):
                for y in range(per):
                    to = (2 * y + c) * own_rows
                    at = (c * per + y) * own_rows
                    g_buf[to : to + own_rows, :] = g_ref[at : at + own_rows, :]
            src = g_buf
        keep = pltpu.make_async_copy(src, sg_ref, sem)

        @pl.when(valid)
        def _():
            keep.start()

        if wide:
            (pack_ref,) = weights
            width = whole
            ga_buf[...] = jnp.dot(
                pack_ref[:, :width], src[...], preferred_element_type=F32
            )
        else:
            w_ref, wc_ref = weights
            ga_buf[...] = jnp.dot(w_ref[0, b], src[...], preferred_element_type=F32)
        row, col = grid_of((GS, positions))
        for at in range(0, chans, GS):
            y, q = divmod(at, own_rows)
            rows = slice(at, at + GS)
            if wide:
                taps_w = pack_ref[rows, width : width + 9 * GS]
                mine_at = (2 * y + core) * own_rows + q
            else:
                taps_w = wc_ref[0, b, q : q + GS, :]
                mine_at = chan_at * own_rows + q
            xhat_q = xhat_ref[at_b, rows, :]
            rw = ga_buf[rows, :] * rate_ref[at_b, rows, :]
            gh = rw - total(rw) * scale - xhat_q * (total(rw * xhat_q) * scale)
            gh = gh.astype(BF16)
            gh_buf[rows, :] = gh
            spread = lax.dot_general(taps_w, gh, TN, preferred_element_type=F32)
            branch = None
            for step_col in (-1, 0, 1):
                part = None
                for step_row in (-1, 0, 1):
                    tap = 3 * (step_row + 1) + step_col + 1
                    term = shifted(spread[tap * GS : (tap + 1) * GS, :], -step_row, 0, row, col)
                    part = term if part is None else part + term
                part = shifted(part, 0, -step_col, row, col)
                branch = part if branch is None else branch + part
            mine = src[pl.ds(pl.multiple_of(mine_at, GS), GS), :].astype(F32)
            out_ref[rows, :] = (mine + branch.astype(BF16).astype(F32)).astype(BF16)

        @pl.when(valid)
        def _():
            mine = (chan_at >> 1) * own_rows if wide else 0
            mine = pl.multiple_of(mine, own_rows) if wide else 0
            sgh_ref[...] = gh_buf[pl.ds(mine, own_rows), :]
            sga_ref[...] = ga_buf[pl.ds(mine, own_rows), :]
            keep.wait()

        if has_latent:

            @pl.when(late)
            def _():
                lat_ref[...] = own_positions(src[...], chan_at, slab)

    shapes = [
        shape_of((chans, positions), BF16),
        shape_of((whole, positions), BF16),
        shape_of((own_rows, positions), BF16),
        shape_of((own_rows, positions), F32),
    ]
    out_specs = [VMEM, ANY, VMEM, VMEM]
    operands = [flags, g, *params, xhat, rate]
    in_specs = [SMEM] + [VMEM] * (len(operands) - 1)
    aliases = {}
    if not first:
        for i, kept in enumerate(saved):
            aliases[len(operands)] = 1 + i
            operands.append(kept)
            in_specs.append(out_specs[1 + i])
    if has_latent:
        shapes.append(shape_of((slab, whole), BF16))
        out_specs.append(VMEM)
        if latent is not None:
            aliases[len(operands)] = 4
            operands.append(latent)
            in_specs.append(VMEM)
    result = pl.pallas_call(
        kernel,
        out_shape=shapes,
        in_specs=in_specs,
        out_specs=out_specs,
        scratch_shapes=[
            pltpu.VMEM((chans, positions), F32),
            pltpu.VMEM((chans, positions), BF16),
            pltpu.VMEM((8, 128) if ordered else (whole, positions), BF16),
            pltpu.SemaphoreType.DMA,
        ],
        input_output_aliases=aliases,
        compiler_params=PARAMS,
        name="wide_block" if wide else "own_block",
    )(*operands)
    return result[0], tuple(result[1:4]), result[4] if has_latent else latent


def weight_blocks(b, act_ref, xhat_ref, slope_ref, x_ref, saved_refs, stack, store):
    g_ref, gh_ref, ga_ref = saved_refs
    chans, positions = x_ref.shape[2:]
    width = g_ref.shape[0]
    row, col = grid_of((GS, positions))
    lane = lax.broadcasted_iota(jnp.int32, (GS, TAIL), 1)
    stack[9 * GS :, :] = jnp.zeros((TAIL - 9 * GS, positions), BF16)
    store(
        slice(0, chans),
        0,
        lax.dot_general(act_ref[b], g_ref[...], NT, preferred_element_type=F32).astype(BF16),
    )
    for q in range(0, chans, GS):
        rows = slice(q, q + GS)
        x = x_ref[0, 0, rows, :].astype(F32)
        for step_row in (-1, 0, 1):
            for step_col in (-1, 0, 1):
                tap = 3 * (step_row + 1) + step_col + 1
                stack[tap * GS : (tap + 1) * GS, :] = shifted(
                    x, step_row, step_col, row, col
                ).astype(BF16)
        taps = lax.dot_general(gh_ref[rows, :], stack[...], NT, preferred_element_type=F32)
        gn = ga_ref[rows, :] * slope_ref[b, rows, :]
        by_gain = jnp.sum(gn * xhat_ref[b, rows, :], axis=1, keepdims=True)
        by_bias = jnp.sum(gn, axis=1, keepdims=True)
        taps = jnp.where(lane == 9 * GS, by_gain, taps)
        taps = jnp.where(lane == 9 * GS + 1, by_bias, taps)
        store(rows, width, taps.astype(BF16))


def storer(out_ref, first_row):
    step = out_ref.shape[2]

    def store(rows, at, value):
        to = slice(first_row + rows.start, first_row + rows.stop)
        for i in range(value.shape[1] // step):
            out_ref[at // step + i, to, :] = value[:, i * step : (i + 1) * step]

    return store


def early_kernel(act_ref, xhat_ref, slope_ref, x_ref, g_ref, gh_ref, ga_ref, out_ref, stack):
    weight_blocks(
        1, act_ref, xhat_ref, slope_ref, x_ref, (g_ref, gh_ref, ga_ref), stack,
        storer(out_ref, 0),
    )


def early_grads(members, act, xhat, slope, x, saved):
    chans, positions = act.shape[1:]
    step = (saved[0].shape[0] + TAIL) // members
    return pl.pallas_call(
        early_kernel,
        out_shape=shape_of((members, chans, step), BF16),
        in_specs=[VMEM] * 7,
        out_specs=VMEM,
        scratch_shapes=[pltpu.VMEM((TAIL, positions), BF16)],
        compiler_params=PARAMS,
        name="early_weight_grads",
    )(act, xhat, slope, x, *saved)


def summed(in_ref, rows):
    acc = in_ref[0, rows, :].astype(F32)
    for m in range(1, in_ref.shape[0]):
        acc = acc + in_ref[m, rows, :].astype(F32)
    return acc.astype(BF16)


def late_kernel(
    flags_ref, last_ref, lat_in_ref, parts_ref, act_ref, xhat_ref, slope_ref, x_ref,
    g_ref, gh_ref, ga_ref, out_ref, lat_ref, stack, g_buf,
):
    chans = x_ref.shape[2]
    weight_blocks(
        0, act_ref, xhat_ref, slope_ref, x_ref, (g_ref, gh_ref, ga_ref), stack,
        storer(out_ref, chans),
    )
    done = summed(parts_ref, slice(0, chans))
    for m in range(out_ref.shape[0]):
        out_ref[m, :chans, :] = done
    lat_ref[...] = lat_in_ref[...]

    @pl.when(flags_ref[0] > 0)
    def _():
        per = last_ref.shape[0] // 2 // chans
        for c in range(2):
            for y in range(per):
                to = (2 * y + c) * chans
                src = (c * per + y) * chans
                g_buf[to : to + chans, :] = last_ref[src : src + chans, :]
        lat_ref[...] = own_positions(g_buf[...], flags_ref[2], lat_ref.shape[0])


def late_grads(flags, last, latent, parts, act, xhat, slope, x, saved):
    members, chans, step = parts.shape
    positions = act.shape[2]
    return pl.pallas_call(
        late_kernel,
        out_shape=(
            shape_of((members, 2 * chans, step), BF16),
            shape_of(latent.shape, BF16),
        ),
        in_specs=[SMEM] + [VMEM] * 10,
        out_specs=[VMEM] * 2,
        scratch_shapes=[
            pltpu.VMEM((TAIL, positions), BF16),
            pltpu.VMEM(last.shape, BF16),
        ],
        compiler_params=PARAMS,
        name="late_weight_grads",
    )(flags, last, latent, parts, act, xhat, slope, x, *saved)


def sum_kernel(in_ref, out_ref):
    chans = out_ref.shape[1]
    done = summed(in_ref, slice(chans, 2 * chans))
    for m in range(out_ref.shape[0]):
        out_ref[m] = done


def late_sums(parts):
    members, rows, step = parts.shape
    return pl.pallas_call(
        sum_kernel,
        out_shape=shape_of((members, rows // 2, step), BF16),
        in_specs=[VMEM],
        out_specs=VMEM,
        compiler_params=PARAMS,
        name="sum_microbatches",
    )(parts)


def widen_kernel(late_ref, early_ref, proj_ref, conv_ref, gain_ref, bias_ref):
    chans, width = proj_ref.shape[2:]
    step = late_ref.shape[2]
    down = lax.broadcasted_iota(jnp.int32, (chans, chans), 0)
    across = lax.broadcasted_iota(jnp.int32, (chans, chans), 1)
    first = width // step
    for b, ref in ((0, late_ref), (1, early_ref)):
        for i in range(first):
            proj_ref[0, b, :, i * step : (i + 1) * step] = ref[i, :chans, :].astype(F32)
        conv_ref[0, b, :, :step] = ref[first, :chans, :].astype(F32)
        side = ref[first + 1, :chans, :].astype(F32)
        conv_ref[0, b, :, step:] = side[:, : 9 * GS - step]
        for i, to in enumerate((gain_ref, bias_ref)):
            at = 9 * GS - step + i
            lined = jnp.where(down == across, side[:, at : at + 1], 0.0)
            to[0, b : b + 1, :] = jnp.sum(lined, axis=0, keepdims=True)


def widen(late, early, width):
    chans = late.shape[1]
    return pl.pallas_call(
        widen_kernel,
        out_shape=(
            shape_of((1, 2, chans, width), F32),
            shape_of((1, 2, chans, 9 * GS), F32),
            shape_of((1, 2, chans), F32),
            shape_of((1, 2, chans), F32),
        ),
        in_specs=[VMEM] * 2,
        out_specs=[VMEM] * 4,
        compiler_params=PARAMS,
        name="widen",
    )(late, early)


def gather(block_, axis, groups=None):
    return lax.all_gather(block_, axis, axis=0, tiled=True, axis_index_groups=groups)


def per_device(
    grad_top,
    inputs_one,
    conv_one,
    inputs_two,
    conv_two,
    proj_weight,
    conv_weight,
    norm_gain,
    norm_bias,
):
    segments = lax.axis_size("segment")
    segment_at = lax.axis_index("segment")
    chan_at = lax.axis_index("chan")
    members = lax.axis_size("dp")
    shards = lax.axis_size("chan")
    chans, positions = conv_one.shape[2:]
    width = proj_weight.shape[3]
    cores = [[2 * y, 2 * y + 1] for y in range(shards // 2)]
    columns = [[2 * y + c for y in range(shards // 2)] for c in range(2)]

    def near(own_only):
        return ("chan", None) if own_only else ("chan", cores)

    def exchange(blocks):
        return lax.all_to_all(blocks, "dp", split_axis=0, concat_axis=0, tiled=True)

    first_pack, second_pack, xhat, slope, rate, act = prepare(
        proj_weight, conv_weight, conv_one, conv_two, norm_gain, norm_bias
    )
    packs = [None, gather(second_pack, "chan", columns)]
    packs[0] = lax.all_gather(
        first_pack[None], "chan", axis=1, tiled=True, axis_index_groups=columns
    )[0]
    own = (proj_weight, conv_weight)
    wide_state = [None, None]
    saved = [None, None]
    latent = None
    out = None
    ordered = True
    parts = None
    for tick in range(segments):
        flags = jnp.stack(
            [
                (segment_at == segments - 1 - tick).astype(jnp.int32),
                (segment_at == segments - tick).astype(jnp.int32),
                chan_at.astype(jnp.int32),
            ]
        )
        if tick == 0:
            g = lax.all_gather(grad_top[0], "chan", axis=1, tiled=True)
        else:
            lower = segments - 1 - tick
            rest = [s for s in range(segments) if s not in (lower, lower + 1)]
            groups = sorted(
                [[lower, lower + 1]] + [rest[i : i + 2] for i in range(0, len(rest), 2)]
            )
            half = out.shape[0]
            g = gather(gather(out, "segment", groups)[half:], *near(half == chans))
        for b in (1, 0):
            wide = tick > 1 or (tick == 1 and b == 1)
            if wide and wide_state[b] is None:
                packs[b], g = lax.optimization_barrier((packs[b], g))
                wide_state[b] = wide_norm(packs[b], width, positions)
            out, saved[b], kept = block(
                b,
                wide,
                flags,
                g,
                ordered,
                chans,
                (packs[b],) if wide else own,
                wide_state[b] if wide else (xhat, rate),
                saved[b],
                latent if b == 1 else None,
                b == 1 and tick == 1,
            )
            latent = kept if b == 1 else latent
            ordered = out.shape[0] == chans
            if b == 1 and tick == segments - 1:
                parts = exchange(
                    early_grads(members, act, xhat, slope, inputs_two, saved[1])
                )
            if b == 1 or tick == segments - 1:
                g = gather(out, *near(ordered))

    both, latent = late_grads(
        flags, g, latent, parts, act, xhat, slope, inputs_one, saved[0]
    )
    both = exchange(both)
    late = exchange(late_sums(both))
    proj, conv, by_gain, by_bias = widen(late, both, width)
    return latent.T[None, None], proj, conv, by_gain, by_bias


def solution(mesh):
    return jax.shard_map(
        per_device,
        mesh=mesh,
        in_specs=(
            P("dp", None, "chan"),
            P("segment", "dp", "chan", None),
            P("segment", "dp", "chan", None),
            P("segment", "dp", "chan", None),
            P("segment", "dp", "chan", None),
            P("segment", None, "chan", None),
            P("segment", None, "chan", None),
            P("segment", None, "chan"),
            P("segment", None, "chan"),
        ),
        out_specs=(
            P("segment", "dp", None, "chan"),
            P("segment", None, "chan", None),
            P("segment", None, "chan", None),
            P("segment", None, "chan"),
            P("segment", None, "chan"),
        ),
        check_vma=False,
    )
```

```python
import functools

import jax
import jax.numpy as jnp
from jax import lax
from jax.experimental import pallas as pl
from jax.experimental.pallas import tpu as pltpu
from jax.sharding import PartitionSpec as P

GS = 48
WW = 64
NORM_EPS = 1e-05
TAIL = 512
F32 = jnp.float32
BF16 = jnp.bfloat16
VMEM = pl.BlockSpec(memory_space=pltpu.VMEM)
SMEM = pl.BlockSpec(memory_space=pltpu.SMEM)
ANY = pl.BlockSpec(memory_space=pl.ANY)
NT = (((1,), (1,)), ((), ()))
TN = (((0,), (0,)), ((), ()))


def vmem(mebibytes):
    return pltpu.CompilerParams(vmem_limit_bytes=mebibytes * 1024 * 1024)


def shape_of(shape, dtype):
    return jax.ShapeDtypeStruct(shape, dtype)


def total(block):
    return jnp.sum(jnp.sum(block, axis=1, keepdims=True), axis=0, keepdims=True)


def norm_group(h, gain, bias):
    scale = 1.0 / (h.shape[0] * h.shape[1])
    pre = h.astype(F32)
    pre = pre - total(pre) * scale
    inv_std = lax.rsqrt(total(pre * pre) * scale + NORM_EPS)
    xhat = pre * inv_std
    n = xhat * gain + bias
    sig = jax.nn.sigmoid(n)
    slope = sig * (1.0 + n * (1.0 - sig))
    return xhat, n, sig, slope, inv_std


def column(line):
    count = line.shape[1]
    down = lax.broadcasted_iota(jnp.int32, (count, count), 0)
    across = lax.broadcasted_iota(jnp.int32, (count, count), 1)
    return jnp.sum(jnp.where(down == across, line, 0.0), axis=1, keepdims=True)


def prepare_kernel(*refs):
    pack_refs = (refs[6], refs[7])
    xhat_ref, slope_ref, rate_ref, act_ref = refs[8:12]
    w_ref, wc_ref, h1_ref, h2_ref, gain_ref, bias_ref, sems = refs[12:]
    copies = [
        pltpu.make_async_copy(refs[i], refs[12 + i], sems.at[i]) for i in range(6)
    ]
    for copy in copies:
        copy.start()
    for copy in copies:
        copy.wait()
    chans, width = w_ref.shape[2:]
    taps = wc_ref.shape[3]
    lane = lax.broadcasted_iota(jnp.int32, (chans, TAIL - 384), 1)
    for b, h_ref in ((1, h2_ref), (0, h1_ref)):
        pack_ref = pack_refs[b]
        pack_ref[:, :width] = w_ref[0, b]
        pack_ref[:, width : width + 384] = wc_ref[0, b, :, :384]
        last = wc_ref[0, b, :, 384:].astype(F32)
        last = jnp.concatenate(
            [last, jnp.zeros((chans, TAIL - taps), F32)], axis=1
        )
        gain = column(gain_ref[0, b : b + 1, :])
        bias = column(bias_ref[0, b : b + 1, :])
        at = taps - 384
        for whole in (gain, bias):
            rest = whole
            for _ in range(3):
                piece = rest.astype(BF16).astype(F32)
                rest = rest - piece
                last = jnp.where(lane == at, piece, last)
                at += 1
        pack_ref[:, width + 384 : width + TAIL] = last.astype(BF16)
        pack_ref[:, width + TAIL :] = h_ref[0, 0]
        for q in range(0, chans, GS):
            rows = slice(q, q + GS)
            xhat, n, sig, slope, inv_std = norm_group(
                h_ref[0, 0, rows, :], gain[rows], bias[rows]
            )
            xhat_ref[b, rows, :] = xhat
            slope_ref[b, rows, :] = slope
            rate_ref[b, rows, :] = slope * (gain[rows] * inv_std)
            act_ref[b, rows, :] = (n * sig).astype(BF16)


def prepare(*operands):
    chans, width = operands[0].shape[2:]
    positions = operands[2].shape[3]
    full = shape_of((2, chans, positions), F32)
    pack = shape_of((chans, width + TAIL + positions), BF16)
    return pl.pallas_call(
        prepare_kernel,
        out_shape=(pack, pack, full, full, full, shape_of((2, chans, positions), BF16)),
        in_specs=[pl.BlockSpec(memory_space=pltpu.HBM)] * 6,
        out_specs=[VMEM] * 6,
        scratch_shapes=[pltpu.VMEM(x.shape, x.dtype) for x in operands]
        + [pltpu.SemaphoreType.DMA((6,))],
        compiler_params=vmem(56),
        name="prepare",
    )(*operands)


def shifted(value, step_row, step_col, row, col):
    length = value.shape[1]
    rows = length // WW
    by = step_row * WW + step_col
    if by == 0:
        return value
    moved = pltpu.roll(value, (-by) % length, axis=1)
    inside = None
    if step_row:
        inside = row < rows - 1 if step_row > 0 else row > 0
    if step_col:
        here = col < WW - 1 if step_col > 0 else col > 0
        inside = here if inside is None else inside & here
    return jnp.where(inside, moved, 0.0)


def grid_of(shape):
    lane = lax.broadcasted_iota(jnp.int32, shape, 1)
    return lane // WW, lane % WW


def own_positions(g, chan_at, count):
    down = lax.broadcasted_iota(jnp.int32, (count, g.shape[1]), 0)
    across = lax.broadcasted_iota(jnp.int32, (count, g.shape[1]), 1)
    pick = jnp.where(across == down + chan_at * count, 1.0, 0.0).astype(BF16)
    return lax.dot_general(pick, g, NT, preferred_element_type=F32).astype(BF16)


def block(b, mode, flags, g, ordered, own_rows, params, state):
    whole, positions = g.shape
    per = whole // 2 // own_rows
    chans = own_rows if mode == "own" else per * own_rows
    width = whole
    scale = 1.0 / (GS * positions)
    at_b = b if mode == "own" else 0

    def kernel(*refs):
        refs = list(refs)
        take = lambda k: [refs.pop(0) for _ in range(k)]
        flags_ref, g_ref = take(2)
        weights = take(len(params))
        state_refs = take(0 if mode == "first" else 2)
        out_ref, gh_ref, ga_ref = take(3)
        if mode == "first":
            xhat_ref, rate_ref = take(2)
            w_ref, taps_ref, h_ref, sems = take(4)
            (pack_ref,) = weights
            loads = [
                pltpu.make_async_copy(pack_ref.at[:, at : at + n], to, sems.at[i])
                for i, (at, n, to) in enumerate(
                    (
                        (width + TAIL, positions, h_ref),
                        (width, TAIL, taps_ref),
                        (0, width, w_ref),
                    )
                )
            ]
            for load in loads:
                load.start()
        else:
            xhat_ref, rate_ref = state_refs
        (g_buf,) = refs
        chan_at = flags_ref[1]
        core = chan_at & 1
        if ordered:
            src = g_ref
        else:
            for c in range(2):
                for y in range(per):
                    to = (2 * y + c) * own_rows
                    at = (c * per + y) * own_rows
                    g_buf[to : to + own_rows, :] = g_ref[at : at + own_rows, :]
            src = g_buf

        if mode == "first":
            loads[0].wait()
            loads[1].wait()
            at = 9 * GS - 384
            for q in range(0, chans, GS):
                rows = slice(q, q + GS)
                side = taps_ref[rows, 384:].astype(F32)
                gain, bias = (
                    side[:, i : i + 1] + side[:, i + 1 : i + 2] + side[:, i + 2 : i + 3]
                    for i in (at, at + 3)
                )
                xhat, _, _, slope, inv_std = norm_group(h_ref[rows, :], gain, bias)
                xhat_ref[0, rows, :] = xhat
                rate_ref[0, rows, :] = slope * (gain * inv_std)
            loads[2].wait()
            matrix = w_ref[...]
        elif mode == "wide":
            (pack_ref,) = weights
            matrix = pack_ref[:, :width]
        else:
            matrix = weights[0][0, b]
        ga_ref[...] = jnp.dot(matrix, src[...], preferred_element_type=F32)
        row, col = grid_of((GS, positions))
        for at in range(0, chans, GS):
            y, q = divmod(at, own_rows)
            rows = slice(at, at + GS)
            if mode == "first":
                taps_w = taps_ref[rows, : 9 * GS]
            elif mode == "wide":
                taps_w = pack_ref[rows, width : width + 9 * GS]
            else:
                taps_w = weights[1][0, b, rows, :]
            mine_at = (chan_at if mode == "own" else 2 * y + core) * own_rows + q
            xhat = xhat_ref[at_b, rows, :]
            rw = ga_ref[rows, :] * rate_ref[at_b, rows, :]
            gh = rw - total(rw) * scale - xhat * (total(rw * xhat) * scale)
            gh = gh.astype(BF16)
            gh_ref[rows, :] = gh
            spread = lax.dot_general(taps_w, gh, TN, preferred_element_type=F32)
            branch = None
            for step_col in (-1, 0, 1):
                part = None
                for step_row in (-1, 0, 1):
                    tap = 3 * (step_row + 1) + step_col + 1
                    term = shifted(spread[tap * GS : (tap + 1) * GS, :], -step_row, 0, row, col)
                    part = term if part is None else part + term
                part = shifted(part, 0, -step_col, row, col)
                branch = part if branch is None else branch + part
            mine = src[pl.ds(pl.multiple_of(mine_at, GS), GS), :].astype(F32)
            out_ref[rows, :] = (mine + branch.astype(BF16).astype(F32)).astype(BF16)

    shapes = [
        shape_of((chans, positions), BF16),
        shape_of((chans, positions), BF16),
        shape_of((chans, positions), F32),
    ]
    scratch = []
    if mode == "first":
        shapes += [shape_of((1, chans, positions), F32)] * 2
        scratch += [
            pltpu.VMEM((chans, width), BF16),
            pltpu.VMEM((chans, TAIL), BF16),
            pltpu.VMEM((chans, positions), BF16),
            pltpu.SemaphoreType.DMA((3,)),
        ]
    scratch.append(pltpu.VMEM((16, 128) if ordered else (whole, positions), BF16))
    operands = [flags, g, *params, *(() if mode == "first" else state)]
    in_specs = [SMEM] + [VMEM] * (len(operands) - 1)
    if mode == "first":
        in_specs[2] = ANY
    result = pl.pallas_call(
        kernel,
        out_shape=shapes,
        in_specs=in_specs,
        out_specs=[VMEM] * len(shapes),
        scratch_shapes=scratch,
        compiler_params=vmem({"own": 6, "wide": 14, "first": 56}[mode]),
        name=mode + "_block",
    )(*operands)
    return result[:3], tuple(result[3:]) if mode == "first" else state


def weight_blocks(b, act_ref, xhat_ref, slope_ref, x_ref, saved_refs, stack, store):
    g, gh_ref, ga_ref = saved_refs
    chans, positions = x_ref.shape[2:]
    width = g.shape[0]
    row, col = grid_of((GS, positions))
    lane = lax.broadcasted_iota(jnp.int32, (GS, TAIL), 1)
    stack[9 * GS :, :] = jnp.zeros((TAIL - 9 * GS, positions), BF16)
    store(
        slice(0, chans),
        0,
        lax.dot_general(act_ref[b], g, NT, preferred_element_type=F32).astype(BF16),
    )
    for q in range(0, chans, GS):
        rows = slice(q, q + GS)
        x = x_ref[0, 0, rows, :].astype(F32)
        for step_row in (-1, 0, 1):
            for step_col in (-1, 0, 1):
                tap = 3 * (step_row + 1) + step_col + 1
                stack[tap * GS : (tap + 1) * GS, :] = shifted(
                    x, step_row, step_col, row, col
                ).astype(BF16)
        taps = lax.dot_general(gh_ref[rows, :], stack[...], NT, preferred_element_type=F32)
        gn = ga_ref[rows, :] * slope_ref[b, rows, :]
        by_gain = jnp.sum(gn * xhat_ref[b, rows, :], axis=1, keepdims=True)
        by_bias = jnp.sum(gn, axis=1, keepdims=True)
        taps = jnp.where(lane == 9 * GS, by_gain, taps)
        taps = jnp.where(lane == 9 * GS + 1, by_bias, taps)
        store(rows, width, taps.astype(BF16))


def storer(out_ref, first_row):
    step = out_ref.shape[2]

    def store(rows, at, value):
        to = slice(first_row + rows.start, first_row + rows.stop)
        for i in range(value.shape[1] // step):
            out_ref[at // step + i, to, :] = value[:, i * step : (i + 1) * step]

    return store


def summed(in_ref, rows):
    acc = in_ref[0, rows, :].astype(F32)
    for m in range(1, in_ref.shape[0]):
        acc = acc + in_ref[m, rows, :].astype(F32)
    return acc.astype(BF16)


def weight_grads(flags, orders, kept, latents, act, xhat, slope, inputs):
    ticks = len(latents)
    chans, positions = act.shape[1:]
    width = kept[0][0][0].shape[0]
    shards = width // chans
    slab = positions // shards
    members = lax.axis_size("dp")
    step = (width + TAIL) // members
    pairs = shards // 2

    def split(g, in_order):
        return g.reshape((pairs, 2, chans, positions) if in_order else (2, pairs, chans, positions))

    operands = []
    for b in range(2):
        for t in range(ticks):
            g, gh, ga = kept[b][t]
            operands += [split(g, orders[b][t]), gh, ga]
    operands += [split(g, in_order) for in_order, g in latents]

    def kernel(*refs):
        refs = list(refs)
        take = lambda k: [refs.pop(0) for _ in range(k)]
        (flags_ref,) = take(1)
        fetched = take(len(operands))
        act_ref, xhat_ref, slope_ref, *x_refs = take(5)
        out_ref, lat_ref, stack, g_bufs, gh_bufs, ga_bufs, sems = refs
        segment_at, chan_at = flags_ref[0], flags_ref[1]

        def copies(t):
            made = []

            def put(src, to):
                made.append(pltpu.make_async_copy(src, to, sems.at[len(made)]))

            for b in range(2):
                g, gh, ga = fetched[3 * (ticks * b + t) :][:3]
                for c in range(2):
                    put(g.at[:, c] if orders[b][t] else g.at[c], g_bufs.at[b, :, c])
                at = 0
                if gh.shape[0] > chans:
                    at = pl.multiple_of((chan_at >> 1) * chans, chans)
                put(gh.at[pl.ds(at, chans)], gh_bufs.at[b])
                put(ga.at[pl.ds(at, chans)], ga_bufs.at[b])
            g = fetched[6 * ticks + t]
            for c in range(2):
                put(g.at[:, c] if latents[t][0] else g.at[c], g_bufs.at[2, :, c])
            return made

        for t in range(ticks):

            @pl.when(segment_at == ticks - 1 - t)
            def _():
                for copy in copies(t):
                    copy.start()
                for copy in copies(t):
                    copy.wait()

        whole = lambda i: g_bufs[i].reshape(width, positions)
        for b in range(2):
            weight_blocks(
                b, act_ref, xhat_ref, slope_ref, x_refs[b],
                (whole(b), gh_bufs.at[b], ga_bufs.at[b]), stack, storer(out_ref, b * chans),
            )
        lat_ref[...] = own_positions(whole(2), chan_at, slab)

    return pl.pallas_call(
        kernel,
        out_shape=(
            shape_of((members, 2 * chans, step), BF16),
            shape_of((slab, width), BF16),
        ),
        in_specs=[SMEM] + [ANY] * len(operands) + [VMEM] * 5,
        out_specs=[VMEM] * 2,
        scratch_shapes=[
            pltpu.VMEM((TAIL, positions), BF16),
            pltpu.VMEM((3, pairs, 2, chans, positions), BF16),
            pltpu.VMEM((2, chans, positions), BF16),
            pltpu.VMEM((2, chans, positions), F32),
            pltpu.SemaphoreType.DMA((10,)),
        ],
        compiler_params=vmem(56),
        name="weight_grads",
    )(flags, *operands, act, xhat, slope, *inputs)


def sum_kernel(in_ref, out_ref):
    done = summed(in_ref, slice(0, out_ref.shape[1]))
    for m in range(out_ref.shape[0]):
        out_ref[m] = done


def spread_sums(parts):
    return pl.pallas_call(
        sum_kernel,
        out_shape=shape_of(parts.shape, BF16),
        in_specs=[VMEM],
        out_specs=VMEM,
        compiler_params=vmem(6),
        name="sum_microbatches",
    )(parts)


def widen_kernel(in_ref, proj_ref, conv_ref, gain_ref, bias_ref):
    chans, width = proj_ref.shape[2:]
    step = in_ref.shape[2]
    down = lax.broadcasted_iota(jnp.int32, (chans, chans), 0)
    across = lax.broadcasted_iota(jnp.int32, (chans, chans), 1)
    first = width // step
    for b in range(2):
        rows = slice(b * chans, (b + 1) * chans)
        for i in range(first):
            proj_ref[0, b, :, i * step : (i + 1) * step] = in_ref[i, rows, :].astype(F32)
        conv_ref[0, b, :, :step] = in_ref[first, rows, :].astype(F32)
        side = in_ref[first + 1, rows, :].astype(F32)
        conv_ref[0, b, :, step:] = side[:, : 9 * GS - step]
        for i, to in enumerate((gain_ref, bias_ref)):
            at = 9 * GS - step + i
            lined = jnp.where(down == across, side[:, at : at + 1], 0.0)
            to[0, b : b + 1, :] = jnp.sum(lined, axis=0, keepdims=True)


def widen(sums, width):
    chans = sums.shape[1] // 2
    return pl.pallas_call(
        widen_kernel,
        out_shape=(
            shape_of((1, 2, chans, width), F32),
            shape_of((1, 2, chans, 9 * GS), F32),
            shape_of((1, 2, chans), F32),
            shape_of((1, 2, chans), F32),
        ),
        in_specs=[VMEM],
        out_specs=[VMEM] * 4,
        compiler_params=vmem(8),
        name="widen",
    )(sums)


def gather(block_, axis, groups=None):
    return lax.all_gather(block_, axis, axis=0, tiled=True, axis_index_groups=groups)


def per_device(
    grad_top,
    inputs_one,
    conv_one,
    inputs_two,
    conv_two,
    proj_weight,
    conv_weight,
    norm_gain,
    norm_bias,
):
    segments = lax.axis_size("segment")
    segment_at = lax.axis_index("segment")
    chan_at = lax.axis_index("chan")
    members = lax.axis_size("dp")
    shards = lax.axis_size("chan")
    chans, positions = conv_one.shape[2:]
    width = proj_weight.shape[3]
    cores = [[2 * y, 2 * y + 1] for y in range(shards // 2)]
    columns = [[2 * y + c for y in range(shards // 2)] for c in range(2)]

    def exchange(blocks):
        return lax.all_to_all(blocks, "dp", split_axis=0, concat_axis=0, tiled=True)

    first_pack, second_pack, xhat, slope, rate, act = prepare(
        proj_weight, conv_weight, conv_one, conv_two, norm_gain, norm_bias
    )
    packs = [None, gather(second_pack, "chan", columns)]
    packs[0] = lax.all_gather(
        first_pack[None], "chan", axis=1, tiled=True, axis_index_groups=columns
    )[0]
    own = (proj_weight, conv_weight)
    states = [None, None]
    kept = [[], []]
    orders = [[], []]
    latents = []
    flags = jnp.stack([segment_at.astype(jnp.int32), chan_at.astype(jnp.int32)])
    for tick in range(segments):
        if tick == 0:
            g = lax.all_gather(grad_top[0], "chan", axis=1, tiled=True)
            ordered = True
        else:
            lower = segments - 1 - tick
            rest = [s for s in range(segments) if s not in (lower, lower + 1)]
            groups = sorted(
                [[lower, lower + 1]] + [rest[i : i + 2] for i in range(0, len(rest), 2)]
            )
            ordered = out.shape[0] == chans
            moved = gather(out, "segment", groups)[out.shape[0] :]
            g = gather(moved, "chan", None if ordered else cores)
            latents.append((ordered, g))
        for b in (1, 0):
            if tick > 1 or (tick == 1 and b == 1):
                mode = "wide" if states[b] is not None else "first"
            else:
                mode = "own"
            if mode == "first":
                packs[b], g = lax.optimization_barrier((packs[b], g))
            (out, gh, ga), state = block(
                b,
                mode,
                flags,
                g,
                ordered,
                chans,
                own if mode == "own" else (packs[b],),
                (xhat, rate) if mode == "own" else states[b],
            )
            if mode != "own":
                states[b] = state
            kept[b].append((g, gh, ga))
            orders[b].append(ordered)
            if b == 1 or tick == segments - 1:
                ordered = out.shape[0] == chans
                g = gather(out, "chan", None if ordered else cores)
    latents.append((ordered, g))

    parts, latent = weight_grads(
        flags, orders, kept, latents, act, xhat, slope, (inputs_one, inputs_two)
    )
    sums = exchange(spread_sums(exchange(parts)))
    proj, conv, by_gain, by_bias = widen(sums, width)
    return latent.T[None, None], proj, conv, by_gain, by_bias


def solution(mesh):
    return jax.shard_map(
        per_device,
        mesh=mesh,
        in_specs=(
            P("dp", None, "chan"),
            P("segment", "dp", "chan", None),
            P("segment", "dp", "chan", None),
            P("segment", "dp", "chan", None),
            P("segment", "dp", "chan", None),
            P("segment", None, "chan", None),
            P("segment", None, "chan", None),
            P("segment", None, "chan"),
            P("segment", None, "chan"),
        ),
        out_specs=(
            P("segment", "dp", None, "chan"),
            P("segment", None, "chan", None),
            P("segment", None, "chan", None),
            P("segment", None, "chan"),
            P("segment", None, "chan"),
        ),
        check_vma=False,
    )
```

```python
import functools

import jax
import jax.numpy as jnp
from jax import lax
from jax.experimental import pallas as pl
from jax.experimental.pallas import tpu as pltpu
from jax.sharding import PartitionSpec as P

GS = 48
WW = 64
NORM_EPS = 1e-05
TAIL = 512
F32 = jnp.float32
BF16 = jnp.bfloat16
VMEM = pl.BlockSpec(memory_space=pltpu.VMEM)
SMEM = pl.BlockSpec(memory_space=pltpu.SMEM)
ANY = pl.BlockSpec(memory_space=pl.ANY)
NT = (((1,), (1,)), ((), ()))
TN = (((0,), (0,)), ((), ()))


def vmem(mebibytes):
    return pltpu.CompilerParams(vmem_limit_bytes=mebibytes * 1024 * 1024)


def shape_of(shape, dtype):
    return jax.ShapeDtypeStruct(shape, dtype)


def total(block):
    return jnp.sum(jnp.sum(block, axis=1, keepdims=True), axis=0, keepdims=True)


def norm_group(h, gain, bias):
    scale = 1.0 / (h.shape[0] * h.shape[1])
    pre = h.astype(F32)
    pre = pre - total(pre) * scale
    inv_std = lax.rsqrt(total(pre * pre) * scale + NORM_EPS)
    xhat = pre * inv_std
    n = xhat * gain + bias
    sig = jax.nn.sigmoid(n)
    slope = sig * (1.0 + n * (1.0 - sig))
    return xhat, n, sig, slope, inv_std


def column(line):
    count = line.shape[1]
    down = lax.broadcasted_iota(jnp.int32, (count, count), 0)
    across = lax.broadcasted_iota(jnp.int32, (count, count), 1)
    return jnp.sum(jnp.where(down == across, line, 0.0), axis=1, keepdims=True)


def columns_of(gain_ref, bias_ref, b):
    return column(gain_ref[0, b : b + 1, :]), column(bias_ref[0, b : b + 1, :])


def prepare_kernel(*refs):
    pack_refs = (refs[6], refs[7])
    w_ref, wc_ref, h1_ref, h2_ref, gain_ref, bias_ref, sems = refs[8:]
    copies = [
        pltpu.make_async_copy(refs[i], refs[8 + i], sems.at[i]) for i in range(6)
    ]
    for copy in copies:
        copy.start()
    for copy in copies:
        copy.wait()
    chans, width = w_ref.shape[2:]
    taps = wc_ref.shape[3]
    lane = lax.broadcasted_iota(jnp.int32, (chans, TAIL - 384), 1)
    for b, h_ref in ((1, h2_ref), (0, h1_ref)):
        pack_ref = pack_refs[b]
        pack_ref[:, :width] = w_ref[0, b]
        pack_ref[:, width : width + 384] = wc_ref[0, b, :, :384]
        last = wc_ref[0, b, :, 384:].astype(F32)
        last = jnp.concatenate(
            [last, jnp.zeros((chans, TAIL - taps), F32)], axis=1
        )
        at = taps - 384
        for whole in columns_of(gain_ref, bias_ref, b):
            rest = whole
            for _ in range(3):
                piece = rest.astype(BF16).astype(F32)
                rest = rest - piece
                last = jnp.where(lane == at, piece, last)
                at += 1
        pack_ref[:, width + 384 : width + TAIL] = last.astype(BF16)
        pack_ref[:, width + TAIL :] = h_ref[0, 0]


def prepare(*operands):
    chans, width = operands[0].shape[2:]
    positions = operands[2].shape[3]
    pack = shape_of((chans, width + TAIL + positions), BF16)
    return pl.pallas_call(
        prepare_kernel,
        out_shape=(pack, pack),
        in_specs=[ANY] * 6,
        out_specs=[VMEM] * 2,
        scratch_shapes=[pltpu.VMEM(x.shape, x.dtype) for x in operands]
        + [pltpu.SemaphoreType.DMA((6,))],
        compiler_params=vmem(56),
        name="prepare",
    )(*operands)


def shifted(value, step_row, step_col, row, col):
    length = value.shape[1]
    rows = length // WW
    by = step_row * WW + step_col
    if by == 0:
        return value
    moved = pltpu.roll(value, (-by) % length, axis=1)
    inside = None
    if step_row:
        inside = row < rows - 1 if step_row > 0 else row > 0
    if step_col:
        here = col < WW - 1 if step_col > 0 else col > 0
        inside = here if inside is None else inside & here
    return jnp.where(inside, moved, 0.0)


def grid_of(shape):
    lane = lax.broadcasted_iota(jnp.int32, shape, 1)
    return lane // WW, lane % WW


def own_positions(g, chan_at, count):
    down = lax.broadcasted_iota(jnp.int32, (count, g.shape[1]), 0)
    across = lax.broadcasted_iota(jnp.int32, (count, g.shape[1]), 1)
    pick = jnp.where(across == down + chan_at * count, 1.0, 0.0).astype(BF16)
    return lax.dot_general(pick, g, NT, preferred_element_type=F32).astype(BF16)


def gh_of(ga, xhat, rate):
    scale = 1.0 / (ga.shape[0] * ga.shape[1])
    rw = ga * rate
    gh = rw - total(rw) * scale - xhat * (total(rw * xhat) * scale)
    return gh.astype(BF16)


def conv_back(taps_w, gh, row, col):
    spread = lax.dot_general(taps_w, gh, TN, preferred_element_type=F32)
    branch = None
    for step_col in (-1, 0, 1):
        part = None
        for step_row in (-1, 0, 1):
            tap = 3 * (step_row + 1) + step_col + 1
            term = shifted(spread[tap * GS : (tap + 1) * GS, :], -step_row, 0, row, col)
            part = term if part is None else part + term
        part = shifted(part, 0, -step_col, row, col)
        branch = part if branch is None else branch + part
    return branch.astype(BF16)


def in_order(g_buf, g_ref, own_rows):
    per = g_ref.shape[0] // 2 // own_rows
    for c in range(2):
        for y in range(per):
            to = (2 * y + c) * own_rows
            at = (c * per + y) * own_rows
            g_buf[to : to + own_rows, :] = g_ref[at : at + own_rows, :]


def add_branch(out_ref, rows, src, mine_at, branch):
    mine = src[pl.ds(pl.multiple_of(mine_at, GS), GS), :].astype(F32)
    out_ref[rows, :] = (mine + branch.astype(F32)).astype(BF16)


def own_block(b, alone, flags, g, ordered, params):
    whole, positions = g.shape
    proj_weight, conv_weight, h, gain, bias = params
    chans = proj_weight.shape[2]

    def kernel(flags_ref, g_ref, w_ref, wc_ref, h_ref, gain_ref, bias_ref, out_ref, g_buf):
        src = g_ref
        if not ordered:
            in_order(g_buf, g_ref, chans)
            src = g_buf
        ga = jnp.dot(w_ref[0, 0], src[...], preferred_element_type=F32)
        row, col = grid_of((GS, positions))
        gains, biases = columns_of(gain_ref, bias_ref, b)
        for at in range(0, chans, GS):
            rows = slice(at, at + GS)
            xhat, _, _, slope, inv_std = norm_group(h_ref[0, 0, rows, :], gains[rows], biases[rows])
            gh = gh_of(ga[rows, :], xhat, slope * (gains[rows] * inv_std))
            branch = conv_back(wc_ref[0, 0, rows, :], gh, row, col)
            add_branch(out_ref, rows, src, flags_ref[1] * chans + at, branch)

    def at_block(shape):
        return pl.BlockSpec((1, 1) + shape[2:], lambda i: (0, b, 0, 0))

    return pl.pallas_call(
        kernel,
        out_shape=shape_of((chans, positions), BF16),
        grid=(1,),
        in_specs=[SMEM, VMEM, at_block(proj_weight.shape), at_block(conv_weight.shape)]
        + [VMEM] * 3,
        out_specs=VMEM,
        scratch_shapes=[pltpu.VMEM((16, 128) if ordered else (whole, positions), BF16)],
        compiler_params=vmem(56 if alone else 8),
        name="own_block",
    )(flags, g, *params)


def first_block(flags, g, ordered, own_rows, pack):
    whole, positions = g.shape
    chans = pack.shape[0]
    width = whole
    per = whole // 2 // own_rows
    shape = (per, 2, own_rows, positions)
    g = g.reshape(shape if ordered else (2, per, own_rows, positions))

    def kernel(
        flags_ref, g_ref, pack_ref, out_ref, xhat_out, rate_out,
        w_ref, taps_ref, h_ref, g_buf, src, xhat_ref, rate_ref, sems,
    ):
        def copy(i, a, to):
            return pltpu.make_async_copy(a, to, sems.at[i])

        loads = [
            copy(0, pack_ref.at[:, width + TAIL : width + TAIL + positions], h_ref),
            copy(1, pack_ref.at[:, width : width + TAIL], taps_ref),
            copy(2, pack_ref.at[:, :width], w_ref),
        ] + [
            copy(3 + c, g_ref.at[:, c] if ordered else g_ref.at[c], g_buf.at[:, c])
            for c in range(2)
        ]
        for load in loads:
            load.start()
        loads[0].wait()
        loads[1].wait()
        at = 9 * GS - 384
        for q in range(0, chans, GS):
            rows = slice(q, q + GS)
            side = taps_ref[rows, 384:].astype(F32)
            gain, bias = (
                side[:, i : i + 1] + side[:, i + 1 : i + 2] + side[:, i + 2 : i + 3]
                for i in (at, at + 3)
            )
            xhat, _, _, slope, inv_std = norm_group(h_ref[rows, :], gain, bias)
            xhat_ref[rows, :] = xhat
            rate_ref[rows, :] = slope * (gain * inv_std)
        stores = [copy(5, xhat_ref, xhat_out), copy(6, rate_ref, rate_out)]
        for store in stores:
            store.start()
        for load in loads[2:]:
            load.wait()
        src[...] = g_buf[...].reshape(whole, positions)
        wide_body(
            flags_ref, src, w_ref[...], lambda rows: taps_ref[rows, : 9 * GS],
            xhat_ref, rate_ref, out_ref, own_rows,
        )
        for store in stores:
            store.wait()

    full = shape_of((chans, positions), F32)
    return pl.pallas_call(
        kernel,
        out_shape=(shape_of((chans, positions), BF16), full, full),
        in_specs=[SMEM, ANY, ANY],
        out_specs=[VMEM, ANY, ANY],
        scratch_shapes=[
            pltpu.VMEM((chans, width), BF16),
            pltpu.VMEM((chans, TAIL), BF16),
            pltpu.VMEM((chans, positions), BF16),
            pltpu.VMEM(shape, BF16),
            pltpu.VMEM((whole, positions), BF16),
            pltpu.VMEM((chans, positions), F32),
            pltpu.VMEM((chans, positions), F32),
            pltpu.SemaphoreType.DMA((7,)),
        ],
        compiler_params=vmem(56),
        name="first_block",
    )(flags, g, pack)


def wide_body(flags_ref, src, matrix, taps_of, xhat_ref, rate_ref, out_ref, own_rows):
    chans, positions = xhat_ref.shape
    ga = jnp.dot(matrix, src[...], preferred_element_type=F32)
    core = flags_ref[1] & 1
    row, col = grid_of((GS, positions))
    for at in range(0, chans, GS):
        y, q = divmod(at, own_rows)
        rows = slice(at, at + GS)
        gh = gh_of(ga[rows, :], xhat_ref[rows, :], rate_ref[rows, :])
        branch = conv_back(taps_of(rows), gh, row, col)
        add_branch(out_ref, rows, src, (2 * y + core) * own_rows + q, branch)


def wide_block(flags, g, ordered, own_rows, pack, state):
    whole, positions = g.shape
    chans = pack.shape[0]

    def kernel(flags_ref, g_ref, pack_ref, xhat_ref, rate_ref, out_ref, g_buf):
        src = g_ref
        if not ordered:
            in_order(g_buf, g_ref, own_rows)
            src = g_buf
        wide_body(
            flags_ref, src, pack_ref[:, :whole],
            lambda rows: pack_ref[rows, whole : whole + 9 * GS],
            xhat_ref, rate_ref, out_ref, own_rows,
        )

    return pl.pallas_call(
        kernel,
        out_shape=shape_of((chans, positions), BF16),
        in_specs=[SMEM] + [VMEM] * 4,
        out_specs=VMEM,
        scratch_shapes=[pltpu.VMEM((16, 128) if ordered else (whole, positions), BF16)],
        compiler_params=vmem(14),
        name="wide_block",
    )(flags, g, pack, *state)


def storer(out_ref):
    step = out_ref.shape[2]

    def store(first_row, at, value):
        for i in range(value.shape[1] // step):
            out_ref[at // step + i, first_row : first_row + value.shape[0], :] = value[
                :, i * step : (i + 1) * step
            ]

    return store


def summed(in_ref, rows):
    acc = in_ref[0, rows, :].astype(F32)
    for m in range(1, in_ref.shape[0]):
        acc = acc + in_ref[m, rows, :].astype(F32)
    return acc.astype(BF16)


def weight_grads(flags, orders, kept, latents, params, inputs):
    proj_weight, conv_weight, h_one, h_two, gain, bias = params
    ticks = len(latents)
    chans, width = proj_weight.shape[2:]
    positions = h_one.shape[3]
    shards = width // chans
    slab = positions // shards
    members = lax.axis_size("dp")
    step = (width + TAIL) // members
    pairs = shards // 2

    def split(g, ordered):
        return g.reshape((pairs, 2, chans, positions) if ordered else (2, pairs, chans, positions))

    operands = [split(g, o) for b in range(2) for g, o in zip(kept[b], orders[b])]
    operands += [split(g, o) for o, g in latents]
    order_of = [*orders[0], *orders[1], *(o for o, _ in latents)]

    def kernel(*refs):
        flags_ref = refs[0]
        fetched = refs[1 : 1 + len(operands)]
        w_ref, h1_ref, h2_ref, gain_ref, bias_ref, *x_refs = refs[1 + len(operands) : -6]
        out_ref, lat_ref, stacks, g_bufs, g_flat, sems = refs[-6:]
        segment_at, chan_at = flags_ref[0], flags_ref[1]

        def copies(t):
            made = []
            for i in range(3):
                g = fetched[ticks * i + t]
                for c in range(2):
                    made.append(
                        pltpu.make_async_copy(
                            g.at[:, c] if order_of[ticks * i + t] else g.at[c],
                            g_bufs.at[i, :, c],
                            sems.at[len(made)],
                        )
                    )
            return made

        def each(act):
            for t in range(ticks):

                @pl.when(segment_at == ticks - 1 - t)
                def _():
                    for made in copies(t):
                        act(made)

        each(lambda made: made.start())
        row, col = grid_of((GS, positions))
        lane = lax.broadcasted_iota(jnp.int32, (GS, TAIL), 1)
        for b in range(2):
            for q in range(0, chans, GS):
                x = x_refs[b][0, 0, q : q + GS, :].astype(F32)
                for step_row in (-1, 0, 1):
                    for step_col in (-1, 0, 1):
                        tap = 3 * (step_row + 1) + step_col + 1
                        stacks[b, q // GS, tap * GS : (tap + 1) * GS, :] = shifted(
                            x, step_row, step_col, row, col
                        ).astype(BF16)
                stacks[b, q // GS, 9 * GS :, :] = jnp.zeros((TAIL - 9 * GS, positions), BF16)
        each(lambda made: made.wait())
        store = storer(out_ref)
        for b, h_ref in enumerate((h1_ref, h2_ref)):
            g_flat[...] = g_bufs[b].reshape(width, positions)
            ga = jnp.dot(w_ref[0, b], g_flat[...], preferred_element_type=F32)
            gains, biases = columns_of(gain_ref, bias_ref, b)
            acts = []
            for q in range(0, chans, GS):
                rows = slice(q, q + GS)
                xhat, n, sig, slope, inv_std = norm_group(
                    h_ref[0, 0, rows, :], gains[rows], biases[rows]
                )
                acts.append((n * sig).astype(BF16))
                gh = gh_of(ga[rows, :], xhat, slope * (gains[rows] * inv_std))
                taps = lax.dot_general(
                    gh, stacks[b, q // GS], NT, preferred_element_type=F32
                )
                gn = ga[rows, :] * slope
                by_gain = jnp.sum(gn * xhat, axis=1, keepdims=True)
                by_bias = jnp.sum(gn, axis=1, keepdims=True)
                taps = jnp.where(lane == 9 * GS, by_gain, taps)
                taps = jnp.where(lane == 9 * GS + 1, by_bias, taps)
                store(b * chans + q, width, taps.astype(BF16))
            act = jnp.concatenate(acts, axis=0)
            proj = lax.dot_general(act, g_flat[...], NT, preferred_element_type=F32)
            store(b * chans, 0, proj.astype(BF16))
        lat_ref[...] = own_positions(g_bufs[2].reshape(width, positions), chan_at, slab)

    return pl.pallas_call(
        kernel,
        out_shape=(
            shape_of((members, 2 * chans, step), BF16),
            shape_of((slab, width), BF16),
        ),
        in_specs=[SMEM] + [ANY] * len(operands) + [VMEM] * 7,
        out_specs=[VMEM] * 2,
        scratch_shapes=[
            pltpu.VMEM((2, chans // GS, TAIL, positions), BF16),
            pltpu.VMEM((3, pairs, 2, chans, positions), BF16),
            pltpu.VMEM((width, positions), BF16),
            pltpu.SemaphoreType.DMA((6,)),
        ],
        compiler_params=vmem(56),
        name="weight_grads",
    )(flags, *operands, proj_weight, h_one, h_two, gain, bias, *inputs)


def sum_kernel(in_ref, out_ref):
    done = summed(in_ref, slice(0, out_ref.shape[1]))
    for m in range(out_ref.shape[0]):
        out_ref[m] = done


def spread_sums(parts):
    return pl.pallas_call(
        sum_kernel,
        out_shape=shape_of(parts.shape, BF16),
        in_specs=[VMEM],
        out_specs=VMEM,
        compiler_params=vmem(6),
        name="sum_microbatches",
    )(parts)


def widen_kernel(in_ref, proj_ref, conv_ref, gain_ref, bias_ref):
    chans, width = proj_ref.shape[2:]
    step = in_ref.shape[2]
    down = lax.broadcasted_iota(jnp.int32, (chans, chans), 0)
    across = lax.broadcasted_iota(jnp.int32, (chans, chans), 1)
    first = width // step
    for b in range(2):
        rows = slice(b * chans, (b + 1) * chans)
        for i in range(first):
            proj_ref[0, b, :, i * step : (i + 1) * step] = in_ref[i, rows, :].astype(F32)
        conv_ref[0, b, :, :step] = in_ref[first, rows, :].astype(F32)
        side = in_ref[first + 1, rows, :].astype(F32)
        conv_ref[0, b, :, step:] = side[:, : 9 * GS - step]
        for i, to in enumerate((gain_ref, bias_ref)):
            at = 9 * GS - step + i
            lined = jnp.where(down == across, side[:, at : at + 1], 0.0)
            to[0, b : b + 1, :] = jnp.sum(lined, axis=0, keepdims=True)


def widen(sums, width):
    chans = sums.shape[1] // 2
    return pl.pallas_call(
        widen_kernel,
        out_shape=(
            shape_of((1, 2, chans, width), F32),
            shape_of((1, 2, chans, 9 * GS), F32),
            shape_of((1, 2, chans), F32),
            shape_of((1, 2, chans), F32),
        ),
        in_specs=[VMEM],
        out_specs=[VMEM] * 4,
        compiler_params=vmem(8),
        name="widen",
    )(sums)


def gather(block_, axis, groups=None):
    return lax.all_gather(block_, axis, axis=0, tiled=True, axis_index_groups=groups)


def per_device(
    grad_top,
    inputs_one,
    conv_one,
    inputs_two,
    conv_two,
    proj_weight,
    conv_weight,
    norm_gain,
    norm_bias,
):
    segments = lax.axis_size("segment")
    segment_at = lax.axis_index("segment")
    chan_at = lax.axis_index("chan")
    members = lax.axis_size("dp")
    shards = lax.axis_size("chan")
    chans, positions = conv_one.shape[2:]
    width = proj_weight.shape[3]
    cores = [[2 * y, 2 * y + 1] for y in range(shards // 2)]
    columns = [[2 * y + c for y in range(shards // 2)] for c in range(2)]

    def exchange(blocks):
        return lax.all_to_all(blocks, "dp", split_axis=0, concat_axis=0, tiled=True)

    params = (proj_weight, conv_weight, conv_one, conv_two, norm_gain, norm_bias)
    first_pack, second_pack = prepare(*params)
    packs = [None, gather(second_pack, "chan", columns)]
    packs[0] = lax.all_gather(
        first_pack[None], "chan", axis=1, tiled=True, axis_index_groups=columns
    )[0]
    states = [None, None]
    kept = [[], []]
    orders = [[], []]
    latents = []
    flags = jnp.stack([segment_at.astype(jnp.int32), chan_at.astype(jnp.int32)])
    for tick in range(segments):
        if tick == 0:
            g = lax.all_gather(grad_top[0], "chan", axis=1, tiled=True)
            ordered = True
        else:
            lower = segments - 1 - tick
            rest = [s for s in range(segments) if s not in (lower, lower + 1)]
            groups = sorted(
                [[lower, lower + 1]] + [rest[i : i + 2] for i in range(0, len(rest), 2)]
            )
            ordered = out.shape[0] == chans
            moved = gather(out, "segment", groups)[out.shape[0] :]
            g = gather(moved, "chan", None if ordered else cores)
            latents.append((ordered, g))
        for b in (1, 0):
            kept[b].append(g)
            if tick == 0 or (tick == 1 and b == 0):
                h = conv_two if b == 1 else conv_one
                out = own_block(
                    b, tick == 1, flags, g, ordered,
                    (proj_weight, conv_weight, h, norm_gain, norm_bias),
                )
            elif states[b] is None:
                packs[b], g = lax.optimization_barrier((packs[b], g))
                out, *states[b] = first_block(flags, g, ordered, chans, packs[b])
            else:
                out = wide_block(flags, g, ordered, chans, packs[b], states[b])
            orders[b].append(ordered)
            if b == 1 or tick == segments - 1:
                ordered = out.shape[0] == chans
                g = gather(out, "chan", None if ordered else cores)
    latents.append((ordered, g))

    parts, latent = weight_grads(
        flags, orders, kept, latents, params, (inputs_one, inputs_two)
    )
    sums = exchange(spread_sums(exchange(parts)))
    proj, conv, by_gain, by_bias = widen(sums, width)
    return latent.T[None, None], proj, conv, by_gain, by_bias


def solution(mesh):
    return jax.shard_map(
        per_device,
        mesh=mesh,
        in_specs=(
            P("dp", None, "chan"),
            P("segment", "dp", "chan", None),
            P("segment", "dp", "chan", None),
            P("segment", "dp", "chan", None),
            P("segment", "dp", "chan", None),
            P("segment", None, "chan", None),
            P("segment", None, "chan", None),
            P("segment", None, "chan"),
            P("segment", None, "chan"),
        ),
        out_specs=(
            P("segment", "dp", None, "chan"),
            P("segment", None, "chan", None),
            P("segment", None, "chan", None),
            P("segment", None, "chan"),
            P("segment", None, "chan"),
        ),
        check_vma=False,
    )
```

```python
import functools

import jax
import jax.numpy as jnp
from jax import lax
from jax.experimental import pallas as pl
from jax.experimental.pallas import tpu as pltpu
from jax.sharding import PartitionSpec as P

GS = 48
WW = 64
NORM_EPS = 1e-05
TAIL = 512
F32 = jnp.float32
BF16 = jnp.bfloat16
VMEM = pl.BlockSpec(memory_space=pltpu.VMEM)
SMEM = pl.BlockSpec(memory_space=pltpu.SMEM)
ANY = pl.BlockSpec(memory_space=pl.ANY)
NT = (((1,), (1,)), ((), ()))
TN = (((0,), (0,)), ((), ()))


def vmem(mebibytes):
    return pltpu.CompilerParams(vmem_limit_bytes=mebibytes * 1024 * 1024)


def shape_of(shape, dtype):
    return jax.ShapeDtypeStruct(shape, dtype)


def total(block):
    return jnp.sum(jnp.sum(block, axis=1, keepdims=True), axis=0, keepdims=True)


def norm_stats(blocks):
    scale = 1.0 / (blocks[0].shape[0] * blocks[0].shape[1])
    means = [total(h.astype(F32)) * scale for h in blocks]
    spreads = []
    for h, mean in zip(blocks, means):
        pre = h.astype(F32) - mean
        spreads.append(lax.rsqrt(total(pre * pre) * scale + NORM_EPS))
    return list(zip(means, spreads))


def norm_group(h, gain, bias, stats=None):
    mean, inv_std = norm_stats([h])[0] if stats is None else stats
    pre = h.astype(F32) - mean
    xhat = pre * inv_std
    n = xhat * gain + bias
    sig = jax.nn.sigmoid(n)
    slope = sig * (1.0 + n * (1.0 - sig))
    return xhat, n, sig, slope, inv_std


def column(line):
    count = line.shape[1]
    down = lax.broadcasted_iota(jnp.int32, (count, count), 0)
    across = lax.broadcasted_iota(jnp.int32, (count, count), 1)
    return jnp.sum(jnp.where(down == across, line, 0.0), axis=1, keepdims=True)


def columns_of(gain_ref, bias_ref, b):
    return column(gain_ref[0, b : b + 1, :]), column(bias_ref[0, b : b + 1, :])


def prepare_kernel(*refs):
    pack_refs = (refs[6], refs[7])
    w_ref, wc_ref, h1_ref, h2_ref, gain_ref, bias_ref, sems = refs[8:]
    copies = [
        pltpu.make_async_copy(refs[i], refs[8 + i], sems.at[i]) for i in range(6)
    ]
    for copy in copies:
        copy.start()
    for copy in copies:
        copy.wait()
    chans, width = w_ref.shape[2:]
    taps = wc_ref.shape[3]
    lane = lax.broadcasted_iota(jnp.int32, (chans, TAIL - 384), 1)
    down = lax.broadcasted_iota(jnp.int32, (GS, GS), 0)
    across = lax.broadcasted_iota(jnp.int32, (GS, GS), 1)
    same = jnp.where(down == across, 1.0, 0.0).astype(BF16)
    for b, h_ref in ((1, h2_ref), (0, h1_ref)):
        pack_ref = pack_refs[b]
        pack_ref[:, :width] = w_ref[0, b]
        turned = []
        for q in range(0, chans, GS):
            taps_w = [
                lax.dot_general(
                    same,
                    wc_ref[0, b, q : q + GS, k * GS : (k + 1) * GS],
                    NT,
                    preferred_element_type=F32,
                )
                for k in range(taps // GS)
            ]
            turned.append(
                jnp.concatenate([*taps_w, jnp.zeros((GS, TAIL - taps), F32)], axis=1)
            )
        turned = jnp.concatenate(turned, axis=0)
        pack_ref[:, width : width + 384] = turned[:, :384].astype(BF16)
        last = turned[:, 384:]
        at = taps - 384
        for whole in columns_of(gain_ref, bias_ref, b):
            rest = whole
            for _ in range(3):
                piece = rest.astype(BF16).astype(F32)
                rest = rest - piece
                last = jnp.where(lane == at, piece, last)
                at += 1
        pack_ref[:, width + 384 : width + TAIL] = last.astype(BF16)
        pack_ref[:, width + TAIL :] = h_ref[0, 0]


def prepare(*operands):
    chans, width = operands[0].shape[2:]
    positions = operands[2].shape[3]
    pack = shape_of((chans, width + TAIL + positions), BF16)
    return pl.pallas_call(
        prepare_kernel,
        out_shape=(pack, pack),
        in_specs=[ANY] * 6,
        out_specs=[VMEM] * 2,
        scratch_shapes=[pltpu.VMEM(x.shape, x.dtype) for x in operands]
        + [pltpu.SemaphoreType.DMA((6,))],
        compiler_params=vmem(56),
        name="prepare",
    )(*operands)


def shifted(value, step_row, step_col, row, col):
    length = value.shape[1]
    rows = length // WW
    by = step_row * WW + step_col
    if by == 0:
        return value
    moved = pltpu.roll(value, (-by) % length, axis=1)
    inside = None
    if step_row:
        inside = row < rows - 1 if step_row > 0 else row > 0
    if step_col:
        here = col < WW - 1 if step_col > 0 else col > 0
        inside = here if inside is None else inside & here
    return jnp.where(inside, moved, 0.0)


def grid_of(shape):
    lane = lax.broadcasted_iota(jnp.int32, shape, 1)
    return lane // WW, lane % WW


def own_positions(g, chan_at, count):
    down = lax.broadcasted_iota(jnp.int32, (count, g.shape[1]), 0)
    across = lax.broadcasted_iota(jnp.int32, (count, g.shape[1]), 1)
    pick = jnp.where(across == down + chan_at * count, 1.0, 0.0).astype(BF16)
    return lax.dot_general(pick, g, NT, preferred_element_type=F32).astype(BF16)


def gh_means(ga, xhat, rate):
    scale = 1.0 / (ga.shape[0] * ga.shape[1])
    rw = ga * rate
    return total(rw) * scale, total(rw * xhat) * scale


def gh_of(ga, xhat, rate, means=None):
    first, second = gh_means(ga, xhat, rate) if means is None else means
    return (ga * rate - first - xhat * second).astype(BF16)


def conv_back(taps_w, gh, row, col):
    spread = lax.dot_general(taps_w, gh, TN, preferred_element_type=F32)
    branch = None
    for step_col in (-1, 0, 1):
        part = None
        for step_row in (-1, 0, 1):
            tap = 3 * (step_row + 1) + step_col + 1
            term = shifted(spread[tap * GS : (tap + 1) * GS, :], -step_row, 0, row, col)
            part = term if part is None else part + term
        part = shifted(part, 0, -step_col, row, col)
        branch = part if branch is None else branch + part
    return branch.astype(BF16)


def conv_back_stacked(taps_w, gh, row, col, stack):
    gh = gh.astype(F32)
    for step_col in (-1, 0, 1):
        moved = shifted(gh, 0, -step_col, row, col)
        for step_row in (-1, 0, 1):
            tap = 3 * (step_row + 1) + step_col + 1
            stack[tap * GS : (tap + 1) * GS, :] = shifted(
                moved, -step_row, 0, row, col
            ).astype(BF16)
    return jnp.dot(taps_w, stack[...], preferred_element_type=F32).astype(BF16)


def in_order(g_buf, g_ref, own_rows):
    per = g_ref.shape[0] // 2 // own_rows
    for c in range(2):
        for y in range(per):
            to = (2 * y + c) * own_rows
            at = (c * per + y) * own_rows
            g_buf[to : to + own_rows, :] = g_ref[at : at + own_rows, :]


def add_branch(out_ref, rows, src, mine_at, branch):
    mine = src[pl.ds(pl.multiple_of(mine_at, GS), GS), :].astype(F32)
    out_ref[rows, :] = (mine + branch.astype(F32)).astype(BF16)


def own_block(b, alone, flags, g, ordered, params):
    whole, positions = g.shape
    proj_weight, conv_weight, h, gain, bias = params
    chans = proj_weight.shape[2]

    def kernel(flags_ref, g_ref, w_ref, wc_ref, h_ref, gain_ref, bias_ref, out_ref, g_buf):
        src = g_ref
        if not ordered:
            in_order(g_buf, g_ref, chans)
            src = g_buf
        ga = jnp.dot(w_ref[0, 0], src[...], preferred_element_type=F32)
        row, col = grid_of((GS, positions))
        gains, biases = columns_of(gain_ref, bias_ref, b)
        for at in range(0, chans, GS):
            rows = slice(at, at + GS)
            xhat, _, _, slope, inv_std = norm_group(h_ref[0, 0, rows, :], gains[rows], biases[rows])
            gh = gh_of(ga[rows, :], xhat, slope * (gains[rows] * inv_std))
            branch = conv_back(wc_ref[0, 0, rows, :], gh, row, col)
            add_branch(out_ref, rows, src, flags_ref[1] * chans + at, branch)

    def at_block(shape):
        return pl.BlockSpec((1, 1) + shape[2:], lambda i: (0, b, 0, 0))

    return pl.pallas_call(
        kernel,
        out_shape=shape_of((chans, positions), BF16),
        grid=(1,),
        in_specs=[SMEM, VMEM, at_block(proj_weight.shape), at_block(conv_weight.shape)]
        + [VMEM] * 3,
        out_specs=VMEM,
        scratch_shapes=[pltpu.VMEM((16, 128) if ordered else (whole, positions), BF16)],
        compiler_params=vmem(56 if alone else 8),
        name="own_block",
    )(flags, g, *params)


def first_block(flags, g, ordered, own_rows, pack):
    whole, positions = g.shape
    chans = pack.shape[0]
    width = whole
    per = whole // 2 // own_rows
    shape = (per, 2, own_rows, positions)
    g = g.reshape(shape if ordered else (2, per, own_rows, positions))

    def kernel(
        flags_ref, g_ref, pack_ref, out_ref, xhat_out, rate_out,
        w_ref, taps_ref, h_ref, g_buf, src, xhat_ref, rate_ref, stacks, sems,
    ):
        def copy(i, a, to):
            return pltpu.make_async_copy(a, to, sems.at[i])

        loads = [
            copy(0, pack_ref.at[:, width + TAIL : width + TAIL + positions], h_ref),
            copy(1, pack_ref.at[:, width : width + TAIL], taps_ref),
            copy(2, pack_ref.at[:, :width], w_ref),
        ] + [
            copy(3 + c, g_ref.at[:, c] if ordered else g_ref.at[c], g_buf.at[:, c])
            for c in range(2)
        ]
        for load in loads:
            load.start()
        loads[0].wait()
        loads[1].wait()
        at = 9 * GS - 384
        stats = norm_stats([h_ref[q : q + GS, :] for q in range(0, chans, GS)])
        for q in range(0, chans, GS):
            rows = slice(q, q + GS)
            side = taps_ref[rows, 384:].astype(F32)
            gain, bias = (
                side[:, i : i + 1] + side[:, i + 1 : i + 2] + side[:, i + 2 : i + 3]
                for i in (at, at + 3)
            )
            xhat, _, _, slope, inv_std = norm_group(h_ref[rows, :], gain, bias, stats[q // GS])
            xhat_ref[rows, :] = xhat
            rate_ref[rows, :] = slope * (gain * inv_std)
        stores = [copy(5, xhat_ref, xhat_out), copy(6, rate_ref, rate_out)]
        for store in stores:
            store.start()
        for load in loads[2:]:
            load.wait()
        src[...] = g_buf[...].reshape(whole, positions)
        wide_body(
            flags_ref, src, w_ref[...], lambda rows: taps_ref[rows, : 9 * GS],
            xhat_ref, rate_ref, out_ref, own_rows, stacks,
        )
        for store in stores:
            store.wait()

    full = shape_of((chans, positions), F32)
    return pl.pallas_call(
        kernel,
        out_shape=(shape_of((chans, positions), BF16), full, full),
        in_specs=[SMEM, ANY, ANY],
        out_specs=[VMEM, ANY, ANY],
        scratch_shapes=[
            pltpu.VMEM((chans, width), BF16),
            pltpu.VMEM((chans, TAIL), BF16),
            pltpu.VMEM((chans, positions), BF16),
            pltpu.VMEM(shape, BF16),
            pltpu.VMEM((whole, positions), BF16),
            pltpu.VMEM((chans, positions), F32),
            pltpu.VMEM((chans, positions), F32),
            pltpu.VMEM((4, 9 * GS, positions), BF16),
            pltpu.SemaphoreType.DMA((7,)),
        ],
        compiler_params=vmem(56),
        name="first_block",
    )(flags, g, pack)


def wide_body(flags_ref, src, matrix, taps_of, xhat_ref, rate_ref, out_ref, own_rows, stacks):
    chans, positions = xhat_ref.shape
    ga = jnp.dot(matrix, src[...], preferred_element_type=F32)
    core = flags_ref[1] & 1
    row, col = grid_of((GS, positions))
    means = [
        gh_means(ga[at : at + GS, :], xhat_ref[at : at + GS, :], rate_ref[at : at + GS, :])
        for at in range(0, chans, GS)
    ]
    for at in range(0, chans, GS):
        y, q = divmod(at, own_rows)
        rows = slice(at, at + GS)
        gh = gh_of(ga[rows, :], xhat_ref[rows, :], rate_ref[rows, :], means[at // GS])
        stack = stacks.at[at // GS % stacks.shape[0]]
        branch = conv_back_stacked(taps_of(rows), gh, row, col, stack)
        add_branch(out_ref, rows, src, (2 * y + core) * own_rows + q, branch)


def wide_block(flags, g, ordered, own_rows, pack, state):
    whole, positions = g.shape
    chans = pack.shape[0]

    def kernel(flags_ref, g_ref, pack_ref, xhat_ref, rate_ref, out_ref, g_buf, stacks):
        src = g_ref
        if not ordered:
            in_order(g_buf, g_ref, own_rows)
            src = g_buf
        wide_body(
            flags_ref, src, pack_ref[:, :whole],
            lambda rows: pack_ref[rows, whole : whole + 9 * GS],
            xhat_ref, rate_ref, out_ref, own_rows, stacks,
        )

    return pl.pallas_call(
        kernel,
        out_shape=shape_of((chans, positions), BF16),
        in_specs=[SMEM] + [VMEM] * 4,
        out_specs=VMEM,
        scratch_shapes=[
            pltpu.VMEM((16, 128) if ordered else (whole, positions), BF16),
            pltpu.VMEM((4, 9 * GS, positions), BF16),
        ],
        compiler_params=vmem(14),
        name="wide_block",
    )(flags, g, pack, *state)


def storer(out_ref):
    step = out_ref.shape[2]

    def store(first_row, at, value):
        for i in range(value.shape[1] // step):
            out_ref[at // step + i, first_row : first_row + value.shape[0], :] = value[
                :, i * step : (i + 1) * step
            ]

    return store


def summed(in_ref, rows):
    acc = in_ref[0, rows, :].astype(F32)
    for m in range(1, in_ref.shape[0]):
        acc = acc + in_ref[m, rows, :].astype(F32)
    return acc.astype(BF16)


def weight_grads(flags, orders, kept, latents, params, inputs):
    proj_weight, conv_weight, h_one, h_two, gain, bias = params
    ticks = len(latents)
    chans, width = proj_weight.shape[2:]
    positions = h_one.shape[3]
    shards = width // chans
    slab = positions // shards
    members = lax.axis_size("dp")
    step = (width + TAIL) // members
    pairs = shards // 2

    def split(g, ordered):
        return g.reshape((pairs, 2, chans, positions) if ordered else (2, pairs, chans, positions))

    operands = [split(g, o) for b in range(2) for g, o in zip(kept[b], orders[b])]
    operands += [split(g, o) for o, g in latents]
    order_of = [*orders[0], *orders[1], *(o for o, _ in latents)]

    def kernel(*refs):
        flags_ref = refs[0]
        fetched = refs[1 : 1 + len(operands)]
        w_ref, h1_ref, h2_ref, gain_ref, bias_ref, *x_refs = refs[1 + len(operands) : -5]
        out_ref, lat_ref, stacks, g_bufs, sems = refs[-5:]
        segment_at, chan_at = flags_ref[0], flags_ref[1]

        def copies(t):
            made = []
            for i in range(3):
                g = fetched[ticks * i + t]
                for c in range(2):
                    made.append(
                        pltpu.make_async_copy(
                            g.at[:, c] if order_of[ticks * i + t] else g.at[c],
                            g_bufs.at[i, :, c],
                            sems.at[len(made)],
                        )
                    )
            return made

        def each(act):
            for t in range(ticks):

                @pl.when(segment_at == ticks - 1 - t)
                def _():
                    for made in copies(t):
                        act(made)

        each(lambda made: made.start())
        row, col = grid_of((GS, positions))
        lane = lax.broadcasted_iota(jnp.int32, (GS, TAIL), 1)
        for b in range(2):
            for q in range(0, chans, GS):
                x = x_refs[b][0, 0, q : q + GS, :].astype(F32)
                for step_row in (-1, 0, 1):
                    for step_col in (-1, 0, 1):
                        tap = 3 * (step_row + 1) + step_col + 1
                        stacks[b, q // GS, tap * GS : (tap + 1) * GS, :] = shifted(
                            x, step_row, step_col, row, col
                        ).astype(BF16)
                stacks[b, q // GS, 9 * GS :, :] = jnp.zeros((TAIL - 9 * GS, positions), BF16)
        each(lambda made: made.wait())
        store = storer(out_ref)
        for b, h_ref in enumerate((h1_ref, h2_ref)):
            g = g_bufs[b].reshape(width, positions)
            ga = jnp.dot(w_ref[0, b], g, preferred_element_type=F32)
            gains, biases = columns_of(gain_ref, bias_ref, b)
            acts = []
            for q in range(0, chans, GS):
                rows = slice(q, q + GS)
                xhat, n, sig, slope, inv_std = norm_group(
                    h_ref[0, 0, rows, :], gains[rows], biases[rows]
                )
                acts.append((n * sig).astype(BF16))
                gh = gh_of(ga[rows, :], xhat, slope * (gains[rows] * inv_std))
                taps = lax.dot_general(
                    gh, stacks[b, q // GS], NT, preferred_element_type=F32
                )
                gn = ga[rows, :] * slope
                by_gain = jnp.sum(gn * xhat, axis=1, keepdims=True)
                by_bias = jnp.sum(gn, axis=1, keepdims=True)
                taps = jnp.where(lane == 9 * GS, by_gain, taps)
                taps = jnp.where(lane == 9 * GS + 1, by_bias, taps)
                store(b * chans + q, width, taps.astype(BF16))
            act = jnp.concatenate(acts, axis=0)
            proj = lax.dot_general(act, g, NT, preferred_element_type=F32)
            store(b * chans, 0, proj.astype(BF16))
        lat_ref[...] = own_positions(g_bufs[2].reshape(width, positions), chan_at, slab)

    return pl.pallas_call(
        kernel,
        out_shape=(
            shape_of((members, 2 * chans, step), BF16),
            shape_of((slab, width), BF16),
        ),
        in_specs=[SMEM] + [ANY] * len(operands) + [VMEM] * 7,
        out_specs=[VMEM] * 2,
        scratch_shapes=[
            pltpu.VMEM((2, chans // GS, TAIL, positions), BF16),
            pltpu.VMEM((3, pairs, 2, chans, positions), BF16),
            pltpu.SemaphoreType.DMA((6,)),
        ],
        compiler_params=vmem(56),
        name="weight_grads",
    )(flags, *operands, proj_weight, h_one, h_two, gain, bias, *inputs)


def sum_kernel(in_ref, out_ref):
    done = summed(in_ref, slice(0, out_ref.shape[1]))
    for m in range(out_ref.shape[0]):
        out_ref[m] = done


def spread_sums(parts):
    return pl.pallas_call(
        sum_kernel,
        out_shape=shape_of(parts.shape, BF16),
        in_specs=[VMEM],
        out_specs=VMEM,
        compiler_params=vmem(6),
        name="sum_microbatches",
    )(parts)


def widen_kernel(in_ref, proj_ref, conv_ref, gain_ref, bias_ref):
    chans, width = proj_ref.shape[2:]
    step = in_ref.shape[2]
    down = lax.broadcasted_iota(jnp.int32, (chans, chans), 0)
    across = lax.broadcasted_iota(jnp.int32, (chans, chans), 1)
    first = width // step
    for b in range(2):
        rows = slice(b * chans, (b + 1) * chans)
        for i in range(first):
            proj_ref[0, b, :, i * step : (i + 1) * step] = in_ref[i, rows, :].astype(F32)
        conv_ref[0, b, :, :step] = in_ref[first, rows, :].astype(F32)
        side = in_ref[first + 1, rows, :].astype(F32)
        conv_ref[0, b, :, step:] = side[:, : 9 * GS - step]
        for i, to in enumerate((gain_ref, bias_ref)):
            at = 9 * GS - step + i
            lined = jnp.where(down == across, side[:, at : at + 1], 0.0)
            to[0, b : b + 1, :] = jnp.sum(lined, axis=0, keepdims=True)


def widen(sums, width):
    chans = sums.shape[1] // 2
    return pl.pallas_call(
        widen_kernel,
        out_shape=(
            shape_of((1, 2, chans, width), F32),
            shape_of((1, 2, chans, 9 * GS), F32),
            shape_of((1, 2, chans), F32),
            shape_of((1, 2, chans), F32),
        ),
        in_specs=[VMEM],
        out_specs=[VMEM] * 4,
        compiler_params=vmem(8),
        name="widen",
    )(sums)


def gather(block_, axis, groups=None):
    return lax.all_gather(block_, axis, axis=0, tiled=True, axis_index_groups=groups)


def per_device(
    grad_top,
    inputs_one,
    conv_one,
    inputs_two,
    conv_two,
    proj_weight,
    conv_weight,
    norm_gain,
    norm_bias,
):
    segments = lax.axis_size("segment")
    segment_at = lax.axis_index("segment")
    chan_at = lax.axis_index("chan")
    members = lax.axis_size("dp")
    shards = lax.axis_size("chan")
    chans, positions = conv_one.shape[2:]
    width = proj_weight.shape[3]
    cores = [[2 * y, 2 * y + 1] for y in range(shards // 2)]
    columns = [[2 * y + c for y in range(shards // 2)] for c in range(2)]

    def exchange(blocks):
        return lax.all_to_all(blocks, "dp", split_axis=0, concat_axis=0, tiled=True)

    params = (proj_weight, conv_weight, conv_one, conv_two, norm_gain, norm_bias)
    first_pack, second_pack = prepare(*params)
    packs = [None, gather(second_pack, "chan", columns)]
    packs[0] = lax.all_gather(
        first_pack[None], "chan", axis=1, tiled=True, axis_index_groups=columns
    )[0]
    states = [None, None]
    kept = [[], []]
    orders = [[], []]
    latents = []
    flags = jnp.stack([segment_at.astype(jnp.int32), chan_at.astype(jnp.int32)])
    for tick in range(segments):
        if tick == 0:
            g = lax.all_gather(grad_top[0], "chan", axis=1, tiled=True)
            ordered = True
        else:
            lower = segments - 1 - tick
            rest = [s for s in range(segments) if s not in (lower, lower + 1)]
            groups = sorted(
                [[lower, lower + 1]] + [rest[i : i + 2] for i in range(0, len(rest), 2)]
            )
            ordered = out.shape[0] == chans
            moved = gather(out, "segment", groups)[out.shape[0] :]
            g = gather(moved, "chan", None if ordered else cores)
            latents.append((ordered, g))
        for b in (1, 0):
            kept[b].append(g)
            if tick == 0 or (tick == 1 and b == 0):
                h = conv_two if b == 1 else conv_one
                out = own_block(
                    b, tick == 1, flags, g, ordered,
                    (proj_weight, conv_weight, h, norm_gain, norm_bias),
                )
            elif states[b] is None:
                packs[b], g = lax.optimization_barrier((packs[b], g))
                out, *states[b] = first_block(flags, g, ordered, chans, packs[b])
            else:
                out = wide_block(flags, g, ordered, chans, packs[b], states[b])
            orders[b].append(ordered)
            if b == 1 or tick == segments - 1:
                ordered = out.shape[0] == chans
                g = gather(out, "chan", None if ordered else cores)
    latents.append((ordered, g))

    parts, latent = weight_grads(
        flags, orders, kept, latents, params, (inputs_one, inputs_two)
    )
    sums = exchange(spread_sums(exchange(parts)))
    proj, conv, by_gain, by_bias = widen(sums, width)
    return latent.T[None, None], proj, conv, by_gain, by_bias


def solution(mesh):
    return jax.shard_map(
        per_device,
        mesh=mesh,
        in_specs=(
            P("dp", None, "chan"),
            P("segment", "dp", "chan", None),
            P("segment", "dp", "chan", None),
            P("segment", "dp", "chan", None),
            P("segment", "dp", "chan", None),
            P("segment", None, "chan", None),
            P("segment", None, "chan", None),
            P("segment", None, "chan"),
            P("segment", None, "chan"),
        ),
        out_specs=(
            P("segment", "dp", None, "chan"),
            P("segment", None, "chan", None),
            P("segment", None, "chan", None),
            P("segment", None, "chan"),
            P("segment", None, "chan"),
        ),
        check_vma=False,
    )
```

```python
import functools

import jax
import jax.numpy as jnp
from jax import lax
from jax.experimental import pallas as pl
from jax.experimental.pallas import tpu as pltpu
from jax.sharding import PartitionSpec as P

GS = 48
WW = 64
NORM_EPS = 1e-05
TAIL = 512
F32 = jnp.float32
BF16 = jnp.bfloat16
VMEM = pl.BlockSpec(memory_space=pltpu.VMEM)
SMEM = pl.BlockSpec(memory_space=pltpu.SMEM)
ANY = pl.BlockSpec(memory_space=pl.ANY)
NT = (((1,), (1,)), ((), ()))
TN = (((0,), (0,)), ((), ()))


def vmem(mebibytes):
    return pltpu.CompilerParams(vmem_limit_bytes=mebibytes * 1024 * 1024)


def shape_of(shape, dtype):
    return jax.ShapeDtypeStruct(shape, dtype)


def total(block):
    return jnp.sum(jnp.sum(block, axis=1, keepdims=True), axis=0, keepdims=True)


def norm_stats(blocks):
    scale = 1.0 / (blocks[0].shape[0] * blocks[0].shape[1])
    means = [total(h.astype(F32)) * scale for h in blocks]
    spreads = []
    for h, mean in zip(blocks, means):
        pre = h.astype(F32) - mean
        spreads.append(lax.rsqrt(total(pre * pre) * scale + NORM_EPS))
    return list(zip(means, spreads))


def norm_group(h, gain, bias, stats=None):
    mean, inv_std = norm_stats([h])[0] if stats is None else stats
    pre = h.astype(F32) - mean
    xhat = pre * inv_std
    n = xhat * gain + bias
    sig = jax.nn.sigmoid(n)
    slope = sig * (1.0 + n * (1.0 - sig))
    return xhat, n, sig, slope, inv_std


def column(line):
    count = line.shape[1]
    down = lax.broadcasted_iota(jnp.int32, (count, count), 0)
    across = lax.broadcasted_iota(jnp.int32, (count, count), 1)
    return jnp.sum(jnp.where(down == across, line, 0.0), axis=1, keepdims=True)


def columns_of(gain_ref, bias_ref, b):
    return column(gain_ref[0, b : b + 1, :]), column(bias_ref[0, b : b + 1, :])


def prepare_kernel(*refs):
    pack_refs = (refs[6], refs[7])
    w_ref, wc_ref, h1_ref, h2_ref, gain_ref, bias_ref, sems = refs[8:]
    copies = [
        pltpu.make_async_copy(refs[i], refs[8 + i], sems.at[i]) for i in range(6)
    ]
    for copy in copies:
        copy.start()
    for copy in copies:
        copy.wait()
    chans, width = w_ref.shape[2:]
    taps = wc_ref.shape[3]
    lane = lax.broadcasted_iota(jnp.int32, (chans, TAIL - 384), 1)
    down = lax.broadcasted_iota(jnp.int32, (GS, GS), 0)
    across = lax.broadcasted_iota(jnp.int32, (GS, GS), 1)
    same = jnp.where(down == across, 1.0, 0.0).astype(BF16)
    for b, h_ref in ((1, h2_ref), (0, h1_ref)):
        pack_ref = pack_refs[b]
        pack_ref[:, :width] = w_ref[0, b]
        turned = []
        for q in range(0, chans, GS):
            taps_w = [
                lax.dot_general(
                    same,
                    wc_ref[0, b, q : q + GS, k * GS : (k + 1) * GS],
                    NT,
                    preferred_element_type=F32,
                )
                for k in range(taps // GS)
            ]
            turned.append(
                jnp.concatenate([*taps_w, jnp.zeros((GS, TAIL - taps), F32)], axis=1)
            )
        turned = jnp.concatenate(turned, axis=0)
        pack_ref[:, width : width + 384] = turned[:, :384].astype(BF16)
        last = turned[:, 384:]
        at = taps - 384
        for whole in columns_of(gain_ref, bias_ref, b):
            rest = whole
            for _ in range(3):
                piece = rest.astype(BF16).astype(F32)
                rest = rest - piece
                last = jnp.where(lane == at, piece, last)
                at += 1
        pack_ref[:, width + 384 : width + TAIL] = last.astype(BF16)
        pack_ref[:, width + TAIL :] = h_ref[0, 0]


def prepare(*operands):
    chans, width = operands[0].shape[2:]
    positions = operands[2].shape[3]
    pack = shape_of((chans, width + TAIL + positions), BF16)
    return pl.pallas_call(
        prepare_kernel,
        out_shape=(pack, pack),
        in_specs=[ANY] * 6,
        out_specs=[VMEM] * 2,
        scratch_shapes=[pltpu.VMEM(x.shape, x.dtype) for x in operands]
        + [pltpu.SemaphoreType.DMA((6,))],
        compiler_params=vmem(56),
        name="prepare",
    )(*operands)


def shifted(value, step_row, step_col, row, col):
    length = value.shape[1]
    rows = length // WW
    by = step_row * WW + step_col
    if by == 0:
        return value
    moved = pltpu.roll(value, (-by) % length, axis=1)
    inside = None
    if step_row:
        inside = row < rows - 1 if step_row > 0 else row > 0
    if step_col:
        here = col < WW - 1 if step_col > 0 else col > 0
        inside = here if inside is None else inside & here
    return jnp.where(inside, moved, 0.0)


def grid_of(shape):
    lane = lax.broadcasted_iota(jnp.int32, shape, 1)
    return lane // WW, lane % WW


def own_positions(g, chan_at, count):
    down = lax.broadcasted_iota(jnp.int32, (count, g.shape[1]), 0)
    across = lax.broadcasted_iota(jnp.int32, (count, g.shape[1]), 1)
    pick = jnp.where(across == down + chan_at * count, 1.0, 0.0).astype(BF16)
    return lax.dot_general(pick, g, NT, preferred_element_type=F32).astype(BF16)


def gh_means(ga, xhat, rate):
    scale = 1.0 / (ga.shape[0] * ga.shape[1])
    rw = ga * rate
    return total(rw) * scale, total(rw * xhat) * scale


def gh_of(ga, xhat, rate, means=None):
    first, second = gh_means(ga, xhat, rate) if means is None else means
    return (ga * rate - first - xhat * second).astype(BF16)


def conv_back(taps_w, gh, row, col):
    spread = lax.dot_general(taps_w, gh, TN, preferred_element_type=F32)
    branch = None
    for step_col in (-1, 0, 1):
        part = None
        for step_row in (-1, 0, 1):
            tap = 3 * (step_row + 1) + step_col + 1
            term = shifted(spread[tap * GS : (tap + 1) * GS, :], -step_row, 0, row, col)
            part = term if part is None else part + term
        part = shifted(part, 0, -step_col, row, col)
        branch = part if branch is None else branch + part
    return branch.astype(BF16)


def conv_back_stacked(taps_w, gh, row, col, stack):
    gh = gh.astype(F32)
    for step_col in (-1, 0, 1):
        moved = shifted(gh, 0, -step_col, row, col)
        for step_row in (-1, 0, 1):
            tap = 3 * (step_row + 1) + step_col + 1
            stack[tap * GS : (tap + 1) * GS, :] = shifted(
                moved, -step_row, 0, row, col
            ).astype(BF16)
    return jnp.dot(taps_w, stack[...], preferred_element_type=F32).astype(BF16)


def in_order(g_buf, g_ref, own_rows):
    per = g_ref.shape[0] // 2 // own_rows
    for c in range(2):
        for y in range(per):
            to = (2 * y + c) * own_rows
            at = (c * per + y) * own_rows
            g_buf[to : to + own_rows, :] = g_ref[at : at + own_rows, :]


def add_branch(out_ref, rows, src, mine_at, branch):
    mine = src[pl.ds(pl.multiple_of(mine_at, GS), GS), :].astype(F32)
    out_ref[rows, :] = (mine + branch.astype(F32)).astype(BF16)


def own_block(b, alone, flags, g, ordered, params):
    whole, positions = g.shape
    proj_weight, conv_weight, h, gain, bias = params
    chans = proj_weight.shape[2]

    def kernel(flags_ref, g_ref, w_ref, wc_ref, h_ref, gain_ref, bias_ref, out_ref, g_buf):
        src = g_ref
        if not ordered:
            in_order(g_buf, g_ref, chans)
            src = g_buf
        ga = jnp.dot(w_ref[0, 0], src[...], preferred_element_type=F32)
        row, col = grid_of((GS, positions))
        gains, biases = columns_of(gain_ref, bias_ref, b)
        for at in range(0, chans, GS):
            rows = slice(at, at + GS)
            xhat, _, _, slope, inv_std = norm_group(h_ref[0, 0, rows, :], gains[rows], biases[rows])
            gh = gh_of(ga[rows, :], xhat, slope * (gains[rows] * inv_std))
            branch = conv_back(wc_ref[0, 0, rows, :], gh, row, col)
            add_branch(out_ref, rows, src, flags_ref[1] * chans + at, branch)

    def at_block(shape):
        return pl.BlockSpec((1, 1) + shape[2:], lambda i: (0, b, 0, 0))

    return pl.pallas_call(
        kernel,
        out_shape=shape_of((chans, positions), BF16),
        grid=(1,),
        in_specs=[SMEM, VMEM, at_block(proj_weight.shape), at_block(conv_weight.shape)]
        + [VMEM] * 3,
        out_specs=VMEM,
        scratch_shapes=[pltpu.VMEM((16, 128) if ordered else (whole, positions), BF16)],
        compiler_params=vmem(8 if alone else 8),
        name="own_block",
    )(flags, g, *params)


def first_block(flags, g, ordered, own_rows, pack):
    whole, positions = g.shape
    chans = pack.shape[0]
    width = whole
    per = whole // 2 // own_rows
    shape = (per, 2, own_rows, positions)
    g = g.reshape(shape if ordered else (2, per, own_rows, positions))

    def kernel(
        flags_ref, g_ref, pack_ref, out_ref, xhat_out, rate_out,
        w_ref, taps_ref, h_ref, g_buf, src, xhat_ref, rate_ref, stacks, sems,
    ):
        def copy(i, a, to):
            return pltpu.make_async_copy(a, to, sems.at[i])

        loads = [
            copy(0, pack_ref.at[:, width + TAIL : width + TAIL + positions], h_ref),
            copy(1, pack_ref.at[:, width : width + TAIL], taps_ref),
            copy(2, pack_ref.at[:, :width], w_ref),
        ] + [
            copy(3 + c, g_ref.at[:, c] if ordered else g_ref.at[c], g_buf.at[:, c])
            for c in range(2)
        ]
        for load in loads:
            load.start()
        loads[0].wait()
        loads[1].wait()
        at = 9 * GS - 384
        stats = norm_stats([h_ref[q : q + GS, :] for q in range(0, chans, GS)])
        for q in range(0, chans, GS):
            rows = slice(q, q + GS)
            side = taps_ref[rows, 384:].astype(F32)
            gain, bias = (
                side[:, i : i + 1] + side[:, i + 1 : i + 2] + side[:, i + 2 : i + 3]
                for i in (at, at + 3)
            )
            xhat, _, _, slope, inv_std = norm_group(h_ref[rows, :], gain, bias, stats[q // GS])
            xhat_ref[rows, :] = xhat
            rate_ref[rows, :] = slope * (gain * inv_std)
        stores = [copy(5, xhat_ref, xhat_out), copy(6, rate_ref, rate_out)]
        for store in stores:
            store.start()
        for load in loads[2:]:
            load.wait()
        src[...] = g_buf[...].reshape(whole, positions)
        wide_body(
            flags_ref, src, w_ref[...], lambda rows: taps_ref[rows, : 9 * GS],
            xhat_ref, rate_ref, out_ref, own_rows, stacks,
        )
        for store in stores:
            store.wait()

    full = shape_of((chans, positions), F32)
    return pl.pallas_call(
        kernel,
        out_shape=(shape_of((chans, positions), BF16), full, full),
        in_specs=[SMEM, ANY, ANY],
        out_specs=[VMEM, ANY, ANY],
        scratch_shapes=[
            pltpu.VMEM((chans, width), BF16),
            pltpu.VMEM((chans, TAIL), BF16),
            pltpu.VMEM((chans, positions), BF16),
            pltpu.VMEM(shape, BF16),
            pltpu.VMEM((whole, positions), BF16),
            pltpu.VMEM((chans, positions), F32),
            pltpu.VMEM((chans, positions), F32),
            pltpu.VMEM((4, 9 * GS, positions), BF16),
            pltpu.SemaphoreType.DMA((7,)),
        ],
        compiler_params=vmem(40),
        name="first_block",
    )(flags, g, pack)


def wide_body(flags_ref, src, matrix, taps_of, xhat_ref, rate_ref, out_ref, own_rows, stacks):
    chans, positions = xhat_ref.shape
    ga = jnp.dot(matrix, src[...], preferred_element_type=F32)
    core = flags_ref[1] & 1
    row, col = grid_of((GS, positions))
    means = [
        gh_means(ga[at : at + GS, :], xhat_ref[at : at + GS, :], rate_ref[at : at + GS, :])
        for at in range(0, chans, GS)
    ]
    for at in range(0, chans, GS):
        y, q = divmod(at, own_rows)
        rows = slice(at, at + GS)
        gh = gh_of(ga[rows, :], xhat_ref[rows, :], rate_ref[rows, :], means[at // GS])
        stack = stacks.at[at // GS % stacks.shape[0]]
        branch = conv_back_stacked(taps_of(rows), gh, row, col, stack)
        add_branch(out_ref, rows, src, (2 * y + core) * own_rows + q, branch)


def wide_block(flags, g, ordered, own_rows, pack, state):
    whole, positions = g.shape
    chans = pack.shape[0]

    def kernel(flags_ref, g_ref, pack_ref, xhat_ref, rate_ref, out_ref, g_buf, stacks):
        src = g_ref
        if not ordered:
            in_order(g_buf, g_ref, own_rows)
            src = g_buf
        wide_body(
            flags_ref, src, pack_ref[:, :whole],
            lambda rows: pack_ref[rows, whole : whole + 9 * GS],
            xhat_ref, rate_ref, out_ref, own_rows, stacks,
        )

    return pl.pallas_call(
        kernel,
        out_shape=shape_of((chans, positions), BF16),
        in_specs=[SMEM] + [VMEM] * 4,
        out_specs=VMEM,
        scratch_shapes=[
            pltpu.VMEM((16, 128) if ordered else (whole, positions), BF16),
            pltpu.VMEM((4, 9 * GS, positions), BF16),
        ],
        compiler_params=vmem(14),
        name="wide_block",
    )(flags, g, pack, *state)


def storer(out_ref):
    step = out_ref.shape[2]

    def store(first_row, at, value):
        for i in range(value.shape[1] // step):
            out_ref[at // step + i, first_row : first_row + value.shape[0], :] = value[
                :, i * step : (i + 1) * step
            ]

    return store


def summed(in_ref, rows):
    acc = in_ref[0, rows, :].astype(F32)
    for m in range(1, in_ref.shape[0]):
        acc = acc + in_ref[m, rows, :].astype(F32)
    return acc.astype(BF16)


def weight_grads(flags, orders, kept, latents, params, inputs):
    proj_weight, conv_weight, h_one, h_two, gain, bias = params
    ticks = len(latents)
    chans, width = proj_weight.shape[2:]
    positions = h_one.shape[3]
    shards = width // chans
    slab = positions // shards
    members = lax.axis_size("dp")
    step = (width + TAIL) // members
    pairs = shards // 2

    def split(g, ordered):
        return g.reshape((pairs, 2, chans, positions) if ordered else (2, pairs, chans, positions))

    operands = [split(g, o) for b in range(2) for g, o in zip(kept[b], orders[b])]
    operands += [split(g, o) for o, g in latents]
    order_of = [*orders[0], *orders[1], *(o for o, _ in latents)]

    def kernel(*refs):
        flags_ref = refs[0]
        fetched = refs[1 : 1 + len(operands)]
        w_ref, h1_ref, h2_ref, gain_ref, bias_ref, *x_refs = refs[1 + len(operands) : -7]
        out_ref, lat_ref, stacks, g_bufs, kept_ref, act_ref, sems = refs[-7:]
        segment_at, chan_at = flags_ref[0], flags_ref[1]

        def copies(t):
            made = []
            for i in range(3):
                g = fetched[ticks * i + t]
                for c in range(2):
                    made.append(
                        pltpu.make_async_copy(
                            g.at[:, c] if order_of[ticks * i + t] else g.at[c],
                            g_bufs.at[i, :, c],
                            sems.at[len(made)],
                        )
                    )
            return made

        def each(act, only=slice(None)):
            for t in range(ticks):

                @pl.when(segment_at == ticks - 1 - t)
                def _():
                    for made in copies(t)[only]:
                        act(made)

        each(lambda made: made.start())
        row, col = grid_of((GS, positions))
        lane = lax.broadcasted_iota(jnp.int32, (GS, TAIL), 1)
        for b in range(2):
            for q in range(0, chans, GS):
                x = x_refs[b][0, 0, q : q + GS, :].astype(F32)
                for step_row in (-1, 0, 1):
                    for step_col in (-1, 0, 1):
                        tap = 3 * (step_row + 1) + step_col + 1
                        stacks[b, q // GS, tap * GS : (tap + 1) * GS, :] = shifted(
                            x, step_row, step_col, row, col
                        ).astype(BF16)
                stacks[b, q // GS, 9 * GS :, :] = jnp.zeros((TAIL - 9 * GS, positions), BF16)
        norms = []
        for b, h_ref in enumerate((h1_ref, h2_ref)):
            gains, biases = columns_of(gain_ref, bias_ref, b)
            blocks = [h_ref[0, 0, q : q + GS, :] for q in range(0, chans, GS)]
            stats = norm_stats(blocks)
            for i, h in enumerate(blocks):
                rows = slice(i * GS, (i + 1) * GS)
                xhat, n, sig, slope, inv_std = norm_group(h, gains[rows], biases[rows], stats[i])
                kept_ref[0, b, rows, :] = xhat
                kept_ref[1, b, rows, :] = slope
                kept_ref[2, b, rows, :] = slope * (gains[rows] * inv_std)
                act_ref[b, rows, :] = (n * sig).astype(BF16)
        store = storer(out_ref)
        for b in range(2):
            each(lambda made: made.wait(), slice(2 * b, 2 * b + 2))
            g = g_bufs[b].reshape(width, positions)
            ga = jnp.dot(w_ref[0, b], g, preferred_element_type=F32)
            proj = lax.dot_general(act_ref[b], g, NT, preferred_element_type=F32)
            store(b * chans, 0, proj.astype(BF16))
            for q in range(0, chans, GS):
                rows = slice(q, q + GS)
                xhat = kept_ref[0, b, rows, :]
                gh = gh_of(ga[rows, :], xhat, kept_ref[2, b, rows, :])
                taps = lax.dot_general(
                    gh, stacks[b, q // GS], NT, preferred_element_type=F32
                )
                gn = ga[rows, :] * kept_ref[1, b, rows, :]
                by_gain = jnp.sum(gn * xhat, axis=1, keepdims=True)
                by_bias = jnp.sum(gn, axis=1, keepdims=True)
                taps = jnp.where(lane == 9 * GS, by_gain, taps)
                taps = jnp.where(lane == 9 * GS + 1, by_bias, taps)
                store(b * chans + q, width, taps.astype(BF16))
        each(lambda made: made.wait(), slice(4, 6))
        lat_ref[...] = own_positions(g_bufs[2].reshape(width, positions), chan_at, slab)

    return pl.pallas_call(
        kernel,
        out_shape=(
            shape_of((members, 2 * chans, step), BF16),
            shape_of((slab, width), BF16),
        ),
        in_specs=[SMEM] + [ANY] * len(operands) + [VMEM] * 7,
        out_specs=[VMEM] * 2,
        scratch_shapes=[
            pltpu.VMEM((2, chans // GS, TAIL, positions), BF16),
            pltpu.VMEM((3, pairs, 2, chans, positions), BF16),
            pltpu.VMEM((3, 2, chans, positions), F32),
            pltpu.VMEM((2, chans, positions), BF16),
            pltpu.SemaphoreType.DMA((6,)),
        ],
        compiler_params=vmem(56),
        name="weight_grads",
    )(flags, *operands, proj_weight, h_one, h_two, gain, bias, *inputs)


def sum_kernel(in_ref, out_ref):
    done = summed(in_ref, slice(0, out_ref.shape[1]))
    for m in range(out_ref.shape[0]):
        out_ref[m] = done


def spread_sums(parts):
    return pl.pallas_call(
        sum_kernel,
        out_shape=shape_of(parts.shape, BF16),
        in_specs=[VMEM],
        out_specs=VMEM,
        compiler_params=vmem(6),
        name="sum_microbatches",
    )(parts)


def widen_kernel(in_ref, proj_ref, conv_ref, gain_ref, bias_ref):
    chans, width = proj_ref.shape[2:]
    step = in_ref.shape[2]
    down = lax.broadcasted_iota(jnp.int32, (chans, chans), 0)
    across = lax.broadcasted_iota(jnp.int32, (chans, chans), 1)
    first = width // step
    for b in range(2):
        rows = slice(b * chans, (b + 1) * chans)
        for i in range(first):
            proj_ref[0, b, :, i * step : (i + 1) * step] = in_ref[i, rows, :].astype(F32)
        conv_ref[0, b, :, :step] = in_ref[first, rows, :].astype(F32)
        side = in_ref[first + 1, rows, :].astype(F32)
        conv_ref[0, b, :, step:] = side[:, : 9 * GS - step]
        for i, to in enumerate((gain_ref, bias_ref)):
            at = 9 * GS - step + i
            lined = jnp.where(down == across, side[:, at : at + 1], 0.0)
            to[0, b : b + 1, :] = jnp.sum(lined, axis=0, keepdims=True)


def widen(sums, width):
    chans = sums.shape[1] // 2
    return pl.pallas_call(
        widen_kernel,
        out_shape=(
            shape_of((1, 2, chans, width), F32),
            shape_of((1, 2, chans, 9 * GS), F32),
            shape_of((1, 2, chans), F32),
            shape_of((1, 2, chans), F32),
        ),
        in_specs=[VMEM],
        out_specs=[VMEM] * 4,
        compiler_params=vmem(8),
        name="widen",
    )(sums)


def gather(block_, axis, groups=None):
    return lax.all_gather(block_, axis, axis=0, tiled=True, axis_index_groups=groups)


def per_device(
    grad_top,
    inputs_one,
    conv_one,
    inputs_two,
    conv_two,
    proj_weight,
    conv_weight,
    norm_gain,
    norm_bias,
):
    segments = lax.axis_size("segment")
    segment_at = lax.axis_index("segment")
    chan_at = lax.axis_index("chan")
    members = lax.axis_size("dp")
    shards = lax.axis_size("chan")
    chans, positions = conv_one.shape[2:]
    width = proj_weight.shape[3]
    cores = [[2 * y, 2 * y + 1] for y in range(shards // 2)]
    columns = [[2 * y + c for y in range(shards // 2)] for c in range(2)]

    def exchange(blocks):
        return lax.all_to_all(blocks, "dp", split_axis=0, concat_axis=0, tiled=True)

    params = (proj_weight, conv_weight, conv_one, conv_two, norm_gain, norm_bias)
    first_pack, second_pack = prepare(*params)
    packs = [None, gather(second_pack, "chan", columns)]
    packs[0] = lax.all_gather(
        first_pack[None], "chan", axis=1, tiled=True, axis_index_groups=columns
    )[0]
    states = [None, None]
    kept = [[], []]
    orders = [[], []]
    latents = []
    flags = jnp.stack([segment_at.astype(jnp.int32), chan_at.astype(jnp.int32)])
    for tick in range(segments):
        if tick == 0:
            g = lax.all_gather(grad_top[0], "chan", axis=1, tiled=True)
            ordered = True
        else:
            lower = segments - 1 - tick
            rest = [s for s in range(segments) if s not in (lower, lower + 1)]
            groups = sorted(
                [[lower, lower + 1]] + [rest[i : i + 2] for i in range(0, len(rest), 2)]
            )
            ordered = out.shape[0] == chans
            moved = gather(out, "segment", groups)[out.shape[0] :]
            g = gather(moved, "chan", None if ordered else cores)
            latents.append((ordered, g))
        for b in (1, 0):
            kept[b].append(g)
            if tick == 0 or (tick == 1 and b == 0):
                h = conv_two if b == 1 else conv_one
                out = own_block(
                    b, tick == 1, flags, g, ordered,
                    (proj_weight, conv_weight, h, norm_gain, norm_bias),
                )
            elif states[b] is None:
                packs[b], g = lax.optimization_barrier((packs[b], g))
                out, *states[b] = first_block(flags, g, ordered, chans, packs[b])
            else:
                out = wide_block(flags, g, ordered, chans, packs[b], states[b])
            orders[b].append(ordered)
            if b == 1 or tick == segments - 1:
                ordered = out.shape[0] == chans
                g = gather(out, "chan", None if ordered else cores)
    latents.append((ordered, g))

    parts, latent = weight_grads(
        flags, orders, kept, latents, params, (inputs_one, inputs_two)
    )
    sums = exchange(spread_sums(exchange(parts)))
    proj, conv, by_gain, by_bias = widen(sums, width)
    return latent.T[None, None], proj, conv, by_gain, by_bias


def solution(mesh):
    return jax.shard_map(
        per_device,
        mesh=mesh,
        in_specs=(
            P("dp", None, "chan"),
            P("segment", "dp", "chan", None),
            P("segment", "dp", "chan", None),
            P("segment", "dp", "chan", None),
            P("segment", "dp", "chan", None),
            P("segment", None, "chan", None),
            P("segment", None, "chan", None),
            P("segment", None, "chan"),
            P("segment", None, "chan"),
        ),
        out_specs=(
            P("segment", "dp", None, "chan"),
            P("segment", None, "chan", None),
            P("segment", None, "chan", None),
            P("segment", None, "chan"),
            P("segment", None, "chan"),
        ),
        check_vma=False,
    )
```

```python
import functools

import jax
import jax.numpy as jnp
from jax import lax
from jax.experimental import pallas as pl
from jax.experimental.pallas import tpu as pltpu
from jax.sharding import PartitionSpec as P

GS = 48
WW = 64
NORM_EPS = 1e-05
TAIL = 512
F32 = jnp.float32
BF16 = jnp.bfloat16
VMEM = pl.BlockSpec(memory_space=pltpu.VMEM)
SMEM = pl.BlockSpec(memory_space=pltpu.SMEM)
ANY = pl.BlockSpec(memory_space=pl.ANY)
NT = (((1,), (1,)), ((), ()))
TN = (((0,), (0,)), ((), ()))


def vmem(mebibytes):
    return pltpu.CompilerParams(vmem_limit_bytes=mebibytes * 1024 * 1024)


def shape_of(shape, dtype):
    return jax.ShapeDtypeStruct(shape, dtype)


def total(block):
    return jnp.sum(jnp.sum(block, axis=1, keepdims=True), axis=0, keepdims=True)


def norm_stats(blocks):
    scale = 1.0 / (blocks[0].shape[0] * blocks[0].shape[1])
    means = [total(h.astype(F32)) * scale for h in blocks]
    spreads = []
    for h, mean in zip(blocks, means):
        pre = h.astype(F32) - mean
        spreads.append(lax.rsqrt(total(pre * pre) * scale + NORM_EPS))
    return list(zip(means, spreads))


def norm_group(h, gain, bias, stats=None):
    mean, inv_std = norm_stats([h])[0] if stats is None else stats
    pre = h.astype(F32) - mean
    xhat = pre * inv_std
    n = xhat * gain + bias
    sig = jax.nn.sigmoid(n)
    slope = sig * (1.0 + n * (1.0 - sig))
    return xhat, n, sig, slope, inv_std


def column(line):
    count = line.shape[1]
    down = lax.broadcasted_iota(jnp.int32, (count, count), 0)
    across = lax.broadcasted_iota(jnp.int32, (count, count), 1)
    return jnp.sum(jnp.where(down == across, line, 0.0), axis=1, keepdims=True)


def columns_of(gain_ref, bias_ref, b):
    return column(gain_ref[0, b : b + 1, :]), column(bias_ref[0, b : b + 1, :])


def prepare_kernel(*refs):
    pack_refs = (refs[6], refs[7])
    w_ref, wc_ref, h1_ref, h2_ref, gain_ref, bias_ref, sems = refs[8:]
    copies = [
        pltpu.make_async_copy(refs[i], refs[8 + i], sems.at[i]) for i in range(6)
    ]
    for copy in copies:
        copy.start()
    for copy in copies:
        copy.wait()
    chans, width = w_ref.shape[2:]
    taps = wc_ref.shape[3]
    lane = lax.broadcasted_iota(jnp.int32, (chans, TAIL - 384), 1)
    down = lax.broadcasted_iota(jnp.int32, (GS, GS), 0)
    across = lax.broadcasted_iota(jnp.int32, (GS, GS), 1)
    same = jnp.where(down == across, 1.0, 0.0).astype(BF16)
    for b, h_ref in ((1, h2_ref), (0, h1_ref)):
        pack_ref = pack_refs[b]
        pack_ref[:, :width] = w_ref[0, b]
        turned = []
        for q in range(0, chans, GS):
            taps_w = [
                lax.dot_general(
                    same,
                    wc_ref[0, b, q : q + GS, k * GS : (k + 1) * GS],
                    NT,
                    preferred_element_type=F32,
                )
                for k in range(taps // GS)
            ]
            turned.append(
                jnp.concatenate([*taps_w, jnp.zeros((GS, TAIL - taps), F32)], axis=1)
            )
        turned = jnp.concatenate(turned, axis=0)
        pack_ref[:, width : width + 384] = turned[:, :384].astype(BF16)
        last = turned[:, 384:]
        at = taps - 384
        for whole in columns_of(gain_ref, bias_ref, b):
            rest = whole
            for _ in range(3):
                piece = rest.astype(BF16).astype(F32)
                rest = rest - piece
                last = jnp.where(lane == at, piece, last)
                at += 1
        pack_ref[:, width + 384 : width + TAIL] = last.astype(BF16)
        pack_ref[:, width + TAIL :] = h_ref[0, 0]


def prepare(*operands):
    chans, width = operands[0].shape[2:]
    positions = operands[2].shape[3]
    pack = shape_of((chans, width + TAIL + positions), BF16)
    return pl.pallas_call(
        prepare_kernel,
        out_shape=(pack, pack),
        in_specs=[ANY] * 6,
        out_specs=[VMEM] * 2,
        scratch_shapes=[pltpu.VMEM(x.shape, x.dtype) for x in operands]
        + [pltpu.SemaphoreType.DMA((6,))],
        compiler_params=vmem(56),
        name="prepare",
    )(*operands)


def shifted(value, step_row, step_col, row, col):
    length = value.shape[1]
    rows = length // WW
    by = step_row * WW + step_col
    if by == 0:
        return value
    moved = pltpu.roll(value, (-by) % length, axis=1)
    inside = None
    if step_row:
        inside = row < rows - 1 if step_row > 0 else row > 0
    if step_col:
        here = col < WW - 1 if step_col > 0 else col > 0
        inside = here if inside is None else inside & here
    return jnp.where(inside, moved, 0.0)


def grid_of(shape):
    lane = lax.broadcasted_iota(jnp.int32, shape, 1)
    return lane // WW, lane % WW


def own_positions(g, chan_at, count):
    down = lax.broadcasted_iota(jnp.int32, (count, g.shape[1]), 0)
    across = lax.broadcasted_iota(jnp.int32, (count, g.shape[1]), 1)
    pick = jnp.where(across == down + chan_at * count, 1.0, 0.0).astype(BF16)
    return lax.dot_general(pick, g, NT, preferred_element_type=F32).astype(BF16)


def gh_means(ga, xhat, rate):
    scale = 1.0 / (ga.shape[0] * ga.shape[1])
    rw = ga * rate
    return total(rw) * scale, total(rw * xhat) * scale


def gh_of(ga, xhat, rate, means=None):
    first, second = gh_means(ga, xhat, rate) if means is None else means
    return (ga * rate - first - xhat * second).astype(BF16)


def conv_back(taps_w, gh, row, col):
    spread = lax.dot_general(taps_w, gh, TN, preferred_element_type=F32)
    branch = None
    for step_col in (-1, 0, 1):
        part = None
        for step_row in (-1, 0, 1):
            tap = 3 * (step_row + 1) + step_col + 1
            term = shifted(spread[tap * GS : (tap + 1) * GS, :], -step_row, 0, row, col)
            part = term if part is None else part + term
        part = shifted(part, 0, -step_col, row, col)
        branch = part if branch is None else branch + part
    return branch.astype(BF16)


def conv_back_stacked(taps_w, gh, row, col, stack):
    gh = gh.astype(F32)
    for step_col in (-1, 0, 1):
        moved = shifted(gh, 0, -step_col, row, col)
        for step_row in (-1, 0, 1):
            tap = 3 * (step_row + 1) + step_col + 1
            stack[tap * GS : (tap + 1) * GS, :] = shifted(
                moved, -step_row, 0, row, col
            ).astype(BF16)
    return jnp.dot(taps_w, stack[...], preferred_element_type=F32).astype(BF16)


def in_order(g_buf, g_ref, own_rows):
    per = g_ref.shape[0] // 2 // own_rows
    for c in range(2):
        for y in range(per):
            to = (2 * y + c) * own_rows
            at = (c * per + y) * own_rows
            g_buf[to : to + own_rows, :] = g_ref[at : at + own_rows, :]


def add_branch(out_ref, rows, src, mine_at, branch):
    mine = src[pl.ds(pl.multiple_of(mine_at, GS), GS), :].astype(F32)
    out_ref[rows, :] = (mine + branch.astype(F32)).astype(BF16)


def own_block(b, alone, flags, g, ordered, params):
    whole, positions = g.shape
    proj_weight, conv_weight, h, gain, bias = params
    chans = proj_weight.shape[2]

    def kernel(flags_ref, g_ref, w_ref, wc_ref, h_ref, gain_ref, bias_ref, out_ref, g_buf):
        src = g_ref
        if not ordered:
            in_order(g_buf, g_ref, chans)
            src = g_buf
        ga = jnp.dot(w_ref[0, 0], src[...], preferred_element_type=F32)
        row, col = grid_of((GS, positions))
        gains, biases = columns_of(gain_ref, bias_ref, b)
        for at in range(0, chans, GS):
            rows = slice(at, at + GS)
            xhat, _, _, slope, inv_std = norm_group(h_ref[0, 0, rows, :], gains[rows], biases[rows])
            gh = gh_of(ga[rows, :], xhat, slope * (gains[rows] * inv_std))
            branch = conv_back(wc_ref[0, 0, rows, :], gh, row, col)
            add_branch(out_ref, rows, src, flags_ref[1] * chans + at, branch)

    def at_block(shape):
        return pl.BlockSpec((1, 1) + shape[2:], lambda i: (0, b, 0, 0))

    return pl.pallas_call(
        kernel,
        out_shape=shape_of((chans, positions), BF16),
        grid=(1,),
        in_specs=[SMEM, VMEM, at_block(proj_weight.shape), at_block(conv_weight.shape)]
        + [VMEM] * 3,
        out_specs=VMEM,
        scratch_shapes=[pltpu.VMEM((16, 128) if ordered else (whole, positions), BF16)],
        compiler_params=vmem(8 if alone else 8),
        name="own_block",
    )(flags, g, *params)


def first_block(flags, g, ordered, own_rows, pack):
    whole, positions = g.shape
    chans = pack.shape[0]
    width = whole
    per = whole // 2 // own_rows
    shape = (per, 2, own_rows, positions)
    g = g.reshape(shape if ordered else (2, per, own_rows, positions))

    def kernel(
        flags_ref, g_ref, pack_ref, out_ref, xhat_out, rate_out,
        w_ref, taps_ref, h_ref, g_buf, src, xhat_ref, rate_ref, stacks, sems,
    ):
        def copy(i, a, to):
            return pltpu.make_async_copy(a, to, sems.at[i])

        loads = [
            copy(0, pack_ref.at[:, width + TAIL : width + TAIL + positions], h_ref),
            copy(1, pack_ref.at[:, width : width + TAIL], taps_ref),
            copy(2, pack_ref.at[:, :width], w_ref),
        ] + [
            copy(3 + c, g_ref.at[:, c] if ordered else g_ref.at[c], g_buf.at[:, c])
            for c in range(2)
        ]
        for load in loads:
            load.start()
        loads[0].wait()
        loads[1].wait()
        at = 9 * GS - 384
        stats = norm_stats([h_ref[q : q + GS, :] for q in range(0, chans, GS)])
        for q in range(0, chans, GS):
            rows = slice(q, q + GS)
            side = taps_ref[rows, 384:].astype(F32)
            gain, bias = (
                side[:, i : i + 1] + side[:, i + 1 : i + 2] + side[:, i + 2 : i + 3]
                for i in (at, at + 3)
            )
            xhat, _, _, slope, inv_std = norm_group(h_ref[rows, :], gain, bias, stats[q // GS])
            xhat_ref[rows, :] = xhat
            rate_ref[rows, :] = slope * (gain * inv_std)
        stores = [copy(5, xhat_ref, xhat_out), copy(6, rate_ref, rate_out)]
        for store in stores:
            store.start()
        for load in loads[2:]:
            load.wait()
        src[...] = g_buf[...].reshape(whole, positions)
        wide_body(
            flags_ref, src, w_ref[...], lambda rows: taps_ref[rows, : 9 * GS],
            xhat_ref, rate_ref, out_ref, own_rows, stacks,
        )
        for store in stores:
            store.wait()

    full = shape_of((chans, positions), F32)
    return pl.pallas_call(
        kernel,
        out_shape=(shape_of((chans, positions), BF16), full, full),
        in_specs=[SMEM, ANY, ANY],
        out_specs=[VMEM, ANY, ANY],
        scratch_shapes=[
            pltpu.VMEM((chans, width), BF16),
            pltpu.VMEM((chans, TAIL), BF16),
            pltpu.VMEM((chans, positions), BF16),
            pltpu.VMEM(shape, BF16),
            pltpu.VMEM((whole, positions), BF16),
            pltpu.VMEM((chans, positions), F32),
            pltpu.VMEM((chans, positions), F32),
            pltpu.VMEM((4, 9 * GS, positions), BF16),
            pltpu.SemaphoreType.DMA((7,)),
        ],
        compiler_params=vmem(40),
        name="first_block",
    )(flags, g, pack)


def wide_body(flags_ref, src, matrix, taps_of, xhat_ref, rate_ref, out_ref, own_rows, stacks):
    chans, positions = xhat_ref.shape
    ga = jnp.dot(matrix, src[...], preferred_element_type=F32)
    core = flags_ref[1] & 1
    row, col = grid_of((GS, positions))
    means = [
        gh_means(ga[at : at + GS, :], xhat_ref[at : at + GS, :], rate_ref[at : at + GS, :])
        for at in range(0, chans, GS)
    ]
    for at in range(0, chans, GS):
        y, q = divmod(at, own_rows)
        rows = slice(at, at + GS)
        gh = gh_of(ga[rows, :], xhat_ref[rows, :], rate_ref[rows, :], means[at // GS])
        stack = stacks.at[at // GS % stacks.shape[0]]
        branch = conv_back_stacked(taps_of(rows), gh, row, col, stack)
        add_branch(out_ref, rows, src, (2 * y + core) * own_rows + q, branch)


def wide_block(flags, g, ordered, own_rows, pack, state):
    whole, positions = g.shape
    chans = pack.shape[0]

    def kernel(flags_ref, g_ref, pack_ref, xhat_ref, rate_ref, out_ref, g_buf, stacks):
        src = g_ref
        if not ordered:
            in_order(g_buf, g_ref, own_rows)
            src = g_buf
        wide_body(
            flags_ref, src, pack_ref[:, :whole],
            lambda rows: pack_ref[rows, whole : whole + 9 * GS],
            xhat_ref, rate_ref, out_ref, own_rows, stacks,
        )

    return pl.pallas_call(
        kernel,
        out_shape=shape_of((chans, positions), BF16),
        in_specs=[SMEM] + [VMEM] * 4,
        out_specs=VMEM,
        scratch_shapes=[
            pltpu.VMEM((16, 128) if ordered else (whole, positions), BF16),
            pltpu.VMEM((4, 9 * GS, positions), BF16),
        ],
        compiler_params=vmem(14),
        name="wide_block",
    )(flags, g, pack, *state)


def storer(out_ref):
    step = out_ref.shape[2]

    def store(first_row, at, value):
        for i in range(value.shape[1] // step):
            out_ref[at // step + i, first_row : first_row + value.shape[0], :] = value[
                :, i * step : (i + 1) * step
            ]

    return store


def summed(in_ref, rows):
    acc = in_ref[0, rows, :].astype(F32)
    for m in range(1, in_ref.shape[0]):
        acc = acc + in_ref[m, rows, :].astype(F32)
    return acc.astype(BF16)


def weight_grads(flags, orders, kept, latents, params, inputs):
    proj_weight, conv_weight, h_one, h_two, gain, bias = params
    ticks = len(latents)
    chans, width = proj_weight.shape[2:]
    positions = h_one.shape[3]
    shards = width // chans
    slab = positions // shards
    members = lax.axis_size("dp")
    step = (width + TAIL) // members
    pairs = shards // 2

    def split(g, ordered):
        return g.reshape((pairs, 2, chans, positions) if ordered else (2, pairs, chans, positions))

    operands = [split(g, o) for b in range(2) for g, o in zip(kept[b], orders[b])]
    operands += [split(g, o) for o, g in latents]
    order_of = [*orders[0], *orders[1], *(o for o, _ in latents)]

    def kernel(*refs):
        flags_ref = refs[0]
        fetched = refs[1 : 1 + len(operands)]
        w_ref, h1_ref, h2_ref, gain_ref, bias_ref, *x_refs = refs[1 + len(operands) : -7]
        out_ref, lat_ref, stacks, g_bufs, kept_ref, act_ref, sems = refs[-7:]
        segment_at, chan_at = flags_ref[0], flags_ref[1]

        def copies(t):
            made = []
            for i in range(3):
                g = fetched[ticks * i + t]
                for c in range(2):
                    made.append(
                        pltpu.make_async_copy(
                            g.at[:, c] if order_of[ticks * i + t] else g.at[c],
                            g_bufs.at[i, :, c],
                            sems.at[len(made)],
                        )
                    )
            return made

        def each(act, only=slice(None)):
            for t in range(ticks):

                @pl.when(segment_at == ticks - 1 - t)
                def _():
                    for made in copies(t)[only]:
                        act(made)

        each(lambda made: made.start())
        row, col = grid_of((GS, positions))
        lane = lax.broadcasted_iota(jnp.int32, (GS, TAIL), 1)
        for b in range(2):
            for q in range(0, chans, GS):
                x = x_refs[b][0, 0, q : q + GS, :].astype(F32)
                for step_row in (-1, 0, 1):
                    for step_col in (-1, 0, 1):
                        tap = 3 * (step_row + 1) + step_col + 1
                        stacks[b, q // GS, tap * GS : (tap + 1) * GS, :] = shifted(
                            x, step_row, step_col, row, col
                        ).astype(BF16)
                stacks[b, q // GS, 9 * GS :, :] = jnp.zeros((TAIL - 9 * GS, positions), BF16)
        norms = []
        for b, h_ref in enumerate((h1_ref, h2_ref)):
            gains, biases = columns_of(gain_ref, bias_ref, b)
            blocks = [h_ref[0, 0, q : q + GS, :] for q in range(0, chans, GS)]
            stats = norm_stats(blocks)
            for i, h in enumerate(blocks):
                rows = slice(i * GS, (i + 1) * GS)
                xhat, n, sig, slope, inv_std = norm_group(h, gains[rows], biases[rows], stats[i])
                kept_ref[0, b, rows, :] = xhat
                kept_ref[1, b, rows, :] = slope
                kept_ref[2, b, rows, :] = slope * (gains[rows] * inv_std)
                act_ref[b, rows, :] = (n * sig).astype(BF16)
        store = storer(out_ref)
        for b in range(2):
            each(lambda made: made.wait(), slice(2 * b, 2 * b + 2))
            g = g_bufs[b].reshape(width, positions)
            ga = jnp.dot(w_ref[0, b], g, preferred_element_type=F32)
            proj = lax.dot_general(act_ref[b], g, NT, preferred_element_type=F32)
            store(b * chans, 0, proj.astype(BF16))
            for q in range(0, chans, GS):
                rows = slice(q, q + GS)
                xhat = kept_ref[0, b, rows, :]
                gh = gh_of(ga[rows, :], xhat, kept_ref[2, b, rows, :])
                taps = lax.dot_general(
                    gh, stacks[b, q // GS], NT, preferred_element_type=F32
                )
                gn = ga[rows, :] * kept_ref[1, b, rows, :]
                by_gain = jnp.sum(gn * xhat, axis=1, keepdims=True)
                by_bias = jnp.sum(gn, axis=1, keepdims=True)
                taps = jnp.where(lane == 9 * GS, by_gain, taps)
                taps = jnp.where(lane == 9 * GS + 1, by_bias, taps)
                store(b * chans + q, width, taps.astype(BF16))
        each(lambda made: made.wait(), slice(4, 6))
        lat_ref[...] = own_positions(g_bufs[2].reshape(width, positions), chan_at, slab)

    return pl.pallas_call(
        kernel,
        out_shape=(
            shape_of((members, 2 * chans, step), BF16),
            shape_of((slab, width), BF16),
        ),
        in_specs=[SMEM] + [ANY] * len(operands) + [VMEM] * 7,
        out_specs=[VMEM] * 2,
        scratch_shapes=[
            pltpu.VMEM((2, chans // GS, TAIL, positions), BF16),
            pltpu.VMEM((3, pairs, 2, chans, positions), BF16),
            pltpu.VMEM((3, 2, chans, positions), F32),
            pltpu.VMEM((2, chans, positions), BF16),
            pltpu.SemaphoreType.DMA((6,)),
        ],
        compiler_params=vmem(24),
        name="weight_grads",
    )(flags, *operands, proj_weight, h_one, h_two, gain, bias, *inputs)


def sum_kernel(in_ref, out_ref):
    done = summed(in_ref, slice(0, out_ref.shape[1]))
    for m in range(out_ref.shape[0]):
        out_ref[m] = done


def spread_sums(parts):
    return pl.pallas_call(
        sum_kernel,
        out_shape=shape_of(parts.shape, BF16),
        in_specs=[VMEM],
        out_specs=VMEM,
        compiler_params=vmem(6),
        name="sum_microbatches",
    )(parts)


def widen_kernel(in_ref, proj_ref, conv_ref, gain_ref, bias_ref):
    chans, width = proj_ref.shape[2:]
    step = in_ref.shape[2]
    down = lax.broadcasted_iota(jnp.int32, (chans, chans), 0)
    across = lax.broadcasted_iota(jnp.int32, (chans, chans), 1)
    first = width // step
    for b in range(2):
        rows = slice(b * chans, (b + 1) * chans)
        for i in range(first):
            proj_ref[0, b, :, i * step : (i + 1) * step] = in_ref[i, rows, :].astype(F32)
        conv_ref[0, b, :, :step] = in_ref[first, rows, :].astype(F32)
        side = in_ref[first + 1, rows, :].astype(F32)
        conv_ref[0, b, :, step:] = side[:, : 9 * GS - step]
        for i, to in enumerate((gain_ref, bias_ref)):
            at = 9 * GS - step + i
            lined = jnp.where(down == across, side[:, at : at + 1], 0.0)
            to[0, b : b + 1, :] = jnp.sum(lined, axis=0, keepdims=True)


def widen(sums, width):
    chans = sums.shape[1] // 2
    return pl.pallas_call(
        widen_kernel,
        out_shape=(
            shape_of((1, 2, chans, width), F32),
            shape_of((1, 2, chans, 9 * GS), F32),
            shape_of((1, 2, chans), F32),
            shape_of((1, 2, chans), F32),
        ),
        in_specs=[VMEM],
        out_specs=[VMEM] * 4,
        compiler_params=vmem(8),
        name="widen",
    )(sums)


def gather(block_, axis, groups=None):
    return lax.all_gather(block_, axis, axis=0, tiled=True, axis_index_groups=groups)


def per_device(
    grad_top,
    inputs_one,
    conv_one,
    inputs_two,
    conv_two,
    proj_weight,
    conv_weight,
    norm_gain,
    norm_bias,
):
    segments = lax.axis_size("segment")
    segment_at = lax.axis_index("segment")
    chan_at = lax.axis_index("chan")
    members = lax.axis_size("dp")
    shards = lax.axis_size("chan")
    chans, positions = conv_one.shape[2:]
    width = proj_weight.shape[3]
    cores = [[2 * y, 2 * y + 1] for y in range(shards // 2)]
    columns = [[2 * y + c for y in range(shards // 2)] for c in range(2)]

    def exchange(blocks):
        return lax.all_to_all(blocks, "dp", split_axis=0, concat_axis=0, tiled=True)

    params = (proj_weight, conv_weight, conv_one, conv_two, norm_gain, norm_bias)
    first_pack, second_pack = prepare(*params)
    packs = [None, gather(second_pack, "chan", columns)]
    packs[0] = lax.all_gather(
        first_pack[None], "chan", axis=1, tiled=True, axis_index_groups=columns
    )[0]
    states = [None, None]
    kept = [[], []]
    orders = [[], []]
    latents = []
    flags = jnp.stack([segment_at.astype(jnp.int32), chan_at.astype(jnp.int32)])
    for tick in range(segments):
        if tick == 0:
            g = lax.all_gather(grad_top[0], "chan", axis=1, tiled=True)
            ordered = True
        else:
            lower = segments - 1 - tick
            rest = [s for s in range(segments) if s not in (lower, lower + 1)]
            groups = sorted(
                [[lower, lower + 1]] + [rest[i : i + 2] for i in range(0, len(rest), 2)]
            )
            ordered = out.shape[0] == chans
            moved = gather(out, "segment", groups)[out.shape[0] :]
            g = gather(moved, "chan", None if ordered else cores)
            latents.append((ordered, g))
        for b in (1, 0):
            kept[b].append(g)
            if tick == 0 or (tick == 1 and b == 0):
                h = conv_two if b == 1 else conv_one
                out = own_block(
                    b, tick == 1, flags, g, ordered,
                    (proj_weight, conv_weight, h, norm_gain, norm_bias),
                )
            elif states[b] is None:
                packs[b], g = lax.optimization_barrier((packs[b], g))
                out, *states[b] = first_block(flags, g, ordered, chans, packs[b])
            else:
                out = wide_block(flags, g, ordered, chans, packs[b], states[b])
            orders[b].append(ordered)
            if b == 1 or tick == segments - 1:
                ordered = out.shape[0] == chans
                g = gather(out, "chan", None if ordered else cores)
    latents.append((ordered, g))

    parts, latent = weight_grads(
        flags, orders, kept, latents, params, (inputs_one, inputs_two)
    )
    sums = exchange(spread_sums(exchange(parts)))
    proj, conv, by_gain, by_bias = widen(sums, width)
    return latent.T[None, None], proj, conv, by_gain, by_bias


def solution(mesh):
    return jax.shard_map(
        per_device,
        mesh=mesh,
        in_specs=(
            P("dp", None, "chan"),
            P("segment", "dp", "chan", None),
            P("segment", "dp", "chan", None),
            P("segment", "dp", "chan", None),
            P("segment", "dp", "chan", None),
            P("segment", None, "chan", None),
            P("segment", None, "chan", None),
            P("segment", None, "chan"),
            P("segment", None, "chan"),
        ),
        out_specs=(
            P("segment", "dp", None, "chan"),
            P("segment", None, "chan", None),
            P("segment", None, "chan", None),
            P("segment", None, "chan"),
            P("segment", None, "chan"),
        ),
        check_vma=False,
    )
```

```python
import functools

import jax
import jax.numpy as jnp
from jax import lax
from jax.experimental import pallas as pl
from jax.experimental.pallas import tpu as pltpu
from jax.sharding import PartitionSpec as P

GS = 48
WW = 64
NORM_EPS = 1e-05
TAIL = 512
F32 = jnp.float32
BF16 = jnp.bfloat16
VMEM = pl.BlockSpec(memory_space=pltpu.VMEM)
SMEM = pl.BlockSpec(memory_space=pltpu.SMEM)
ANY = pl.BlockSpec(memory_space=pl.ANY)
NT = (((1,), (1,)), ((), ()))
TN = (((0,), (0,)), ((), ()))


def vmem(mebibytes):
    return pltpu.CompilerParams(vmem_limit_bytes=mebibytes * 1024 * 1024)


def shape_of(shape, dtype):
    return jax.ShapeDtypeStruct(shape, dtype)


def total(block):
    return jnp.sum(jnp.sum(block, axis=1, keepdims=True), axis=0, keepdims=True)


def norm_stats(blocks):
    scale = 1.0 / (blocks[0].shape[0] * blocks[0].shape[1])
    means = [total(h.astype(F32)) * scale for h in blocks]
    spreads = []
    for h, mean in zip(blocks, means):
        pre = h.astype(F32) - mean
        spreads.append(lax.rsqrt(total(pre * pre) * scale + NORM_EPS))
    return list(zip(means, spreads))


def norm_group(h, gain, bias, stats=None):
    mean, inv_std = norm_stats([h])[0] if stats is None else stats
    pre = h.astype(F32) - mean
    xhat = pre * inv_std
    n = xhat * gain + bias
    sig = jax.nn.sigmoid(n)
    slope = sig * (1.0 + n * (1.0 - sig))
    return xhat, n, sig, slope, inv_std


def column(line):
    count = line.shape[1]
    down = lax.broadcasted_iota(jnp.int32, (count, count), 0)
    across = lax.broadcasted_iota(jnp.int32, (count, count), 1)
    return jnp.sum(jnp.where(down == across, line, 0.0), axis=1, keepdims=True)


def columns_of(gain_ref, bias_ref, b):
    return column(gain_ref[0, b : b + 1, :]), column(bias_ref[0, b : b + 1, :])


def prepare_kernel(*refs):
    pack_refs = (refs[6], refs[7])
    w_ref, h_refs = refs[0], refs[2:4]
    wc_ref, gain_ref, bias_ref, taps_ref, sems = refs[8:]
    chans, width = w_ref.shape[2:]
    copies = [
        pltpu.make_async_copy(a, to, sems.at[i])
        for i, (a, to) in enumerate(((refs[1], wc_ref), (refs[4], gain_ref), (refs[5], bias_ref)))
    ]
    for b in (1, 0):
        copies += [
            pltpu.make_async_copy(
                w_ref.at[0, b], pack_refs[b].at[:, :width], sems.at[3 + 3 * b]
            ),
            pltpu.make_async_copy(
                h_refs[b].at[0, 0], pack_refs[b].at[:, width + TAIL :], sems.at[4 + 3 * b]
            ),
        ]
    for copy in copies:
        copy.start()
    for copy in copies[:3]:
        copy.wait()
    taps = wc_ref.shape[3]
    lane = lax.broadcasted_iota(jnp.int32, (chans, TAIL - 384), 1)
    down = lax.broadcasted_iota(jnp.int32, (GS, GS), 0)
    across = lax.broadcasted_iota(jnp.int32, (GS, GS), 1)
    same = jnp.where(down == across, 1.0, 0.0).astype(BF16)
    for b in (1, 0):
        turned = []
        for q in range(0, chans, GS):
            taps_w = [
                lax.dot_general(
                    same,
                    wc_ref[0, b, q : q + GS, k * GS : (k + 1) * GS],
                    NT,
                    preferred_element_type=F32,
                )
                for k in range(taps // GS)
            ]
            turned.append(
                jnp.concatenate([*taps_w, jnp.zeros((GS, TAIL - taps), F32)], axis=1)
            )
        turned = jnp.concatenate(turned, axis=0)
        taps_ref[b, :, :384] = turned[:, :384].astype(BF16)
        last = turned[:, 384:]
        at = taps - 384
        for whole in columns_of(gain_ref, bias_ref, b):
            rest = whole
            for _ in range(3):
                piece = rest.astype(BF16).astype(F32)
                rest = rest - piece
                last = jnp.where(lane == at, piece, last)
                at += 1
        taps_ref[b, :, 384:] = last.astype(BF16)
        copies.append(
            pltpu.make_async_copy(
                taps_ref.at[b], pack_refs[b].at[:, width : width + TAIL], sems.at[5 + 3 * b]
            )
        )
        copies[-1].start()
    for copy in copies[3:]:
        copy.wait()


def prepare(*operands):
    chans, width = operands[0].shape[2:]
    positions = operands[2].shape[3]
    pack = shape_of((chans, width + TAIL + positions), BF16)
    return pl.pallas_call(
        prepare_kernel,
        out_shape=(pack, pack),
        in_specs=[ANY] * 6,
        out_specs=[ANY] * 2,
        scratch_shapes=[pltpu.VMEM(operands[i].shape, operands[i].dtype) for i in (1, 4, 5)]
        + [pltpu.VMEM((2, chans, TAIL), BF16), pltpu.SemaphoreType.DMA((9,))],
        compiler_params=vmem(56),
        name="prepare",
    )(*operands)


def shifted(value, step_row, step_col, row, col):
    length = value.shape[1]
    rows = length // WW
    by = step_row * WW + step_col
    if by == 0:
        return value
    moved = pltpu.roll(value, (-by) % length, axis=1)
    inside = None
    if step_row:
        inside = row < rows - 1 if step_row > 0 else row > 0
    if step_col:
        here = col < WW - 1 if step_col > 0 else col > 0
        inside = here if inside is None else inside & here
    return jnp.where(inside, moved, 0.0)


def grid_of(shape):
    lane = lax.broadcasted_iota(jnp.int32, shape, 1)
    return lane // WW, lane % WW


def own_positions(g, chan_at, count):
    down = lax.broadcasted_iota(jnp.int32, (count, g.shape[1]), 0)
    across = lax.broadcasted_iota(jnp.int32, (count, g.shape[1]), 1)
    pick = jnp.where(across == down + chan_at * count, 1.0, 0.0).astype(BF16)
    return lax.dot_general(pick, g, NT, preferred_element_type=F32).astype(BF16)


def gh_means(ga, xhat, rate):
    scale = 1.0 / (ga.shape[0] * ga.shape[1])
    rw = ga * rate
    return total(rw) * scale, total(rw * xhat) * scale


def gh_of(ga, xhat, rate, means=None):
    first, second = gh_means(ga, xhat, rate) if means is None else means
    return (ga * rate - first - xhat * second).astype(BF16)


def conv_back(taps_w, gh, row, col):
    spread = lax.dot_general(taps_w, gh, TN, preferred_element_type=F32)
    branch = None
    for step_col in (-1, 0, 1):
        part = None
        for step_row in (-1, 0, 1):
            tap = 3 * (step_row + 1) + step_col + 1
            term = shifted(spread[tap * GS : (tap + 1) * GS, :], -step_row, 0, row, col)
            part = term if part is None else part + term
        part = shifted(part, 0, -step_col, row, col)
        branch = part if branch is None else branch + part
    return branch.astype(BF16)


def conv_back_stacked(taps_w, gh, row, col, stack):
    gh = gh.astype(F32)
    for step_col in (-1, 0, 1):
        moved = shifted(gh, 0, -step_col, row, col)
        for step_row in (-1, 0, 1):
            tap = 3 * (step_row + 1) + step_col + 1
            stack[tap * GS : (tap + 1) * GS, :] = shifted(
                moved, -step_row, 0, row, col
            ).astype(BF16)
    return jnp.dot(taps_w, stack[...], preferred_element_type=F32).astype(BF16)


def in_order(g_buf, g_ref, own_rows):
    per = g_ref.shape[0] // 2 // own_rows
    for c in range(2):
        for y in range(per):
            to = (2 * y + c) * own_rows
            at = (c * per + y) * own_rows
            g_buf[to : to + own_rows, :] = g_ref[at : at + own_rows, :]


def add_branch(out_ref, rows, src, mine_at, branch):
    mine = src[pl.ds(pl.multiple_of(mine_at, GS), GS), :].astype(F32)
    out_ref[rows, :] = (mine + branch.astype(F32)).astype(BF16)


def own_block(b, alone, flags, g, ordered, params):
    whole, positions = g.shape
    proj_weight, conv_weight, h, gain, bias = params
    chans = proj_weight.shape[2]

    def kernel(flags_ref, g_ref, w_ref, wc_ref, h_ref, gain_ref, bias_ref, out_ref, g_buf):
        src = g_ref
        if not ordered:
            in_order(g_buf, g_ref, chans)
            src = g_buf
        ga = jnp.dot(w_ref[0, 0], src[...], preferred_element_type=F32)
        row, col = grid_of((GS, positions))
        gains, biases = columns_of(gain_ref, bias_ref, b)
        for at in range(0, chans, GS):
            rows = slice(at, at + GS)
            xhat, _, _, slope, inv_std = norm_group(h_ref[0, 0, rows, :], gains[rows], biases[rows])
            gh = gh_of(ga[rows, :], xhat, slope * (gains[rows] * inv_std))
            branch = conv_back(wc_ref[0, 0, rows, :], gh, row, col)
            add_branch(out_ref, rows, src, flags_ref[1] * chans + at, branch)

    def at_block(shape):
        return pl.BlockSpec((1, 1) + shape[2:], lambda i: (0, b, 0, 0))

    return pl.pallas_call(
        kernel,
        out_shape=shape_of((chans, positions), BF16),
        grid=(1,),
        in_specs=[SMEM, VMEM, at_block(proj_weight.shape), at_block(conv_weight.shape)]
        + [VMEM] * 3,
        out_specs=VMEM,
        scratch_shapes=[pltpu.VMEM((16, 128) if ordered else (whole, positions), BF16)],
        compiler_params=vmem(8 if alone else 8),
        name="own_block",
    )(flags, g, *params)


def first_block(flags, g, ordered, own_rows, pack):
    whole, positions = g.shape
    chans = pack.shape[0]
    width = whole
    per = whole // 2 // own_rows
    shape = (per, 2, own_rows, positions)
    g = g.reshape(shape if ordered else (2, per, own_rows, positions))

    def kernel(
        flags_ref, g_ref, pack_ref, out_ref, xhat_out, rate_out,
        w_ref, taps_ref, h_ref, g_buf, src, xhat_ref, rate_ref, stacks, sems,
    ):
        def copy(i, a, to):
            return pltpu.make_async_copy(a, to, sems.at[i])

        loads = [
            copy(0, pack_ref.at[:, width + TAIL : width + TAIL + positions], h_ref),
            copy(1, pack_ref.at[:, width : width + TAIL], taps_ref),
            copy(2, pack_ref.at[:, :width], w_ref),
        ] + [
            copy(3 + c, g_ref.at[:, c] if ordered else g_ref.at[c], g_buf.at[:, c])
            for c in range(2)
        ]
        for load in loads:
            load.start()
        loads[0].wait()
        loads[1].wait()
        at = 9 * GS - 384
        stats = norm_stats([h_ref[q : q + GS, :] for q in range(0, chans, GS)])
        for q in range(0, chans, GS):
            rows = slice(q, q + GS)
            side = taps_ref[rows, 384:].astype(F32)
            gain, bias = (
                side[:, i : i + 1] + side[:, i + 1 : i + 2] + side[:, i + 2 : i + 3]
                for i in (at, at + 3)
            )
            xhat, _, _, slope, inv_std = norm_group(h_ref[rows, :], gain, bias, stats[q // GS])
            xhat_ref[rows, :] = xhat
            rate_ref[rows, :] = slope * (gain * inv_std)
        stores = [copy(5, xhat_ref, xhat_out), copy(6, rate_ref, rate_out)]
        for store in stores:
            store.start()
        for load in loads[2:]:
            load.wait()
        src[...] = g_buf[...].reshape(whole, positions)
        wide_body(
            flags_ref, src, w_ref[...], lambda rows: taps_ref[rows, : 9 * GS],
            xhat_ref, rate_ref, out_ref, own_rows, stacks,
        )
        for store in stores:
            store.wait()

    full = shape_of((chans, positions), F32)
    return pl.pallas_call(
        kernel,
        out_shape=(shape_of((chans, positions), BF16), full, full),
        in_specs=[SMEM, ANY, ANY],
        out_specs=[VMEM, ANY, ANY],
        scratch_shapes=[
            pltpu.VMEM((chans, width), BF16),
            pltpu.VMEM((chans, TAIL), BF16),
            pltpu.VMEM((chans, positions), BF16),
            pltpu.VMEM(shape, BF16),
            pltpu.VMEM((whole, positions), BF16),
            pltpu.VMEM((chans, positions), F32),
            pltpu.VMEM((chans, positions), F32),
            pltpu.VMEM((4, 9 * GS, positions), BF16),
            pltpu.SemaphoreType.DMA((7,)),
        ],
        compiler_params=vmem(40),
        name="first_block",
    )(flags, g, pack)


def wide_body(flags_ref, src, matrix, taps_of, xhat_ref, rate_ref, out_ref, own_rows, stacks):
    chans, positions = xhat_ref.shape
    ga = jnp.dot(matrix, src[...], preferred_element_type=F32)
    core = flags_ref[1] & 1
    row, col = grid_of((GS, positions))
    means = [
        gh_means(ga[at : at + GS, :], xhat_ref[at : at + GS, :], rate_ref[at : at + GS, :])
        for at in range(0, chans, GS)
    ]
    for at in range(0, chans, GS):
        y, q = divmod(at, own_rows)
        rows = slice(at, at + GS)
        gh = gh_of(ga[rows, :], xhat_ref[rows, :], rate_ref[rows, :], means[at // GS])
        stack = stacks.at[at // GS % stacks.shape[0]]
        branch = conv_back_stacked(taps_of(rows), gh, row, col, stack)
        add_branch(out_ref, rows, src, (2 * y + core) * own_rows + q, branch)


def wide_block(flags, g, ordered, own_rows, pack, state):
    whole, positions = g.shape
    chans = pack.shape[0]

    def kernel(flags_ref, g_ref, pack_ref, xhat_ref, rate_ref, out_ref, g_buf, stacks):
        src = g_ref
        if not ordered:
            in_order(g_buf, g_ref, own_rows)
            src = g_buf
        wide_body(
            flags_ref, src, pack_ref[:, :whole],
            lambda rows: pack_ref[rows, whole : whole + 9 * GS],
            xhat_ref, rate_ref, out_ref, own_rows, stacks,
        )

    return pl.pallas_call(
        kernel,
        out_shape=shape_of((chans, positions), BF16),
        in_specs=[SMEM] + [VMEM] * 4,
        out_specs=VMEM,
        scratch_shapes=[
            pltpu.VMEM((16, 128) if ordered else (whole, positions), BF16),
            pltpu.VMEM((4, 9 * GS, positions), BF16),
        ],
        compiler_params=vmem(14),
        name="wide_block",
    )(flags, g, pack, *state)


def storer(out_ref):
    step = out_ref.shape[2]

    def store(first_row, at, value):
        for i in range(value.shape[1] // step):
            out_ref[at // step + i, first_row : first_row + value.shape[0], :] = value[
                :, i * step : (i + 1) * step
            ]

    return store


def summed(in_ref, rows):
    acc = in_ref[0, rows, :].astype(F32)
    for m in range(1, in_ref.shape[0]):
        acc = acc + in_ref[m, rows, :].astype(F32)
    return acc.astype(BF16)


def weight_grads(flags, orders, kept, latents, params, inputs):
    proj_weight, conv_weight, h_one, h_two, gain, bias = params
    ticks = len(latents)
    chans, width = proj_weight.shape[2:]
    positions = h_one.shape[3]
    shards = width // chans
    slab = positions // shards
    members = lax.axis_size("dp")
    step = (width + TAIL) // members
    pairs = shards // 2

    def split(g, ordered):
        return g.reshape((pairs, 2, chans, positions) if ordered else (2, pairs, chans, positions))

    operands = [split(g, o) for b in range(2) for g, o in zip(kept[b], orders[b])]
    operands += [split(g, o) for o, g in latents]
    order_of = [*orders[0], *orders[1], *(o for o, _ in latents)]

    def kernel(*refs):
        flags_ref = refs[0]
        fetched = refs[1 : 1 + len(operands)]
        w_ref, h1_ref, h2_ref, gain_ref, bias_ref, *x_refs = refs[1 + len(operands) : -7]
        out_ref, lat_ref, stacks, g_bufs, kept_ref, act_ref, sems = refs[-7:]
        segment_at, chan_at = flags_ref[0], flags_ref[1]

        def copies(t):
            made = []
            for i in range(3):
                g = fetched[ticks * i + t]
                for c in range(2):
                    made.append(
                        pltpu.make_async_copy(
                            g.at[:, c] if order_of[ticks * i + t] else g.at[c],
                            g_bufs.at[i, :, c],
                            sems.at[len(made)],
                        )
                    )
            return made

        def each(act, only=slice(None)):
            for t in range(ticks):

                @pl.when(segment_at == ticks - 1 - t)
                def _():
                    for made in copies(t)[only]:
                        act(made)

        each(lambda made: made.start())
        row, col = grid_of((GS, positions))
        lane = lax.broadcasted_iota(jnp.int32, (GS, TAIL), 1)
        for b in range(2):
            for q in range(0, chans, GS):
                x = x_refs[b][0, 0, q : q + GS, :].astype(F32)
                for step_row in (-1, 0, 1):
                    for step_col in (-1, 0, 1):
                        tap = 3 * (step_row + 1) + step_col + 1
                        stacks[b, q // GS, tap * GS : (tap + 1) * GS, :] = shifted(
                            x, step_row, step_col, row, col
                        ).astype(BF16)
                stacks[b, q // GS, 9 * GS :, :] = jnp.zeros((TAIL - 9 * GS, positions), BF16)
        norms = []
        for b, h_ref in enumerate((h1_ref, h2_ref)):
            gains, biases = columns_of(gain_ref, bias_ref, b)
            blocks = [h_ref[0, 0, q : q + GS, :] for q in range(0, chans, GS)]
            stats = norm_stats(blocks)
            for i, h in enumerate(blocks):
                rows = slice(i * GS, (i + 1) * GS)
                xhat, n, sig, slope, inv_std = norm_group(h, gains[rows], biases[rows], stats[i])
                kept_ref[0, b, rows, :] = xhat
                kept_ref[1, b, rows, :] = slope
                kept_ref[2, b, rows, :] = slope * (gains[rows] * inv_std)
                act_ref[b, rows, :] = (n * sig).astype(BF16)
        store = storer(out_ref)
        for b in range(2):
            each(lambda made: made.wait(), slice(2 * b, 2 * b + 2))
            g = g_bufs[b].reshape(width, positions)
            ga = jnp.dot(w_ref[0, b], g, preferred_element_type=F32)
            proj = lax.dot_general(act_ref[b], g, NT, preferred_element_type=F32)
            store(b * chans, 0, proj.astype(BF16))
            for q in range(0, chans, GS):
                rows = slice(q, q + GS)
                xhat = kept_ref[0, b, rows, :]
                gh = gh_of(ga[rows, :], xhat, kept_ref[2, b, rows, :])
                taps = lax.dot_general(
                    gh, stacks[b, q // GS], NT, preferred_element_type=F32
                )
                gn = ga[rows, :] * kept_ref[1, b, rows, :]
                by_gain = jnp.sum(gn * xhat, axis=1, keepdims=True)
                by_bias = jnp.sum(gn, axis=1, keepdims=True)
                taps = jnp.where(lane == 9 * GS, by_gain, taps)
                taps = jnp.where(lane == 9 * GS + 1, by_bias, taps)
                store(b * chans + q, width, taps.astype(BF16))
        each(lambda made: made.wait(), slice(4, 6))
        lat_ref[...] = own_positions(g_bufs[2].reshape(width, positions), chan_at, slab)

    return pl.pallas_call(
        kernel,
        out_shape=(
            shape_of((members, 2 * chans, step), BF16),
            shape_of((slab, width), BF16),
        ),
        in_specs=[SMEM] + [ANY] * len(operands) + [VMEM] * 7,
        out_specs=[VMEM] * 2,
        scratch_shapes=[
            pltpu.VMEM((2, chans // GS, TAIL, positions), BF16),
            pltpu.VMEM((3, pairs, 2, chans, positions), BF16),
            pltpu.VMEM((3, 2, chans, positions), F32),
            pltpu.VMEM((2, chans, positions), BF16),
            pltpu.SemaphoreType.DMA((6,)),
        ],
        compiler_params=vmem(24),
        name="weight_grads",
    )(flags, *operands, proj_weight, h_one, h_two, gain, bias, *inputs)


def sum_kernel(in_ref, out_ref):
    done = summed(in_ref, slice(0, out_ref.shape[1]))
    for m in range(out_ref.shape[0]):
        out_ref[m] = done


def spread_sums(parts):
    return pl.pallas_call(
        sum_kernel,
        out_shape=shape_of(parts.shape, BF16),
        in_specs=[VMEM],
        out_specs=VMEM,
        compiler_params=vmem(6),
        name="sum_microbatches",
    )(parts)


def widen_kernel(in_ref, proj_ref, conv_ref, gain_ref, bias_ref):
    chans, width = proj_ref.shape[2:]
    step = in_ref.shape[2]
    down = lax.broadcasted_iota(jnp.int32, (chans, chans), 0)
    across = lax.broadcasted_iota(jnp.int32, (chans, chans), 1)
    first = width // step
    for b in range(2):
        rows = slice(b * chans, (b + 1) * chans)
        for i in range(first):
            proj_ref[0, b, :, i * step : (i + 1) * step] = in_ref[i, rows, :].astype(F32)
        conv_ref[0, b, :, :step] = in_ref[first, rows, :].astype(F32)
        side = in_ref[first + 1, rows, :].astype(F32)
        conv_ref[0, b, :, step:] = side[:, : 9 * GS - step]
        for i, to in enumerate((gain_ref, bias_ref)):
            at = 9 * GS - step + i
            lined = jnp.where(down == across, side[:, at : at + 1], 0.0)
            to[0, b : b + 1, :] = jnp.sum(lined, axis=0, keepdims=True)


def widen(sums, width):
    chans = sums.shape[1] // 2
    return pl.pallas_call(
        widen_kernel,
        out_shape=(
            shape_of((1, 2, chans, width), F32),
            shape_of((1, 2, chans, 9 * GS), F32),
            shape_of((1, 2, chans), F32),
            shape_of((1, 2, chans), F32),
        ),
        in_specs=[VMEM],
        out_specs=[VMEM] * 4,
        compiler_params=vmem(8),
        name="widen",
    )(sums)


def gather(block_, axis, groups=None):
    return lax.all_gather(block_, axis, axis=0, tiled=True, axis_index_groups=groups)


def per_device(
    grad_top,
    inputs_one,
    conv_one,
    inputs_two,
    conv_two,
    proj_weight,
    conv_weight,
    norm_gain,
    norm_bias,
):
    segments = lax.axis_size("segment")
    segment_at = lax.axis_index("segment")
    chan_at = lax.axis_index("chan")
    members = lax.axis_size("dp")
    shards = lax.axis_size("chan")
    chans, positions = conv_one.shape[2:]
    width = proj_weight.shape[3]
    cores = [[2 * y, 2 * y + 1] for y in range(shards // 2)]
    columns = [[2 * y + c for y in range(shards // 2)] for c in range(2)]

    def exchange(blocks):
        return lax.all_to_all(blocks, "dp", split_axis=0, concat_axis=0, tiled=True)

    params = (proj_weight, conv_weight, conv_one, conv_two, norm_gain, norm_bias)
    first_pack, second_pack = prepare(*params)
    packs = [None, gather(second_pack, "chan", columns)]
    packs[0] = lax.all_gather(
        first_pack[None], "chan", axis=1, tiled=True, axis_index_groups=columns
    )[0]
    states = [None, None]
    kept = [[], []]
    orders = [[], []]
    latents = []
    flags = jnp.stack([segment_at.astype(jnp.int32), chan_at.astype(jnp.int32)])
    for tick in range(segments):
        if tick == 0:
            g = lax.all_gather(grad_top[0], "chan", axis=1, tiled=True)
            ordered = True
        else:
            lower = segments - 1 - tick
            rest = [s for s in range(segments) if s not in (lower, lower + 1)]
            groups = sorted(
                [[lower, lower + 1]] + [rest[i : i + 2] for i in range(0, len(rest), 2)]
            )
            ordered = out.shape[0] == chans
            moved = gather(out, "segment", groups)[out.shape[0] :]
            g = gather(moved, "chan", None if ordered else cores)
            latents.append((ordered, g))
        for b in (1, 0):
            kept[b].append(g)
            if tick == 0 or (tick == 1 and b == 0):
                h = conv_two if b == 1 else conv_one
                out = own_block(
                    b, tick == 1, flags, g, ordered,
                    (proj_weight, conv_weight, h, norm_gain, norm_bias),
                )
            elif states[b] is None:
                packs[b], g = lax.optimization_barrier((packs[b], g))
                out, *states[b] = first_block(flags, g, ordered, chans, packs[b])
            else:
                out = wide_block(flags, g, ordered, chans, packs[b], states[b])
            orders[b].append(ordered)
            if b == 1 or tick == segments - 1:
                ordered = out.shape[0] == chans
                g = gather(out, "chan", None if ordered else cores)
    latents.append((ordered, g))

    parts, latent = weight_grads(
        flags, orders, kept, latents, params, (inputs_one, inputs_two)
    )
    sums = exchange(spread_sums(exchange(parts)))
    proj, conv, by_gain, by_bias = widen(sums, width)
    return latent.T[None, None], proj, conv, by_gain, by_bias


def solution(mesh):
    return jax.shard_map(
        per_device,
        mesh=mesh,
        in_specs=(
            P("dp", None, "chan"),
            P("segment", "dp", "chan", None),
            P("segment", "dp", "chan", None),
            P("segment", "dp", "chan", None),
            P("segment", "dp", "chan", None),
            P("segment", None, "chan", None),
            P("segment", None, "chan", None),
            P("segment", None, "chan"),
            P("segment", None, "chan"),
        ),
        out_specs=(
            P("segment", "dp", None, "chan"),
            P("segment", None, "chan", None),
            P("segment", None, "chan", None),
            P("segment", None, "chan"),
            P("segment", None, "chan"),
        ),
        check_vma=False,
    )
```
